128 devices in a mesh: ctx: 8 (over x, core), head: 16 (over y, z).
Axes of the slice: x: 4, y: 4, z: 4, core: 2. Of those that a mesh axis runs over, the one named last changes fastest.
Arguments:
- q_latent: bfloat16 [1024, 128, 576], P(('ctx', 'head')), may hold values from -84 to 84
- index_query: bfloat16 [1024, 64, 128], P('head'), may hold values from -6 to 6
- index_weight: float32 [1024, 64], P('head'), may hold values from -0.75 to 0.75
- index_keys: bfloat16 [16384, 128], P('ctx'), may hold values from -6 to 6
- latent_cache: bfloat16 [16384, 576], P('ctx'), may hold values from -6 to 6
- block_ids: int32 [8, 32], replicated, may hold values from 0 to 255, as said below
- block_counts: int32 [8], replicated, may hold values from 24 to 32, as said below
Outputs:
- attention: bfloat16 [1024, 128, 512], P('ctx', 'head')
- index_scores: float32 [1024, 16384], P('head', 'ctx')
The draws below stay inside these ranges and needn't reach their ends.
Inputs may be any that keep to these rules, and one draw needn't show every extreme that they name: `block_ids`: row t is query tile t's list of blocks of 64 positions. Its first block_counts[t] entries are distinct, lie at or before the tile's own last block and include the 2 blocks that hold the tile's own queries; of these counted entries at most 8 lie in one context shard of 32 blocks, and exactly 8 lie in the shard of the newest positions. Entries after the count are arbitrary block ids. `block_counts`: some tile has all 32 entries counted.
All inputs are finite; a program needn't handle non-finite values.
Results may differ from the reference program's by a relative error of at most 0.0034.
Values may be sent and summed in bfloat16 or wider, within the bound.
No kernel may reach another device: no remote copies, remote signals or barrier semaphores. Data moves between devices by JAX's collectives and lax.ppermute only.
A program may use at most 128 MiB of HBM per device.

```python
import jax
import jax.numpy as jnp
from jax import lax

HEADS = 128
LATENT = 512
ROPE = 64
IDX_HEADS = 64
IDX_DIM = 128
BLOCK = 64
TILE = 128
NSEL = 32
CAP = 8
KEYS_DEV = 2048
TILES = 8
QUERIES = 1024
CONTEXT = 16384


def base_cache(key):
    return jax.random.truncated_normal(jax.random.fold_in(key, 3), -6.0, 6.0, (CONTEXT, LATENT + ROPE), jnp.float32)


def draw_latent_cache(key, part):
    return base_cache(key).astype(jnp.bfloat16)


def draw_q_latent(key, part):
    base_draw = 1.5 * jax.random.truncated_normal(jax.random.fold_in(key, 5), -6.0, 6.0, (QUERIES, HEADS, LATENT + ROPE), jnp.float32)
    return base_draw.astype(jnp.bfloat16)


def block_plan(key):
    plan_keys = jax.random.split(jax.random.fold_in(key, 11), 7)
    blocks_dev = KEYS_DEV // BLOCK
    span_blocks = TILE // BLOCK
    first_new = CONTEXT // BLOCK - TILES * span_blocks
    last_start = CONTEXT // BLOCK - blocks_dev
    counts = jax.random.randint(plan_keys[0], (TILES,), NSEL - NSEL // 4, NSEL + 1)
    full_tile = jax.random.randint(plan_keys[1], (), 0, TILES)
    tile_range = jnp.arange(TILES)
    counts = jnp.where(tile_range == full_tile, NSEL, counts)
    local_index = jnp.arange(blocks_dev)
    limit_local = first_new - last_start + tile_range * span_blocks
    rand_last = jax.random.randint(plan_keys[2], (TILES, blocks_dev), 0, 1 << 20)
    score_last = jnp.where(local_index[None, :] < limit_local[:, None], rand_last, (1 << 20) + local_index[None, :]) * blocks_dev + local_index[None, :]
    pick_last = jnp.argsort(score_last, axis=1)[:, :CAP - span_blocks] + last_start
    diagonal_blocks = first_new + tile_range[:, None] * span_blocks + jnp.arange(span_blocks)[None, :]
    others = TILES - 1
    rand_other = jax.random.randint(plan_keys[3], (TILES, others, blocks_dev), 0, 1 << 20) * blocks_dev + local_index[None, None, :]
    pick_other = jnp.argsort(rand_other, axis=2)[:, :, :CAP] + (jnp.arange(others) * blocks_dev)[None, :, None]
    pool_blocks = pick_other.reshape(TILES, others * CAP)
    rand_pool = jax.random.randint(plan_keys[4], (TILES, others * CAP), 0, 1 << 20) * (others * CAP) + jnp.arange(others * CAP)[None, :]
    pool_blocks = jnp.take_along_axis(pool_blocks, jnp.argsort(rand_pool, axis=1), axis=1)[:, :NSEL - CAP]
    ordered = jnp.concatenate([diagonal_blocks, pick_last, pool_blocks], axis=1)
    entry_index = jnp.arange(NSEL)
    rand_valid = jax.random.randint(plan_keys[5], (TILES, NSEL), 0, 1 << 20) * NSEL + entry_index[None, :]
    order_score = jnp.where(entry_index[None, :] < counts[:, None], rand_valid, ((1 << 20) + 1) * NSEL + entry_index[None, :])
    shuffled = jnp.take_along_axis(ordered, jnp.argsort(order_score, axis=1), axis=1)
    filler = jax.random.randint(plan_keys[6], (TILES, NSEL), 0, CONTEXT // BLOCK)
    listed = jnp.where(entry_index[None, :] < counts[:, None], shuffled, filler)
    return (listed.astype(jnp.int32), counts.astype(jnp.int32))


def draw_block_ids(key, part):
    listed, counts = block_plan(key)
    return listed


def draw_block_counts(key, part):
    listed, counts = block_plan(key)
    return counts


def shard_levels(stream_key, extent, shards, low, top_value):
    def one(position, blocks):
        steps = jax.random.uniform(jax.random.fold_in(jax.random.fold_in(stream_key, 6), position), (blocks,), jnp.float32, low / len(shards), top_value / len(shards))
        return jnp.repeat(jnp.exp(steps), extent[position] // blocks).reshape((-1,) + (1,) * (len(extent) - position - 1))

    factor_of = one(*shards[0])
    for cut in shards[1:]:
        factor_of = factor_of * one(*cut)
    return factor_of


def gaussian(stream_key, extent, spread, limit, pieces=(), kind=jnp.bfloat16):
    entries = jax.random.normal(stream_key, extent, jnp.float32) * spread
    if len(pieces) > 0:
        entries = shard_levels(stream_key, extent, pieces, -0.22, 0.18) * entries
    return jnp.clip(entries, min=-limit, max=limit).astype(kind)


def setup_inputs(seed: int = 0) -> dict:
    arg_keys = jax.random.split(jax.random.key(seed), 8)
    return {
        "q_latent": draw_q_latent(jax.random.fold_in(arg_keys[7], 71), 0),
        "index_query": gaussian(arg_keys[1], (QUERIES, IDX_HEADS, IDX_DIM), 1.0, 6.0, ((0, 16),)),
        "index_weight": gaussian(arg_keys[2], (QUERIES, IDX_HEADS), IDX_HEADS ** -0.5, 0.75, ((0, 16),), jnp.float32),
        "index_keys": gaussian(arg_keys[3], (CONTEXT, IDX_DIM), 1.0, 6.0, ((0, 8),)),
        "latent_cache": draw_latent_cache(jax.random.fold_in(arg_keys[7], 71), 0),
        "block_ids": draw_block_ids(jax.random.fold_in(arg_keys[7], 71), 0),
        "block_counts": draw_block_counts(jax.random.fold_in(arg_keys[7], 71), 0),
    }


softmax_scale = 192.0 ** -0.5


def index_block(index_query, index_weight, key_block):
    flat_query = index_query.reshape(-1, index_query.shape[2])
    raw_dots = lax.dot_general(flat_query, key_block, (((1,), (1,)), ((), ())), preferred_element_type=jnp.float32)
    gated_dots = jax.nn.relu(raw_dots * index_query.shape[2] ** -0.5).reshape(index_query.shape[0], index_query.shape[1], -1)
    return jnp.sum(gated_dots * index_weight[:, :, None], axis=1)


def attend_rows(query_block, key_rows, allowed):
    rows_here = query_block.shape[0]
    heads_here = query_block.shape[1]
    flat_query = query_block.reshape(rows_here * heads_here, -1)
    raw_scores = lax.dot_general(flat_query, key_rows, (((1,), (1,)), ((), ())), preferred_element_type=jnp.float32)
    raw_scores = raw_scores.reshape(rows_here, heads_here, -1) * softmax_scale
    masked = jnp.where(allowed[:, None, :], raw_scores, -jnp.inf)
    row_max = jnp.max(masked, axis=2, keepdims=True)
    exp_scores = jnp.exp(masked - row_max)
    totals = jnp.sum(exp_scores, axis=2, keepdims=True)
    weights = exp_scores.astype(jnp.bfloat16).reshape(rows_here * heads_here, -1)
    weighted_sum = jnp.dot(weights, key_rows[:, :LATENT], preferred_element_type=jnp.float32)
    return (weighted_sum.reshape(rows_here, heads_here, LATENT) / totals).astype(jnp.bfloat16)


def reference(q_latent, index_query, index_weight, index_keys, latent_cache, block_ids, block_counts):
    context = latent_cache.shape[0]
    queries = q_latent.shape[0]
    key_span = 8 * BLOCK
    key_blocks = index_keys.reshape(context // key_span, key_span, IDX_DIM)
    per_block = lax.map(lambda key_block: index_block(index_query, index_weight, key_block), key_blocks)
    index_scores = jnp.transpose(per_block, (1, 0, 2)).reshape(queries, context)

    def one_tile(tile_index):
        tile_blocks = block_ids[tile_index]
        entry_index = jnp.arange(NSEL, dtype=jnp.int32)
        tile_live = entry_index < block_counts[tile_index]
        key_pos = (tile_blocks[:, None] * BLOCK + jnp.arange(BLOCK, dtype=jnp.int32)[None, :]).reshape(-1)
        key_live = jnp.repeat(tile_live, BLOCK)
        key_rows = jnp.take(latent_cache, key_pos, axis=0)
        query_pos = (context - queries) + tile_index * TILE + jnp.arange(TILE, dtype=jnp.int32)
        allowed = key_live[None, :] & (key_pos[None, :] <= query_pos[:, None])
        tile_query = lax.dynamic_slice_in_dim(q_latent, (tile_index * TILE).astype(jnp.int32), TILE, 0)
        return attend_rows(tile_query, key_rows, allowed)

    per_tile = lax.map(one_tile, jnp.arange(TILES, dtype=jnp.int32))
    attention = per_tile.reshape(queries, HEADS, LATENT)
    return attention, index_scores
```

```python
import functools

import jax
import jax.numpy as jnp
from jax import lax
from jax.experimental import pallas as pl
from jax.experimental.pallas import tpu as pltpu
from jax.sharding import PartitionSpec as P

BLOCK = 64
TILE = 128
CAP = 8
NSEL = 32
SHARDS = 8
PART = 16
SCALE = 192.0 ** (-0.5)
INDEX_SCALE = 128.0 ** (-0.5)
F32 = jnp.float32
BF16 = jnp.bfloat16
VMEM = pl.BlockSpec(memory_space=pltpu.VMEM)
SMEM = pl.BlockSpec(memory_space=pltpu.SMEM)


def iota(shape, dim):
    return lax.broadcasted_iota(jnp.int32, shape, dim)


def gather_kernel(pos_ref, ids_ref, counts_ref, cache_ref, out_ref):
    shard, row_y, row_z = pos_ref[0], pos_ref[1], pos_ref[2]
    tiles, entries = ids_ref.shape
    ids = jnp.where(iota((tiles, entries), 1) < counts_ref[...], ids_ref[...], -1)
    lane = iota((tiles, 128), 1)
    block_of_lane = lane + shard * 32
    member = jnp.zeros((tiles, 128), F32)
    for j in range(entries):
        member = jnp.where(ids[:, j : j + 1] == block_of_lane, 1.0, member)
    member = jnp.where(lane < 32, member, 0.0)
    before = (iota((128, 128), 0) < iota((128, 128), 1)).astype(BF16)
    rank = jnp.dot(member.astype(BF16), before, preferred_element_type=F32)
    rank = jnp.where(member > 0.0, rank, -1.0)
    slot = (lane >> 4).astype(F32)
    part = lane & 15
    row = jnp.where(part < 8, row_z * 8 + part, 24 + row_y * 8 + part)
    target = jnp.full((tiles, 128), -1, jnp.int32)
    for b in range(32):
        target = jnp.where(rank[:, b : b + 1] == slot, b * BLOCK + row, target)
    keys = cache_ref.shape[1]
    key_index = iota((keys, 128), 0)
    for t in range(0, tiles, 2):
        hot = jnp.concatenate(
            [(key_index == target[u : u + 1, :]).astype(F32).astype(BF16) for u in (t, t + 1)], axis=1
        )
        got = jnp.dot(cache_ref[...], hot, preferred_element_type=F32).astype(BF16)
        out_ref[t] = got[:, :128]
        out_ref[t + 1] = got[:, 128:]


def gather_parts(pos, block_ids, block_counts, cache_t):
    width, keys = cache_t.shape
    return pl.pallas_call(
        gather_kernel,
        out_shape=jax.ShapeDtypeStruct((block_ids.shape[0], width, 128), BF16),
        in_specs=[SMEM, VMEM, VMEM, VMEM],
        out_specs=VMEM,
        cost_estimate=pl.CostEstimate(
            flops=2 * width * keys * 1024, bytes_accessed=2 * width * keys * 2, transcendentals=0
        ),
        name="gather_parts",
    )(pos, block_ids, block_counts.reshape(-1, 1), cache_t)


def compact_kernel(pos_ref, ids_ref, counts_ref, parts_ref, first_ref, second_ref):
    tile = pos_ref[0]
    tiles, entries = ids_ref.shape
    ids = jnp.where(iota((tiles, entries), 1) < counts_ref[...], ids_ref[...], -1)
    mine = jnp.where(iota((tiles, entries), 0) == tile, ids, -1)
    column = iota((8, 512), 1)
    entry = (column & 255) >> 3
    part = (column & 7) + ((column >> 8) << 3)
    source = entry * PART + part
    end = jnp.zeros((1, 1), jnp.int32)
    for s in range(SHARDS):
        here = jnp.sum((mine >> 5 == s).astype(F32), axis=(0, 1), keepdims=True).astype(jnp.int32)
        end = end + here
        source = source + jnp.where(entry >= end, 128 - 16 * here, 0)
    source = source[0:1]
    row = iota((128, 512), 0)
    total = jnp.zeros((first_ref.shape[0], 512), F32)
    for s in range(0, SHARDS, 2):
        pick = jnp.concatenate(
            [(row + u * 128 == source).astype(F32).astype(BF16) for u in (s, s + 1)], axis=0
        )
        pair = jnp.concatenate([parts_ref[s], parts_ref[s + 1]], axis=1)
        total = total + jnp.dot(pair, pick, preferred_element_type=F32)
    total = total.astype(BF16)
    first_ref[...] = total[:, :256]
    second_ref[...] = total[:, 256:]


def compact_parts(pos, block_ids, block_counts, parts):
    width = parts.shape[1]
    half = jax.ShapeDtypeStruct((width, 256), BF16)
    return pl.pallas_call(
        compact_kernel,
        out_shape=(half, half),
        in_specs=[SMEM, VMEM, VMEM, VMEM],
        out_specs=(VMEM, VMEM),
        cost_estimate=pl.CostEstimate(
            flops=2 * width * 1024 * 512, bytes_accessed=width * 1536 * 2, transcendentals=0
        ),
        name="compact_parts",
    )(pos, block_ids, block_counts.reshape(-1, 1), parts)


def index_kernel(query_ref, weight_ref, keys_ref, out_ref):
    rows, heads, dim = query_ref.shape
    flat = query_ref[...].reshape(rows * heads, dim)
    weight = weight_ref[...] * INDEX_SCALE
    span = 256
    for c in range(keys_ref.shape[0] // span):
        dots = lax.dot_general(
            flat, keys_ref[c * span : (c + 1) * span, :], (((1,), (1,)), ((), ())), preferred_element_type=F32
        ).reshape(rows, heads, span)
        out_ref[:, c * span : (c + 1) * span] = jnp.sum(
            jnp.maximum(dots, 0.0) * weight[:, :, None], axis=1
        )


def index_scores_of(index_query, index_weight, index_keys):
    rows, heads, dim = index_query.shape
    keys = index_keys.shape[0]
    step = 8
    return pl.pallas_call(
        index_kernel,
        grid=(rows // step,),
        out_shape=jax.ShapeDtypeStruct((rows, keys), F32),
        in_specs=[
            pl.BlockSpec((step, heads, dim), lambda i: (i, 0, 0)),
            pl.BlockSpec((step, heads), lambda i: (i, 0)),
            pl.BlockSpec((keys, dim), lambda i: (0, 0)),
        ],
        out_specs=pl.BlockSpec((step, keys), lambda i: (i, 0)),
        cost_estimate=pl.CostEstimate(
            flops=8 * rows * heads * dim * keys, bytes_accessed=rows * heads * dim * 2 + rows * keys * 4, transcendentals=0
        ),
        name="index_scores",
    )(index_query, index_weight, index_keys)


def attend_kernel(pos_ref, q_ref, *refs):
    parts, out_ref = refs[:-1], refs[-1]
    rows = q_ref.shape[0]
    count, row_y, row_z = pos_ref[3], pos_ref[1], pos_ref[2]
    first_query = pl.program_id(0) * (rows // 8)
    query = first_query + (iota((rows, 128), 0) >> 3) + (count - 2) * BLOCK
    lane = iota((rows, 128), 1) + 128
    key = ((lane >> 3) * BLOCK) + (lane & 7)
    q = q_ref[...]
    scores = []
    top = None
    for p, part in enumerate(parts):
        offset = lax.rem(row_z - p + 4, 4) * 8 if p < 4 else 32 + lax.rem(row_y - (p - 4) + 4, 4) * 8
        s = jnp.dot(q, part[...], preferred_element_type=F32)
        s = jnp.concatenate([s[:, :128], jnp.where(key + offset <= query, s[:, 128:], -jnp.inf)], axis=1)
        scores.append(s)
        m = jnp.maximum(s[:, :128], s[:, 128:])
        top = m if top is None else jnp.maximum(top, m)
    top = jnp.max(top, axis=1, keepdims=True) * SCALE
    total = None
    mixed = None
    for s, part in zip(scores, parts):
        e = jnp.exp(s * SCALE - top)
        t = e[:, :128] + e[:, 128:]
        total = t if total is None else total + t
        o = lax.dot_general(
            e.astype(BF16), part[0:512, :], (((1,), (1,)), ((), ())), preferred_element_type=F32
        )
        mixed = o if mixed is None else mixed + o
    total = jnp.sum(total, axis=1, keepdims=True)
    out_ref[...] = (mixed / total).astype(BF16)


def attend(pos, q, parts):
    rows, width = q.shape
    step = 128
    part_spec = pl.BlockSpec((width, 256), lambda i: (0, 0))
    keys = 256 * len(parts)
    return pl.pallas_call(
        attend_kernel,
        grid=(rows // step,),
        out_shape=jax.ShapeDtypeStruct((rows, 512), BF16),
        in_specs=[SMEM, pl.BlockSpec((step, width), lambda i: (i, 0))] + [part_spec] * len(parts),
        out_specs=pl.BlockSpec((step, 512), lambda i: (i, 0)),
        cost_estimate=pl.CostEstimate(
            flops=2 * rows * keys * (width + 512),
            bytes_accessed=rows * (width + 512) * 2 + keys * width * 2,
            transcendentals=rows * keys,
        ),
        name="attend",
    )(pos, q, *parts)


def line(dy, dz):
    return [(y * 4 + z, ((y + dy) % 4) * 4 + (z + dz) % 4) for y in range(4) for z in range(4)]


def body(q_latent, index_query, index_weight, index_keys, latent_cache, block_ids, block_counts):
    shard_here = lax.axis_index("ctx")
    group_here = lax.axis_index("head")
    count_here = lax.dynamic_index_in_dim(block_counts, shard_here, keepdims=False)
    pos = jnp.stack([shard_here, group_here // 4, group_here % 4, count_here]).astype(jnp.int32)
    outgoing = gather_parts(pos, block_ids, block_counts, latent_cache.T)
    incoming = lax.all_to_all(outgoing, "ctx", split_axis=0, concat_axis=0, tiled=True)
    head_query = lax.all_to_all(q_latent, "head", split_axis=1, concat_axis=0, tiled=True)
    index_scores = index_scores_of(index_query, index_weight, index_keys)
    first, second = compact_parts(pos, block_ids, block_counts, incoming)
    firsts = [first] + [lax.ppermute(first, "head", line(0, d)) for d in (1, 2, 3)]
    seconds = [second] + [lax.ppermute(second, "head", line(d, 0)) for d in (1, 2, 3)]
    rows, heads, width = head_query.shape
    attention = attend(pos, head_query.reshape(rows * heads, width), firsts + seconds)
    return attention.reshape(rows, heads, 512), index_scores


def solution(mesh):
    return jax.shard_map(
        body,
        mesh=mesh,
        in_specs=(
            P(("ctx", "head"), None, None),
            P("head", None, None),
            P("head", None),
            P("ctx", None),
            P("ctx", None),
            P(),
            P(),
        ),
        out_specs=(P("ctx", "head", None), P("head", "ctx")),
        check_vma=False,
    )
```

```python
import jax
import jax.numpy as jnp
from jax import lax
from jax.experimental import pallas as pl
from jax.experimental.pallas import tpu as pltpu
from jax.sharding import PartitionSpec as P


BLOCK = 64
SHARDS = 8
PART = 16
SCALE = 192.0 ** (-0.5)
INDEX_SCALE = 128.0 ** (-0.5)
F32 = jnp.float32
BF16 = jnp.bfloat16
VMEM = pl.BlockSpec(memory_space=pltpu.VMEM)
SMEM = pl.BlockSpec(memory_space=pltpu.SMEM)


def iota(shape, dim):
    return lax.broadcasted_iota(jnp.int32, shape, dim)


def valid_ids(ids_ref, counts_ref):
    tiles, entries = ids_ref.shape
    tile = iota((tiles, entries), 0)
    count = jnp.zeros((tiles, entries), jnp.int32)
    for t in range(tiles):
        count = jnp.where(tile == t, counts_ref[t], count)
    return jnp.where(iota((tiles, entries), 1) < count, ids_ref[...], -1)


def place():
    group = lax.axis_index("head")
    return lax.axis_index("ctx"), group >> 2, group & 3


def row_of(part, row_y, row_z):
    return jnp.where(part < 8, row_z * 8 + part, 24 + row_y * 8 + part)


def hot(index, target):
    return (index == target).astype(F32).astype(BF16)


def gather_kernel(ids_ref, counts_ref, cache_ref, *out_refs):
    shard, row_y, row_z = place()
    ids = valid_ids(ids_ref, counts_ref)
    tiles, entries = ids.shape
    keys = cache_ref.shape[1]
    blocks = keys // BLOCK
    lane = iota((tiles, 128), 1)
    block_of_lane = jnp.where(lane < blocks, lane + shard * blocks, -2)
    member = jnp.zeros((tiles, 128), F32)
    for j in range(entries):
        member = jnp.where(ids[:, j : j + 1] == block_of_lane, 1.0, member)
    before = (iota((128, 128), 0) < iota((128, 128), 1)).astype(BF16)
    rank = jnp.dot(member.astype(BF16), before, preferred_element_type=F32)
    rank = jnp.where(member > 0.0, rank, -1.0)
    slot = (lane >> 4).astype(F32)
    target = jnp.full((tiles, 128), -1, jnp.int32)
    for b in range(blocks):
        target = jnp.where(rank[:, b : b + 1] == slot, b * PART + (lane & 15), target)
    column = iota((512, 128), 1)
    keep = hot(iota((512, 128), 0), (column >> 4) * BLOCK + row_of(column & 15, row_y, row_z))
    own = jnp.concatenate(
        [
            jnp.dot(cache_ref[:, c : c + 512], keep, preferred_element_type=F32).astype(BF16)
            for c in range(0, keys, 512)
        ],
        axis=1,
    )
    index = iota((own.shape[1], 128), 0)
    for d in range(0, tiles, 2):
        pair = []
        for u in (d, d + 1):
            chosen = iota((tiles, 128), 0) == ((shard + u) & 7)
            pair.append(hot(index, jnp.sum(jnp.where(chosen, target, 0), axis=0, keepdims=True)))
        got = jnp.dot(own, jnp.concatenate(pair, axis=1), preferred_element_type=F32).astype(BF16)
        out_refs[d][...] = got[:, :128]
        out_refs[d + 1][...] = got[:, 128:]


def gather_parts(block_ids, block_counts, cache_t):
    width, keys = cache_t.shape
    tiles = block_ids.shape[0]
    return pl.pallas_call(
        gather_kernel,
        out_shape=[jax.ShapeDtypeStruct((width, 128), BF16)] * tiles,
        in_specs=[VMEM, SMEM, VMEM],
        out_specs=[VMEM] * tiles,
        cost_estimate=pl.CostEstimate(
            flops=2 * width * keys * 1024, bytes_accessed=2 * width * keys * 2, transcendentals=0
        ),
        compiler_params=pltpu.CompilerParams(vmem_limit_bytes=24 << 20),
        name="gather_parts",
    )(block_ids, block_counts, cache_t)


def compact_kernel(ids_ref, counts_ref, *refs):
    part_refs, (first_ref, second_ref) = refs[:-2], refs[-2:]
    tile = lax.axis_index("ctx")
    ids = valid_ids(ids_ref, counts_ref)
    mine = jnp.sum(jnp.where(iota(ids.shape, 0) == tile, ids, 0), axis=0, keepdims=True)
    owner = jnp.where(mine < 0, 2 * SHARDS, mine >> 5)
    shard = iota(ids.shape, 0)
    here = jnp.sum((owner == shard).astype(F32), axis=1, keepdims=True).astype(jnp.int32)
    end = jnp.sum((owner <= shard).astype(F32), axis=1, keepdims=True).astype(jnp.int32)
    column = iota((SHARDS, 512), 1)
    entry = (column & 255) >> 3
    skipped = jnp.sum(jnp.where(entry >= end, 128 - 16 * here, 0), axis=0, keepdims=True)
    part = (column & 7) + ((column >> 8) << 3)
    source = (entry * PART + part)[0:1] + skipped
    row = iota((128, 512), 0)
    total = jnp.zeros((first_ref.shape[0], 512), F32)
    for d in range(0, SHARDS, 2):
        pick = jnp.concatenate([hot(row + ((tile - u) & 7) * 128, source) for u in (d, d + 1)], axis=0)
        pair = jnp.concatenate([part_refs[d][...], part_refs[d + 1][...]], axis=1)
        total = total + jnp.dot(pair, pick, preferred_element_type=F32)
    total = total.astype(BF16)
    first_ref[...] = total[:, :256]
    second_ref[...] = total[:, 256:]


def compact_parts(block_ids, block_counts, parts):
    width = parts[0].shape[0]
    half = jax.ShapeDtypeStruct((width, 256), BF16)
    return pl.pallas_call(
        compact_kernel,
        out_shape=(half, half),
        in_specs=[VMEM, SMEM] + [VMEM] * len(parts),
        out_specs=(VMEM, VMEM),
        cost_estimate=pl.CostEstimate(
            flops=2 * width * 1024 * 512, bytes_accessed=width * 1536 * 2, transcendentals=0
        ),
        compiler_params=pltpu.CompilerParams(vmem_limit_bytes=24 << 20),
        name="compact_parts",
    )(block_ids, block_counts, *parts)


def q_prep_kernel(q_ref, out_ref):
    groups, rows, heads, width = out_ref.shape
    for i in range(rows):
        out_ref[:, i] = q_ref[i].T.reshape(groups, heads, width)


def q_by_group(q_latent, groups):
    rows, heads, width = q_latent.shape
    return pl.pallas_call(
        q_prep_kernel,
        out_shape=jax.ShapeDtypeStruct((groups, rows, heads // groups, width), BF16),
        in_specs=[VMEM],
        out_specs=VMEM,
        cost_estimate=pl.CostEstimate(flops=0, bytes_accessed=rows * heads * width * 4, transcendentals=0),
        compiler_params=pltpu.CompilerParams(vmem_limit_bytes=16 << 20),
        name="q_by_group",
    )(q_latent.transpose(0, 2, 1))


def index_kernel(query_ref, weight_ref, keys_ref, out_ref):
    rows, heads, dim = query_ref.shape
    flat = query_ref[...].reshape(rows * heads, dim)
    weight = weight_ref[...] * INDEX_SCALE
    span = 256
    for c in range(keys_ref.shape[0] // span):
        dots = lax.dot_general(
            flat, keys_ref[c * span : (c + 1) * span, :], (((1,), (1,)), ((), ())), preferred_element_type=F32
        ).reshape(rows, heads, span)
        out_ref[:, c * span : (c + 1) * span] = jnp.sum(
            jnp.maximum(dots, 0.0) * weight[:, :, None], axis=1
        )


def index_scores_of(index_query, index_weight, index_keys):
    rows, heads, dim = index_query.shape
    keys = index_keys.shape[0]
    step = 8
    return pl.pallas_call(
        index_kernel,
        grid=(rows // step,),
        out_shape=jax.ShapeDtypeStruct((rows, keys), F32),
        in_specs=[
            pl.BlockSpec((step, heads, dim), lambda i: (i, 0, 0)),
            pl.BlockSpec((step, heads), lambda i: (i, 0)),
            pl.BlockSpec((keys, dim), lambda i: (0, 0)),
        ],
        out_specs=pl.BlockSpec((step, keys), lambda i: (i, 0)),
        cost_estimate=pl.CostEstimate(
            flops=8 * rows * heads * dim * keys, bytes_accessed=rows * heads * dim * 2 + rows * keys * 4, transcendentals=0
        ),
        compiler_params=pltpu.CompilerParams(vmem_limit_bytes=32 << 20),
        name="index_scores",
    )(index_query, index_weight, index_keys)


def attend_kernel(counts_ref, q_ref, *refs):
    parts, out_ref = refs[:-1], refs[-1]
    rows = q_ref.shape[0]
    tile, row_y, row_z = place()
    count = counts_ref[tile]
    first_query = pl.program_id(0) * (rows // 8)
    query = first_query + (iota((rows, 128), 0) >> 3) + (count - 2) * BLOCK
    lane = iota((rows, 128), 1) + 128
    key = ((lane >> 3) * BLOCK) + (lane & 7)
    q = q_ref[...]
    scores = []
    top = None
    for p, part in enumerate(parts):
        offset = lax.rem(row_z - p + 4, 4) * 8 if p < 4 else 32 + lax.rem(row_y - (p - 4) + 4, 4) * 8
        s = jnp.dot(q, part[...], preferred_element_type=F32)
        s = jnp.concatenate([s[:, :128], jnp.where(key + offset <= query, s[:, 128:], -jnp.inf)], axis=1)
        scores.append(s)
        m = jnp.maximum(s[:, :128], s[:, 128:])
        top = m if top is None else jnp.maximum(top, m)
    top = jnp.max(top, axis=1, keepdims=True) * SCALE
    total = None
    mixed = None
    for s, part in zip(scores, parts):
        e = jnp.exp(s * SCALE - top)
        t = e[:, :128] + e[:, 128:]
        total = t if total is None else total + t
        o = lax.dot_general(
            e.astype(BF16), part[0:512, :], (((1,), (1,)), ((), ())), preferred_element_type=F32
        )
        mixed = o if mixed is None else mixed + o
    total = jnp.sum(total, axis=1, keepdims=True)
    out_ref[...] = (mixed / total).astype(BF16)


def attend(block_counts, q, parts):
    rows, width = q.shape
    step = 128
    part_spec = pl.BlockSpec((width, 256), lambda i: (0, 0))
    keys = 256 * len(parts)
    return pl.pallas_call(
        attend_kernel,
        grid=(rows // step,),
        out_shape=jax.ShapeDtypeStruct((rows, 512), BF16),
        in_specs=[SMEM, pl.BlockSpec((step, width), lambda i: (i, 0))] + [part_spec] * len(parts),
        out_specs=pl.BlockSpec((step, 512), lambda i: (i, 0)),
        cost_estimate=pl.CostEstimate(
            flops=2 * rows * keys * (width + 512),
            bytes_accessed=rows * (width + 512) * 2 + keys * width * 2,
            transcendentals=rows * keys,
        ),
        compiler_params=pltpu.CompilerParams(vmem_limit_bytes=32 << 20),
        name="attend",
    )(block_counts, q, *parts)


def turn(d):
    return [(i, (i + d) % SHARDS) for i in range(SHARDS)]


def line(dy, dz):
    return [(y * 4 + z, ((y + dy) % 4) * 4 + (z + dz) % 4) for y in range(4) for z in range(4)]


def body(q_latent, index_query, index_weight, index_keys, latent_cache, block_ids, block_counts):
    rows, heads, width = q_latent.shape
    groups = lax.axis_size("head")
    outgoing = gather_parts(block_ids, block_counts, latent_cache.T)
    incoming = [outgoing[0]] + [lax.ppermute(outgoing[d], "ctx", turn(d)) for d in range(1, SHARDS)]
    by_group = q_by_group(q_latent, groups)
    head_query = lax.all_to_all(by_group, "head", split_axis=0, concat_axis=0, tiled=True)
    index_scores = index_scores_of(index_query, index_weight, index_keys)
    first, second = compact_parts(block_ids, block_counts, incoming)
    firsts = [first] + [lax.ppermute(first, "head", line(0, d)) for d in (1, 2, 3)]
    seconds = [second] + [lax.ppermute(second, "head", line(d, 0)) for d in (1, 2, 3)]
    attention = attend(block_counts, head_query.reshape(-1, width), firsts + seconds)
    return attention.reshape(rows * groups, heads // groups, 512), index_scores


def solution(mesh):
    return jax.shard_map(
        body,
        mesh=mesh,
        in_specs=(
            P(("ctx", "head"), None, None),
            P("head", None, None),
            P("head", None),
            P("ctx", None),
            P("ctx", None),
            P(),
            P(),
        ),
        out_specs=(P("ctx", "head", None), P("head", "ctx")),
        check_vma=False,
    )
```

```python
import jax
import jax.numpy as jnp
from jax import lax
from jax.experimental import pallas as pl
from jax.experimental.pallas import tpu as pltpu
from jax.sharding import PartitionSpec as P


BLOCK = 64
SHARDS = 8
PART = 16
SCALE = 192.0 ** (-0.5)
INDEX_SCALE = 128.0 ** (-0.5)
F32 = jnp.float32
BF16 = jnp.bfloat16
VMEM = pl.BlockSpec(memory_space=pltpu.VMEM)
SMEM = pl.BlockSpec(memory_space=pltpu.SMEM)


def iota(shape, dim):
    return lax.broadcasted_iota(jnp.int32, shape, dim)


def valid_ids(ids_ref, counts_ref):
    tiles, entries = ids_ref.shape
    tile = iota((tiles, entries), 0)
    count = jnp.zeros((tiles, entries), jnp.int32)
    for t in range(tiles):
        count = jnp.where(tile == t, counts_ref[t], count)
    return jnp.where(iota((tiles, entries), 1) < count, ids_ref[...], -1)


def place():
    group = lax.axis_index("head")
    row_y, row_z = group >> 2, group & 3
    return lax.axis_index("ctx"), (row_y + 2 * row_z) & 3, (2 * row_y + row_z) & 3


def row_of(part, first, second):
    return jnp.where(part < 8, first * 8 + part, 24 + second * 8 + part)


def hot(index, target):
    return (index == target).astype(F32).astype(BF16)


def slot_sources(ids, tile):
    mine = jnp.sum(jnp.where(iota(ids.shape, 0) == tile, ids, 0), axis=0, keepdims=True)
    owner = jnp.where(mine < 0, 2 * SHARDS, mine >> 5)
    shard = iota(ids.shape, 0)
    here = jnp.sum((owner == shard).astype(F32), axis=1, keepdims=True).astype(jnp.int32)
    end = jnp.sum((owner <= shard).astype(F32), axis=1, keepdims=True).astype(jnp.int32)
    column = iota((SHARDS, 512), 1)
    entry = (column & 255) >> 3
    skipped = jnp.sum(jnp.where(entry >= end, 128 - 16 * here, 0), axis=0, keepdims=True)
    part = (column & 7) + ((column >> 8) << 3)
    return entry * PART + part + skipped, end[SHARDS - 1 :, :]


def gather_kernel(ids_ref, counts_ref, cache_ref, *refs):
    out_refs, (source_ref, past_ref, held, sems) = refs[:-4], refs[-4:]
    keys = cache_ref.shape[1]
    copies = []
    for i, c in enumerate(range(0, keys, 512)):
        copies.append(pltpu.make_async_copy(cache_ref.at[:, pl.ds(c, 512)], held.at[i], sems.at[i]))
        copies[i].start()
    shard, first, second = place()
    ids = valid_ids(ids_ref, counts_ref)
    tiles, entries = ids.shape
    blocks = keys // BLOCK
    lane = iota((tiles, 128), 1)
    block_of_lane = jnp.where(lane < blocks, lane + shard * blocks, -2)
    member = jnp.zeros((tiles, 128), F32)
    for j in range(entries):
        member = jnp.where(ids[:, j : j + 1] == block_of_lane, 1.0, member)
    before = (iota((128, 128), 0) < iota((128, 128), 1)).astype(BF16)
    rank = jnp.dot(member.astype(BF16), before, preferred_element_type=F32)
    rank = jnp.where(member > 0.0, rank, -1.0)
    slot = (lane >> 4).astype(F32)
    target = jnp.full((tiles, 128), -1, jnp.int32)
    for b in range(blocks):
        target = jnp.where(rank[:, b : b + 1] == slot, b * PART + (lane & 15), target)
    column = iota((512, 128), 1)
    keep = hot(iota((512, 128), 0), (column >> 4) * BLOCK + row_of(column & 15, first, second))
    own = []
    for i, copy in enumerate(copies):
        copy.wait()
        own.append(jnp.dot(held[i], keep, preferred_element_type=F32).astype(BF16))
    own = jnp.concatenate(own, axis=1)
    index = iota((own.shape[1], 128), 0)
    for d in range(0, tiles, 2):
        pair = []
        for u in (d, d + 1):
            chosen = iota((tiles, 128), 0) == ((shard + u) & 7)
            pair.append(hot(index, jnp.sum(jnp.where(chosen, target, 0), axis=0, keepdims=True)))
        got = jnp.dot(own, jnp.concatenate(pair, axis=1), preferred_element_type=F32).astype(BF16)
        out_refs[d][...] = got[:, :128]
        out_refs[d + 1][...] = got[:, 128:]
    source, count = slot_sources(ids, shard)
    source_ref[...] = source
    past_ref[...] = jnp.broadcast_to((count - 2) * BLOCK, past_ref.shape)


def gather_parts(block_ids, block_counts, cache_t):
    width, keys = cache_t.shape
    tiles = block_ids.shape[0]
    return pl.pallas_call(
        gather_kernel,
        out_shape=[jax.ShapeDtypeStruct((width, 128), BF16)] * tiles
        + [jax.ShapeDtypeStruct((SHARDS, 512), jnp.int32), jax.ShapeDtypeStruct((8, 128), jnp.int32)],
        in_specs=[VMEM, SMEM, pl.BlockSpec(memory_space=pltpu.HBM)],
        out_specs=[VMEM] * (tiles + 2),
        scratch_shapes=[pltpu.VMEM((keys // 512, width, 512), BF16), pltpu.SemaphoreType.DMA((keys // 512,))],
        cost_estimate=pl.CostEstimate(
            flops=2 * width * keys * 1024, bytes_accessed=2 * width * keys * 2, transcendentals=0
        ),
        name="gather_parts",
    )(block_ids, block_counts, cache_t)


def compact_kernel(source_ref, *refs):
    part_refs, (own_ref, up_ref, down_ref, right_ref, left_ref) = refs[:-5], refs[-5:]
    tile = lax.axis_index("ctx")
    source = source_ref[0:1, :]
    row = iota((128, 512), 0)
    total = jnp.zeros((own_ref.shape[0], 512), F32)
    for d in range(0, SHARDS, 2):
        pick = jnp.concatenate([hot(row + ((tile - u) & 7) * 128, source) for u in (d, d + 1)], axis=0)
        pair = jnp.concatenate([part_refs[d][...], part_refs[d + 1][...]], axis=1)
        total = total + jnp.dot(pair, pick, preferred_element_type=F32)
    total = total.astype(BF16)
    own_ref[...] = total
    up_ref[...] = total[:, :384]
    down_ref[:, :256] = total[:, :256]
    down_ref[:, 256:] = total[:, 384:]
    right_ref[:, :256] = total[:, 256:]
    right_ref[:, 256:] = total[:, :128]
    left_ref[:, :256] = total[:, 256:]
    left_ref[:, 256:] = total[:, 128:256]


def compact_parts(source, parts):
    width = parts[0].shape[0]
    sent = jax.ShapeDtypeStruct((width, 384), BF16)
    return pl.pallas_call(
        compact_kernel,
        out_shape=[jax.ShapeDtypeStruct((width, 512), BF16)] + [sent] * 4,
        in_specs=[VMEM] * (1 + len(parts)),
        out_specs=[VMEM] * 5,
        cost_estimate=pl.CostEstimate(
            flops=2 * width * 1024 * 512, bytes_accessed=width * 1536 * 2, transcendentals=0
        ),
        compiler_params=pltpu.CompilerParams(vmem_limit_bytes=12 << 20),
        name="compact_parts",
    )(source, *parts)


def q_prep_kernel(q_ref, out_ref):
    groups, rows, heads, width = out_ref.shape
    for i in range(rows):
        out_ref[:, i] = q_ref[i].T.reshape(groups, heads, width)


def q_by_group(q_latent, groups):
    rows, heads, width = q_latent.shape
    return pl.pallas_call(
        q_prep_kernel,
        out_shape=jax.ShapeDtypeStruct((groups, rows, heads // groups, width), BF16),
        in_specs=[VMEM],
        out_specs=VMEM,
        cost_estimate=pl.CostEstimate(flops=0, bytes_accessed=rows * heads * width * 4, transcendentals=0),
        compiler_params=pltpu.CompilerParams(vmem_limit_bytes=8 << 20),
        name="q_by_group",
    )(q_latent.transpose(0, 2, 1))


def index_kernel(query_ref, weight_ref, keys_ref, out_ref):
    rows, heads, dim = query_ref.shape
    flat = query_ref[...].reshape(rows * heads, dim)
    weight = weight_ref[...] * INDEX_SCALE
    span = 256
    for c in range(keys_ref.shape[0] // span):
        dots = lax.dot_general(
            flat, keys_ref[c * span : (c + 1) * span, :], (((1,), (1,)), ((), ())), preferred_element_type=F32
        ).reshape(rows, heads, span)
        out_ref[:, c * span : (c + 1) * span] = jnp.sum(
            jnp.maximum(dots, 0.0) * weight[:, :, None], axis=1
        )


def index_scores_of(index_query, index_weight, index_keys):
    rows, heads, dim = index_query.shape
    keys = index_keys.shape[0]
    step = 8
    return pl.pallas_call(
        index_kernel,
        grid=(rows // step,),
        out_shape=jax.ShapeDtypeStruct((rows, keys), F32),
        in_specs=[
            pl.BlockSpec((step, heads, dim), lambda i: (i, 0, 0)),
            pl.BlockSpec((step, heads), lambda i: (i, 0)),
            pl.BlockSpec((keys, dim), lambda i: (0, 0)),
        ],
        out_specs=pl.BlockSpec((step, keys), lambda i: (i, 0)),
        cost_estimate=pl.CostEstimate(
            flops=8 * rows * heads * dim * keys, bytes_accessed=rows * heads * dim * 2 + rows * keys * 4, transcendentals=0
        ),
        compiler_params=pltpu.CompilerParams(vmem_limit_bytes=16 << 20),
        name="index_scores",
    )(index_query, index_weight, index_keys)


def masked_scores(q, keys, tiles, limit):
    scores = jnp.dot(q, keys, preferred_element_type=F32)
    rows = q.shape[0]
    lane = iota((rows, 128), 1)
    offset = (lane >> 3) * BLOCK + (lane & 7)
    pieces = []
    for t, first_key in enumerate(tiles):
        piece = scores[:, t * 128 : (t + 1) * 128]
        if first_key is not None:
            piece = jnp.where(offset <= limit - first_key, piece, -jnp.inf)
        pieces.append(piece)
    return jnp.concatenate(pieces, axis=1)


def own_kernel(past_ref, q_ref, keys_ref, top_ref, total_ref, mixed_ref):
    _, first, second = place()
    past = past_ref[0:1, :]
    late = 16 * BLOCK
    tiles = (None, late + first * 8, None, late + 32 + second * 8)
    rows, step = q_ref.shape[0], 256
    for a in range(0, rows, step):
        limit = past + a // 8 + (iota((step, 128), 0) >> 3)
        scores = masked_scores(q_ref[a : a + step, :], keys_ref[...], tiles, limit)
        top = jnp.max(scores, axis=1, keepdims=True)
        weights = jnp.exp((scores - top) * SCALE)
        top_ref[a : a + step, :] = jnp.broadcast_to(top, (step, 128))
        total_ref[a : a + step, :] = jnp.broadcast_to(jnp.sum(weights, axis=1, keepdims=True), (step, 128))
        mixed_ref[a : a + step, :] = lax.dot_general(
            weights.astype(BF16), keys_ref[0:512, :], (((1,), (1,)), ((), ())), preferred_element_type=F32
        )


def attend_own(past, q, keys):
    rows, width = q.shape
    count = keys.shape[1]
    return pl.pallas_call(
        own_kernel,
        out_shape=[
            jax.ShapeDtypeStruct((rows, 128), F32),
            jax.ShapeDtypeStruct((rows, 128), F32),
            jax.ShapeDtypeStruct((rows, 512), F32),
        ],
        in_specs=[VMEM] * 3,
        out_specs=[VMEM] * 3,
        cost_estimate=pl.CostEstimate(
            flops=2 * rows * count * (width + 512), bytes_accessed=rows * 4352, transcendentals=rows * count
        ),
        compiler_params=pltpu.CompilerParams(vmem_limit_bytes=16 << 20),
        name="attend_own",
    )(past, q, keys)


def rest_kernel(past_ref, q_ref, top_ref, total_ref, mixed_ref, up_ref, down_ref, right_ref, left_ref, out_ref, keys_ref):
    _, first, second = place()
    past = past_ref[0:1, :]
    late = 16 * BLOCK

    def of_first(step):
        return late + ((first + step) & 3) * 8

    def of_second(step):
        return late + 32 + ((second + step) & 3) * 8

    tiles = (
        (None, of_first(-1), None)
        + (None, of_first(1), of_second(2))
        + (None, of_second(-1), None)
        + (None, of_second(1), of_first(2))
    )
    for i, ref in enumerate((up_ref, down_ref, right_ref, left_ref)):
        keys_ref[:, i * 384 : (i + 1) * 384] = ref[...]
    rows, step = q_ref.shape[0], 256
    for a in range(0, rows, step):
        limit = past + a // 8 + (iota((step, 128), 0) >> 3)
        scores = masked_scores(q_ref[a : a + step, :], keys_ref[...], tiles, limit)
        before = top_ref[a : a + step, 0:1]
        top = jnp.maximum(jnp.max(scores, axis=1, keepdims=True), before)
        weights = jnp.exp((scores - top) * SCALE)
        fade = jnp.exp((before - top) * SCALE)
        total = total_ref[a : a + step, 0:1] * fade + jnp.sum(weights, axis=1, keepdims=True)
        mixed = mixed_ref[a : a + step, :] * fade + lax.dot_general(
            weights.astype(BF16), keys_ref[0:512, :], (((1,), (1,)), ((), ())), preferred_element_type=F32
        )
        out_ref[a : a + step, :] = (mixed / total).astype(BF16)


def attend_rest(past, q, state, parts):
    rows, width = q.shape
    count = sum(part.shape[1] for part in parts)
    return pl.pallas_call(
        rest_kernel,
        out_shape=jax.ShapeDtypeStruct((rows, 512), BF16),
        in_specs=[VMEM] * (5 + len(parts)),
        out_specs=VMEM,
        scratch_shapes=[pltpu.VMEM((width, count), BF16)],
        cost_estimate=pl.CostEstimate(
            flops=2 * rows * count * (width + 512), bytes_accessed=rows * 5376, transcendentals=rows * count
        ),
        compiler_params=pltpu.CompilerParams(vmem_limit_bytes=24 << 20),
        name="attend_rest",
    )(past, q, *state, *parts)


def turn(d):
    return [(i, (i + d) % SHARDS) for i in range(SHARDS)]


def line(dy, dz):
    return [(y * 4 + z, ((y + dy) % 4) * 4 + (z + dz) % 4) for y in range(4) for z in range(4)]


def body(q_latent, index_query, index_weight, index_keys, latent_cache, block_ids, block_counts):
    rows, heads, width = q_latent.shape
    groups = lax.axis_size("head")
    *outgoing, source, past = gather_parts(block_ids, block_counts, latent_cache.T)
    incoming = [outgoing[0]] + [lax.ppermute(outgoing[d], "ctx", turn(d)) for d in range(1, SHARDS)]
    by_group = q_by_group(q_latent, groups)
    head_query = lax.all_to_all(by_group, "head", split_axis=0, concat_axis=0, tiled=True)
    index_scores = index_scores_of(index_query, index_weight, index_keys)
    own, up, down, right, left = compact_parts(source, incoming)
    parts = [
        lax.ppermute(part, "head", line(*step))
        for part, step in ((up, (1, 0)), (down, (-1, 0)), (right, (0, 1)), (left, (0, -1)))
    ]
    flat_query = head_query.reshape(-1, width)
    state = attend_own(past, flat_query, own)
    attention = attend_rest(past, flat_query, state, parts)
    return attention.reshape(rows * groups, heads // groups, 512), index_scores


def solution(mesh):
    return jax.shard_map(
        body,
        mesh=mesh,
        in_specs=(
            P(("ctx", "head"), None, None),
            P("head", None, None),
            P("head", None),
            P("ctx", None),
            P("ctx", None),
            P(),
            P(),
        ),
        out_specs=(P("ctx", "head", None), P("head", "ctx")),
        check_vma=False,
    )
```

```python
import jax
import jax.numpy as jnp
from jax import lax
from jax.experimental import pallas as pl
from jax.experimental.pallas import tpu as pltpu
from jax.sharding import PartitionSpec as P


BLOCK = 64
SHARDS = 8
PART = 16
SCALE = 192.0 ** (-0.5)
INDEX_SCALE = 128.0 ** (-0.5)
F32 = jnp.float32
BF16 = jnp.bfloat16
VMEM = pl.BlockSpec(memory_space=pltpu.VMEM)
SMEM = pl.BlockSpec(memory_space=pltpu.SMEM)


def iota(shape, dim):
    return lax.broadcasted_iota(jnp.int32, shape, dim)


def in_hbm(x):
    return pltpu.with_memory_space_constraint(x, pltpu.HBM)


def valid_ids(ids_ref, counts_ref):
    tiles, entries = ids_ref.shape
    tile = iota((tiles, entries), 0)
    count = jnp.zeros((tiles, entries), jnp.int32)
    for t in range(tiles):
        count = jnp.where(tile == t, counts_ref[t], count)
    return jnp.where(iota((tiles, entries), 1) < count, ids_ref[...], -1)


def place():
    group = lax.axis_index("head")
    row_y, row_z = group >> 2, group & 3
    return lax.axis_index("ctx"), (row_y + 2 * row_z) & 3, (2 * row_y + row_z) & 3


def row_of(part, first, second):
    return jnp.where(part < 8, first * 8 + part, 24 + second * 8 + part)


def hot(index, target):
    return (index == target).astype(F32).astype(BF16)


def slot_sources(ids, tile):
    mine = jnp.sum(jnp.where(iota(ids.shape, 0) == tile, ids, 0), axis=0, keepdims=True)
    owner = jnp.where(mine < 0, 2 * SHARDS, mine >> 5)
    shard = iota(ids.shape, 0)
    here = jnp.sum((owner == shard).astype(F32), axis=1, keepdims=True).astype(jnp.int32)
    end = jnp.sum((owner <= shard).astype(F32), axis=1, keepdims=True).astype(jnp.int32)
    column = iota((SHARDS, 512), 1)
    entry = (column & 255) >> 3
    skipped = jnp.sum(jnp.where(entry >= end, 128 - 16 * here, 0), axis=0, keepdims=True)
    part = (column & 7) + ((column >> 8) << 3)
    return entry * PART + part + skipped, end[SHARDS - 1 :, :]


def gather_kernel(ids_ref, counts_ref, cache_ref, *refs):
    out_refs, (source_ref, other_ref, past_ref, held, sems) = refs[:-5], refs[-5:]
    keys = cache_ref.shape[1]
    copies = []
    for i, c in enumerate(range(0, keys, 512)):
        copies.append(pltpu.make_async_copy(cache_ref.at[:, pl.ds(c, 512)], held.at[i], sems.at[i]))
        copies[i].start()
    shard, first, second = place()
    ids = valid_ids(ids_ref, counts_ref)
    tiles, entries = ids.shape
    blocks = keys // BLOCK
    lane = iota((tiles, 128), 1)
    block_of_lane = jnp.where(lane < blocks, lane + shard * blocks, -2)
    member = jnp.zeros((tiles, 128), F32)
    for j in range(entries):
        member = jnp.where(ids[:, j : j + 1] == block_of_lane, 1.0, member)
    before = (iota((128, 128), 0) < iota((128, 128), 1)).astype(BF16)
    rank = jnp.dot(member.astype(BF16), before, preferred_element_type=F32)
    rank = jnp.where(member > 0.0, rank, -1.0)
    slot = (lane >> 4).astype(F32)
    target = jnp.full((tiles, 128), -1, jnp.int32)
    for b in range(blocks):
        target = jnp.where(rank[:, b : b + 1] == slot, b * PART + (lane & 15), target)
    column = iota((512, 128), 1)
    keep = hot(iota((512, 128), 0), (column >> 4) * BLOCK + row_of(column & 15, first, second))
    own = []
    for i, copy in enumerate(copies):
        copy.wait()
        own.append(jnp.dot(held[i], keep, preferred_element_type=F32).astype(BF16))
    own = jnp.concatenate(own, axis=1)
    index = iota((own.shape[1], 128), 0)
    for d, out_ref in enumerate(out_refs):
        near = (shard + 2 * d) & 7
        pair = []
        for tile in (near, near ^ 1):
            chosen = iota((tiles, 128), 0) == tile
            pair.append(hot(index, jnp.sum(jnp.where(chosen, target, 0), axis=0, keepdims=True)))
        got = jnp.dot(own, jnp.concatenate(pair, axis=1), preferred_element_type=F32)
        out_ref[...] = got.astype(BF16)
    source, count = slot_sources(ids, shard)
    source_ref[...] = source
    past_ref[...] = jnp.broadcast_to((count - 2) * BLOCK, past_ref.shape)
    other_ref[...] = slot_sources(ids, shard ^ 1)[0]


def gather_parts(block_ids, block_counts, cache_t):
    width, keys = cache_t.shape
    tables = [pltpu.HBM((SHARDS, n), jnp.int32) for n in (512, 512, 128)]
    chips = SHARDS // 2
    return pl.pallas_call(
        gather_kernel,
        out_shape=[pltpu.HBM((width, 256), BF16)] + [jax.ShapeDtypeStruct((width, 256), BF16)] * (chips - 1) + tables,
        in_specs=[VMEM, SMEM, pl.BlockSpec(memory_space=pltpu.HBM)],
        out_specs=[VMEM] * (chips + 3),
        scratch_shapes=[pltpu.VMEM((keys // 512, width, 512), BF16), pltpu.SemaphoreType.DMA((keys // 512,))],
        cost_estimate=pl.CostEstimate(
            flops=2 * width * keys * 1024, bytes_accessed=2 * width * keys * 2, transcendentals=0
        ),
        compiler_params=pltpu.CompilerParams(vmem_limit_bytes=16 << 20),
        name="gather_parts",
    )(in_hbm(block_ids), in_hbm(block_counts), in_hbm(cache_t))


def compact_kernel(source_ref, other_ref, *refs):
    part_refs, (own_out, other_out) = refs[:-2], refs[-2:]
    shard = lax.axis_index("ctx")
    row = iota((128, 512), 0)
    for table_ref, out_ref, left in ((source_ref, own_out, 0), (other_ref, other_out, 128)):
        source = table_ref[0:1, :]
        total = jnp.zeros(out_ref.shape, F32)
        for d in range(0, len(part_refs), 2):
            pick = jnp.concatenate([hot(row + ((shard - 2 * u) & 7) * 128, source) for u in (d, d + 1)], axis=0)
            pair = jnp.concatenate([part_refs[u][:, left : left + 128] for u in (d, d + 1)], axis=1)
            total = total + jnp.dot(pair, pick, preferred_element_type=F32)
        out_ref[...] = total.astype(BF16)


def compact_parts(source, other, parts):
    width = parts[0].shape[0]
    return pl.pallas_call(
        compact_kernel,
        out_shape=[jax.ShapeDtypeStruct((width, 512), BF16)] * 2,
        in_specs=[VMEM] * (2 + len(parts)),
        out_specs=[VMEM] * 2,
        cost_estimate=pl.CostEstimate(
            flops=2 * width * 1024 * 512, bytes_accessed=width * 1536 * 2, transcendentals=0
        ),
        compiler_params=pltpu.CompilerParams(vmem_limit_bytes=12 << 20),
        name="compact_parts",
    )(in_hbm(source), in_hbm(other), in_hbm(parts[0]), *parts[1:])


def spread_kernel(own_ref, other_ref, up_ref, down_ref, right_ref, left_ref):
    first = own_ref[:, :256] + other_ref[:, :256]
    second = own_ref[:, 256:] + other_ref[:, 256:]
    up_ref[:, :256] = first
    up_ref[:, 256:] = second[:, :128]
    down_ref[:, :256] = first
    down_ref[:, 256:] = second[:, 128:]
    right_ref[:, :256] = second
    right_ref[:, 256:] = first[:, :128]
    left_ref[:, :256] = second
    left_ref[:, 256:] = first[:, 128:]


def spread_parts(own, other):
    width = own.shape[0]
    return pl.pallas_call(
        spread_kernel,
        out_shape=[jax.ShapeDtypeStruct((width, 384), BF16)] * 4,
        in_specs=[VMEM] * 2,
        out_specs=[VMEM] * 4,
        cost_estimate=pl.CostEstimate(flops=width * 512, bytes_accessed=width * 2560 * 2, transcendentals=0),
        compiler_params=pltpu.CompilerParams(vmem_limit_bytes=8 << 20),
        name="spread_parts",
    )(own, other)


def q_prep_kernel(q_ref, out_ref):
    groups, rows, heads, width = out_ref.shape
    for i in range(rows):
        out_ref[:, i] = q_ref[i].T.reshape(groups, heads, width)


def q_by_group(q_latent, groups):
    rows, heads, width = q_latent.shape
    return pl.pallas_call(
        q_prep_kernel,
        out_shape=jax.ShapeDtypeStruct((groups, rows, heads // groups, width), BF16),
        in_specs=[VMEM],
        out_specs=VMEM,
        cost_estimate=pl.CostEstimate(flops=0, bytes_accessed=rows * heads * width * 4, transcendentals=0),
        compiler_params=pltpu.CompilerParams(vmem_limit_bytes=8 << 20),
        name="q_by_group",
    )(q_latent.transpose(0, 2, 1))


def index_kernel(query_ref, weight_ref, keys_ref, out_ref):
    rows, heads, dim = query_ref.shape
    flat = query_ref[...].reshape(rows * heads, dim)
    weight = weight_ref[...] * INDEX_SCALE
    span = 256
    for c in range(keys_ref.shape[0] // span):
        dots = lax.dot_general(
            flat, keys_ref[c * span : (c + 1) * span, :], (((1,), (1,)), ((), ())), preferred_element_type=F32
        ).reshape(rows, heads, span)
        out_ref[:, c * span : (c + 1) * span] = jnp.sum(
            jnp.maximum(dots, 0.0) * weight[:, :, None], axis=1
        )


def index_scores_of(index_query, index_weight, index_keys):
    rows, heads, dim = index_query.shape
    keys = index_keys.shape[0]
    step = 8
    return pl.pallas_call(
        index_kernel,
        grid=(rows // step,),
        out_shape=jax.ShapeDtypeStruct((rows, keys), F32),
        in_specs=[
            pl.BlockSpec((step, heads, dim), lambda i: (i, 0, 0)),
            pl.BlockSpec((step, heads), lambda i: (i, 0)),
            pl.BlockSpec((keys, dim), lambda i: (0, 0)),
        ],
        out_specs=pl.BlockSpec((step, keys), lambda i: (i, 0)),
        cost_estimate=pl.CostEstimate(
            flops=8 * rows * heads * dim * keys, bytes_accessed=rows * heads * dim * 2 + rows * keys * 4, transcendentals=0
        ),
        compiler_params=pltpu.CompilerParams(vmem_limit_bytes=16 << 20),
        name="index_scores",
    )(index_query, index_weight, index_keys)


def masked_scores(q, keys, tiles, limit):
    scores = jnp.dot(q, keys, preferred_element_type=F32)
    rows = q.shape[0]
    lane = iota((rows, 128), 1)
    offset = (lane >> 3) * BLOCK + (lane & 7)
    pieces = []
    for t, first_key in enumerate(tiles):
        piece = scores[:, t * 128 : (t + 1) * 128]
        if first_key is not None:
            piece = jnp.where(offset <= limit - first_key, piece, -jnp.inf)
        pieces.append(piece)
    return jnp.concatenate(pieces, axis=1)


def own_kernel(past_ref, q_ref, up_ref, down_ref, top_ref, total_ref, mixed_ref, keys_ref):
    _, first, second = place()
    past = past_ref[0:1, :]
    late = 16 * BLOCK
    tiles = (None, late + first * 8, None, late + 32 + second * 8)
    keys_ref[:, :384] = up_ref[...]
    keys_ref[:, 384:] = down_ref[:, 256:]
    rows, step = q_ref.shape[0], 256
    for a in range(0, rows, step):
        limit = past + a // 8 + (iota((step, 128), 0) >> 3)
        scores = masked_scores(q_ref[a : a + step, :], keys_ref[...], tiles, limit)
        top = jnp.max(scores, axis=1, keepdims=True)
        weights = jnp.exp((scores - top) * SCALE)
        top_ref[a : a + step, :] = jnp.broadcast_to(top, (step, 128))
        total_ref[a : a + step, :] = jnp.broadcast_to(jnp.sum(weights, axis=1, keepdims=True), (step, 128))
        mixed_ref[a : a + step, :] = lax.dot_general(
            weights.astype(BF16), keys_ref[0:512, :], (((1,), (1,)), ((), ())), preferred_element_type=F32
        )


def attend_own(past, q, up, down):
    rows, width = q.shape
    count = 512
    return pl.pallas_call(
        own_kernel,
        out_shape=[
            jax.ShapeDtypeStruct((rows, 128), F32),
            jax.ShapeDtypeStruct((rows, 128), F32),
            jax.ShapeDtypeStruct((rows, 512), F32),
        ],
        in_specs=[VMEM] * 4,
        out_specs=[VMEM] * 3,
        scratch_shapes=[pltpu.VMEM((width, count), BF16)],
        cost_estimate=pl.CostEstimate(
            flops=2 * rows * count * (width + 512), bytes_accessed=rows * 4352, transcendentals=rows * count
        ),
        compiler_params=pltpu.CompilerParams(vmem_limit_bytes=16 << 20),
        name="attend_own",
    )(in_hbm(past), q, up, down)


def rest_kernel(past_ref, q_ref, top_ref, total_ref, mixed_ref, up_ref, down_ref, right_ref, left_ref, out_ref, keys_ref):
    _, first, second = place()
    past = past_ref[0:1, :]
    late = 16 * BLOCK

    def of_first(step):
        return late + ((first + step) & 3) * 8

    def of_second(step):
        return late + 32 + ((second + step) & 3) * 8

    tiles = (
        (None, of_first(-1), None)
        + (None, of_first(1), of_second(2))
        + (None, of_second(-1), None)
        + (None, of_second(1), of_first(2))
    )
    for i, ref in enumerate((up_ref, down_ref, right_ref, left_ref)):
        keys_ref[:, i * 384 : (i + 1) * 384] = ref[...]
    rows, step = q_ref.shape[0], 256
    for a in range(0, rows, step):
        limit = past + a // 8 + (iota((step, 128), 0) >> 3)
        scores = masked_scores(q_ref[a : a + step, :], keys_ref[...], tiles, limit)
        before = top_ref[a : a + step, 0:1]
        top = jnp.maximum(jnp.max(scores, axis=1, keepdims=True), before)
        weights = jnp.exp((scores - top) * SCALE)
        fade = jnp.exp((before - top) * SCALE)
        total = total_ref[a : a + step, 0:1] * fade + jnp.sum(weights, axis=1, keepdims=True)
        mixed = mixed_ref[a : a + step, :] * fade + lax.dot_general(
            weights.astype(BF16), keys_ref[0:512, :], (((1,), (1,)), ((), ())), preferred_element_type=F32
        )
        out_ref[a : a + step, :] = (mixed / total).astype(BF16)


def attend_rest(past, q, state, parts):
    rows, width = q.shape
    count = sum(part.shape[1] for part in parts)
    return pl.pallas_call(
        rest_kernel,
        out_shape=jax.ShapeDtypeStruct((rows, 512), BF16),
        in_specs=[VMEM] * (5 + len(parts)),
        out_specs=VMEM,
        scratch_shapes=[pltpu.VMEM((width, count), BF16)],
        cost_estimate=pl.CostEstimate(
            flops=2 * rows * count * (width + 512), bytes_accessed=rows * 5376, transcendentals=rows * count
        ),
        compiler_params=pltpu.CompilerParams(vmem_limit_bytes=24 << 20),
        name="attend_rest",
    )(in_hbm(past), q, *state, *parts)


def turn(d):
    return [(i, (i + d) % SHARDS) for i in range(SHARDS)]


def line(dy, dz):
    return [(y * 4 + z, ((y + dy) % 4) * 4 + (z + dz) % 4) for y in range(4) for z in range(4)]


def body(q_latent, index_query, index_weight, index_keys, latent_cache, block_ids, block_counts):
    rows, heads, width = q_latent.shape
    groups = lax.axis_size("head")
    *outgoing, source, other, past = gather_parts(block_ids, block_counts, latent_cache.T)
    incoming = [outgoing[0]] + [lax.ppermute(outgoing[d], "ctx", turn(2 * d)) for d in range(1, SHARDS // 2)]
    by_group = q_by_group(q_latent, groups)
    head_query = lax.all_to_all(by_group, "head", split_axis=0, concat_axis=0, tiled=True)
    index_scores = index_scores_of(index_query, index_weight, index_keys)
    mine, theirs = compact_parts(source, other, incoming)
    theirs = lax.ppermute(theirs, "ctx", [(i, i ^ 1) for i in range(SHARDS)])
    up, down, right, left = spread_parts(mine, theirs)
    parts = [
        lax.ppermute(part, "head", line(*step))
        for part, step in ((up, (1, 0)), (down, (-1, 0)), (right, (0, 1)), (left, (0, -1)))
    ]
    flat_query = head_query.reshape(-1, width)
    state = attend_own(past, flat_query, up, down)
    attention = attend_rest(past, flat_query, state, parts)
    return attention.reshape(rows * groups, heads // groups, 512), index_scores


def solution(mesh):
    return jax.shard_map(
        body,
        mesh=mesh,
        in_specs=(
            P(("ctx", "head"), None, None),
            P("head", None, None),
            P("head", None),
            P("ctx", None),
            P("ctx", None),
            P(),
            P(),
        ),
        out_specs=(P("ctx", "head", None), P("head", "ctx")),
        check_vma=False,
    )
```

```python
import jax
import jax.numpy as jnp
from jax import lax
from jax.experimental import pallas as pl
from jax.experimental.pallas import tpu as pltpu
from jax.sharding import PartitionSpec as P


BLOCK = 64
SHARDS = 8
PART = 16
SCALE = 192.0 ** (-0.5)
INDEX_SCALE = 128.0 ** (-0.5)
F32 = jnp.float32
BF16 = jnp.bfloat16
VMEM = pl.BlockSpec(memory_space=pltpu.VMEM)
SMEM = pl.BlockSpec(memory_space=pltpu.SMEM)


def iota(shape, dim):
    return lax.broadcasted_iota(jnp.int32, shape, dim)


def in_hbm(x):
    return pltpu.with_memory_space_constraint(x, pltpu.HBM)


def valid_ids(ids_ref, counts_ref):
    tiles, entries = ids_ref.shape
    tile = iota((tiles, entries), 0)
    count = jnp.zeros((tiles, entries), jnp.int32)
    for t in range(tiles):
        count = jnp.where(tile == t, counts_ref[t], count)
    return jnp.where(iota((tiles, entries), 1) < count, ids_ref[...], -1)


def place():
    group = lax.axis_index("head")
    row_y, row_z = group >> 2, group & 3
    return lax.axis_index("ctx"), (row_y + 2 * row_z) & 3, (2 * row_y + row_z) & 3


def row_of(part, first, second):
    return jnp.where(part < 8, first * 8 + part, 24 + second * 8 + part)


def hot(index, target):
    return (index == target).astype(F32).astype(BF16)


def slot_sources(ids, tile):
    mine = jnp.sum(jnp.where(iota(ids.shape, 0) == tile, ids, 0), axis=0, keepdims=True)
    owner = jnp.where(mine < 0, 2 * SHARDS, mine >> 5)
    shard = iota(ids.shape, 0)
    here = jnp.sum((owner == shard).astype(F32), axis=1, keepdims=True).astype(jnp.int32)
    end = jnp.sum((owner <= shard).astype(F32), axis=1, keepdims=True).astype(jnp.int32)
    column = iota((SHARDS, 512), 1)
    entry = (column & 255) >> 3
    skipped = jnp.sum(jnp.where(entry >= end, 128 - 16 * here, 0), axis=0, keepdims=True)
    part = (column & 7) + ((column >> 8) << 3)
    return entry * PART + part + skipped, end[SHARDS - 1 :, :]


def gather_kernel(ids_hbm, counts_hbm, cache_ref, *refs):
    out_refs, (source_ref, past_ref, ids_ref, counts_ref, held, sems) = refs[:-6], refs[-6:]
    keys = cache_ref.shape[1]
    lists = [
        pltpu.make_async_copy(ids_hbm, ids_ref, sems.at[keys // 512]),
        pltpu.make_async_copy(counts_hbm, counts_ref, sems.at[keys // 512 + 1]),
    ]
    for copy in lists:
        copy.start()
    copies = []
    for i, c in enumerate(range(0, keys, 512)):
        copies.append(pltpu.make_async_copy(cache_ref.at[:, pl.ds(c, 512)], held.at[i], sems.at[i]))
        copies[i].start()
    shard, first, second = place()
    for copy in lists:
        copy.wait()
    ids = valid_ids(ids_ref, counts_ref)
    tiles, entries = ids.shape
    blocks = keys // BLOCK
    lane = iota((tiles, 128), 1)
    block_of_lane = jnp.where(lane < blocks, lane + shard * blocks, -2)
    member = jnp.zeros((tiles, 128), F32)
    for j in range(entries):
        member = jnp.where(ids[:, j : j + 1] == block_of_lane, 1.0, member)
    before = (iota((128, 128), 0) < iota((128, 128), 1)).astype(BF16)
    rank = jnp.dot(member.astype(BF16), before, preferred_element_type=F32)
    rank = jnp.where(member > 0.0, rank, -1.0)
    slot = (lane >> 4).astype(F32)
    target = jnp.full((tiles, 128), -1, jnp.int32)
    for b in range(blocks):
        target = jnp.where(rank[:, b : b + 1] == slot, b * PART + (lane & 15), target)
    column = iota((512, 128), 1)
    keep = hot(iota((512, 128), 0), (column >> 4) * BLOCK + row_of(column & 15, first, second))
    own = []
    for i, copy in enumerate(copies):
        copy.wait()
        own.append(jnp.dot(held[i], keep, preferred_element_type=F32).astype(BF16))
    own = jnp.concatenate(own, axis=1)
    index = iota((own.shape[1], 128), 0)
    for d in range(0, tiles, 2):
        pair = []
        for u in (d, d + 1):
            chosen = iota((tiles, 128), 0) == ((shard + u) & 7)
            pair.append(hot(index, jnp.sum(jnp.where(chosen, target, 0), axis=0, keepdims=True)))
        got = jnp.dot(own, jnp.concatenate(pair, axis=1), preferred_element_type=F32).astype(BF16)
        out_refs[d][...] = got[:, :128]
        out_refs[d + 1][...] = got[:, 128:]
    source, count = slot_sources(ids, shard)
    source_ref[...] = source
    past_ref[...] = jnp.broadcast_to((count - 2) * BLOCK, past_ref.shape)


def gather_parts(block_ids, block_counts, cache_t):
    width, keys = cache_t.shape
    hbm = pl.BlockSpec(memory_space=pltpu.HBM)
    return pl.pallas_call(
        gather_kernel,
        out_shape=[pltpu.HBM((width, 128), BF16)]
        + [pltpu.VMEM((width, 128), BF16)] * (SHARDS - 1)
        + [pltpu.HBM((SHARDS, n), jnp.int32) for n in (512, 128)],
        in_specs=[hbm] * 3,
        out_specs=[VMEM] * (SHARDS + 2),
        scratch_shapes=[
            pltpu.VMEM(block_ids.shape, jnp.int32),
            pltpu.SMEM(block_counts.shape, jnp.int32),
            pltpu.VMEM((keys // 512, width, 512), BF16),
            pltpu.SemaphoreType.DMA((keys // 512 + 2,)),
        ],
        cost_estimate=pl.CostEstimate(
            flops=2 * width * keys * 1024, bytes_accessed=2 * width * keys * 2, transcendentals=0
        ),
        compiler_params=pltpu.CompilerParams(vmem_limit_bytes=16 << 20),
        name="gather_parts",
    )(in_hbm(block_ids), in_hbm(block_counts), in_hbm(cache_t))


def compact_kernel(source_ref, *refs):
    part_refs, (up_ref, down_ref, right_ref, left_ref) = refs[:-4], refs[-4:]
    tile = lax.axis_index("ctx")
    source = source_ref[0:1, :]
    row = iota((128, 512), 0)
    total = jnp.zeros((up_ref.shape[0], 512), F32)
    for d in range(0, SHARDS, 2):
        pick = jnp.concatenate([hot(row + ((tile - u) & 7) * 128, source) for u in (d, d + 1)], axis=0)
        pair = jnp.concatenate([part_refs[d][...], part_refs[d + 1][...]], axis=1)
        total = total + jnp.dot(pair, pick, preferred_element_type=F32)
    total = total.astype(BF16)
    first, second = total[:, :256], total[:, 256:]
    up_ref[:, :256] = first
    up_ref[:, 256:] = second[:, :128]
    down_ref[:, :256] = first
    down_ref[:, 256:] = second[:, 128:]
    right_ref[:, :256] = second
    right_ref[:, 256:] = first[:, :128]
    left_ref[:, :256] = second
    left_ref[:, 256:] = first[:, 128:]


def compact_parts(source, parts):
    width = parts[0].shape[0]
    return pl.pallas_call(
        compact_kernel,
        out_shape=[pltpu.VMEM((width, 384), BF16)] * 4,
        in_specs=[VMEM] * (1 + len(parts)),
        out_specs=[VMEM] * 4,
        cost_estimate=pl.CostEstimate(
            flops=2 * width * 1024 * 512, bytes_accessed=width * 1536 * 2, transcendentals=0
        ),
        compiler_params=pltpu.CompilerParams(vmem_limit_bytes=12 << 20),
        name="compact_parts",
    )(in_hbm(source), in_hbm(parts[0]), *parts[1:-1], in_hbm(parts[-1]))


def q_prep_kernel(q_ref, out_ref):
    groups, rows, heads, width = out_ref.shape
    for i in range(rows):
        out_ref[:, i] = q_ref[i].T.reshape(groups, heads, width)


def q_by_group(q_latent, groups):
    rows, heads, width = q_latent.shape
    return pl.pallas_call(
        q_prep_kernel,
        out_shape=jax.ShapeDtypeStruct((groups, rows, heads // groups, width), BF16),
        in_specs=[VMEM],
        out_specs=VMEM,
        cost_estimate=pl.CostEstimate(flops=0, bytes_accessed=rows * heads * width * 4, transcendentals=0),
        compiler_params=pltpu.CompilerParams(vmem_limit_bytes=8 << 20),
        name="q_by_group",
    )(q_latent.transpose(0, 2, 1))


def index_kernel(query_ref, weight_ref, keys_ref, out_ref):
    rows, heads, dim = query_ref.shape
    flat = query_ref[...].reshape(rows * heads, dim)
    weight = weight_ref[...] * INDEX_SCALE
    span = 256
    for c in range(keys_ref.shape[0] // span):
        dots = lax.dot_general(
            flat, keys_ref[c * span : (c + 1) * span, :], (((1,), (1,)), ((), ())), preferred_element_type=F32
        ).reshape(rows, heads, span)
        out_ref[:, c * span : (c + 1) * span] = jnp.sum(
            jnp.maximum(dots, 0.0) * weight[:, :, None], axis=1
        )


def index_scores_of(index_query, index_weight, index_keys):
    rows, heads, dim = index_query.shape
    keys = index_keys.shape[0]
    step = 8
    return pl.pallas_call(
        index_kernel,
        grid=(rows // step,),
        out_shape=jax.ShapeDtypeStruct((rows, keys), F32),
        in_specs=[
            pl.BlockSpec((step, heads, dim), lambda i: (i, 0, 0)),
            pl.BlockSpec((step, heads), lambda i: (i, 0)),
            pl.BlockSpec((keys, dim), lambda i: (0, 0)),
        ],
        out_specs=pl.BlockSpec((step, keys), lambda i: (i, 0)),
        cost_estimate=pl.CostEstimate(
            flops=8 * rows * heads * dim * keys, bytes_accessed=rows * heads * dim * 2 + rows * keys * 4, transcendentals=0
        ),
        compiler_params=pltpu.CompilerParams(vmem_limit_bytes=16 << 20),
        name="index_scores",
    )(index_query, index_weight, index_keys)


def masked_scores(q, keys, tiles, limit):
    scores = jnp.dot(q, keys, preferred_element_type=F32)
    rows = q.shape[0]
    lane = iota((rows, 128), 1)
    offset = (lane >> 3) * BLOCK + (lane & 7)
    pieces = []
    for t, first_key in enumerate(tiles):
        piece = scores[:, t * 128 : (t + 1) * 128]
        if first_key is not None:
            piece = jnp.where(offset <= limit - first_key, piece, -jnp.inf)
        pieces.append(piece)
    return jnp.concatenate(pieces, axis=1)


def own_kernel(past_ref, q_ref, up_ref, down_ref, top_ref, total_ref, mixed_ref, keys_ref):
    _, first, second = place()
    past = past_ref[0:1, :]
    late = 16 * BLOCK
    tiles = (None, late + first * 8, None, late + 32 + second * 8)
    keys_ref[:, :384] = up_ref[...]
    keys_ref[:, 384:] = down_ref[:, 256:]
    rows, step = q_ref.shape[0], 256
    for a in range(0, rows, step):
        limit = past + a // 8 + (iota((step, 128), 0) >> 3)
        scores = masked_scores(q_ref[a : a + step, :], keys_ref[...], tiles, limit)
        top = jnp.max(scores, axis=1, keepdims=True)
        weights = jnp.exp((scores - top) * SCALE)
        top_ref[a : a + step, :] = jnp.broadcast_to(top, (step, 128))
        total_ref[a : a + step, :] = jnp.broadcast_to(jnp.sum(weights, axis=1, keepdims=True), (step, 128))
        mixed_ref[a : a + step, :] = lax.dot_general(
            weights.astype(BF16), keys_ref[0:512, :], (((1,), (1,)), ((), ())), preferred_element_type=F32
        )


def attend_own(past, q, up, down):
    rows, width = q.shape
    count = 512
    return pl.pallas_call(
        own_kernel,
        out_shape=[
            jax.ShapeDtypeStruct((rows, 128), F32),
            jax.ShapeDtypeStruct((rows, 128), F32),
            jax.ShapeDtypeStruct((rows, 512), F32),
        ],
        in_specs=[VMEM] * 4,
        out_specs=[VMEM] * 3,
        scratch_shapes=[pltpu.VMEM((width, count), BF16)],
        cost_estimate=pl.CostEstimate(
            flops=2 * rows * count * (width + 512), bytes_accessed=rows * 4352, transcendentals=rows * count
        ),
        compiler_params=pltpu.CompilerParams(vmem_limit_bytes=16 << 20),
        name="attend_own",
    )(in_hbm(past), q, up, down)


def rest_kernel(past_ref, q_ref, top_ref, total_ref, mixed_ref, up_ref, down_ref, right_ref, left_ref, out_ref, keys_ref, done_ref, sems):
    _, first, second = place()
    past = past_ref[0:1, :]
    late = 16 * BLOCK

    def of_first(step):
        return late + ((first + step) & 3) * 8

    def of_second(step):
        return late + 32 + ((second + step) & 3) * 8

    tiles = (
        (None, of_first(-1), None)
        + (None, of_first(1), of_second(2))
        + (None, of_second(-1), None)
        + (None, of_second(1), of_first(2))
    )
    for i, ref in enumerate((up_ref, down_ref, right_ref, left_ref)):
        keys_ref[:, i * 384 : (i + 1) * 384] = ref[...]
    rows, step = q_ref.shape[0], 256
    copies = []
    for a in range(0, rows, step):
        limit = past + a // 8 + (iota((step, 128), 0) >> 3)
        scores = masked_scores(q_ref[a : a + step, :], keys_ref[...], tiles, limit)
        before = top_ref[a : a + step, 0:1]
        top = jnp.maximum(jnp.max(scores, axis=1, keepdims=True), before)
        weights = jnp.exp((scores - top) * SCALE)
        fade = jnp.exp((before - top) * SCALE)
        total = total_ref[a : a + step, 0:1] * fade + jnp.sum(weights, axis=1, keepdims=True)
        mixed = mixed_ref[a : a + step, :] * fade + lax.dot_general(
            weights.astype(BF16), keys_ref[0:512, :], (((1,), (1,)), ((), ())), preferred_element_type=F32
        )
        done_ref[a : a + step, :] = (mixed / total).astype(BF16)
        copies.append(
            pltpu.make_async_copy(
                done_ref.at[pl.ds(a, step), :], out_ref.at[pl.ds(a, step), :], sems.at[a // step]
            )
        )
        copies[-1].start()
    for copy in copies:
        copy.wait()


def attend_rest(past, q, state, parts):
    rows, width = q.shape
    count = sum(part.shape[1] for part in parts)
    return pl.pallas_call(
        rest_kernel,
        out_shape=jax.ShapeDtypeStruct((rows, 512), BF16),
        in_specs=[VMEM] * (5 + len(parts)),
        out_specs=pl.BlockSpec(memory_space=pltpu.HBM),
        scratch_shapes=[
            pltpu.VMEM((width, count), BF16),
            pltpu.VMEM((rows, 512), BF16),
            pltpu.SemaphoreType.DMA((rows // 256,)),
        ],
        cost_estimate=pl.CostEstimate(
            flops=2 * rows * count * (width + 512), bytes_accessed=rows * 5376, transcendentals=rows * count
        ),
        compiler_params=pltpu.CompilerParams(vmem_limit_bytes=24 << 20),
        name="attend_rest",
    )(in_hbm(past), q, *state, *parts)


def turn(d):
    return [(i, (i + d) % SHARDS) for i in range(SHARDS)]


def line(dy, dz):
    return [(y * 4 + z, ((y + dy) % 4) * 4 + (z + dz) % 4) for y in range(4) for z in range(4)]


def body(q_latent, index_query, index_weight, index_keys, latent_cache, block_ids, block_counts):
    rows, heads, width = q_latent.shape
    groups = lax.axis_size("head")
    *outgoing, source, past = gather_parts(block_ids, block_counts, latent_cache.T)
    incoming = [outgoing[0]] + [lax.ppermute(outgoing[d], "ctx", turn(d)) for d in range(1, SHARDS)]
    by_group = q_by_group(q_latent, groups)
    head_query = lax.all_to_all(by_group, "head", split_axis=0, concat_axis=0, tiled=True)
    index_scores = index_scores_of(index_query, index_weight, index_keys)
    up, down, right, left = compact_parts(source, incoming)
    parts = [
        lax.ppermute(part, "head", line(*step))
        for part, step in ((up, (1, 0)), (down, (-1, 0)), (right, (0, 1)), (left, (0, -1)))
    ]
    flat_query = head_query.reshape(-1, width)
    state = attend_own(past, flat_query, up, down)
    attention = attend_rest(past, flat_query, state, parts)
    return attention.reshape(rows * groups, heads // groups, 512), index_scores


def solution(mesh):
    return jax.shard_map(
        body,
        mesh=mesh,
        in_specs=(
            P(("ctx", "head"), None, None),
            P("head", None, None),
            P("head", None),
            P("ctx", None),
            P("ctx", None),
            P(),
            P(),
        ),
        out_specs=(P("ctx", "head", None), P("head", "ctx")),
        check_vma=False,
    )
```

```python
import functools

import jax
import jax.numpy as jnp
from jax import lax
from jax.experimental import pallas as pl
from jax.experimental.pallas import tpu as pltpu
from jax.sharding import PartitionSpec as P


BLOCK = 64
SHARDS = 8
PART = 16
SCALE = 192.0 ** (-0.5)
INDEX_SCALE = 128.0 ** (-0.5)
F32 = jnp.float32
BF16 = jnp.bfloat16
VMEM = pl.BlockSpec(memory_space=pltpu.VMEM)
SMEM = pl.BlockSpec(memory_space=pltpu.SMEM)


def iota(shape, dim):
    return lax.broadcasted_iota(jnp.int32, shape, dim)


def in_hbm(x):
    return pltpu.with_memory_space_constraint(x, pltpu.HBM)


def valid_ids(ids_ref, counts_ref):
    tiles, entries = ids_ref.shape
    tile = iota((tiles, entries), 0)
    count = jnp.zeros((tiles, entries), jnp.int32)
    for t in range(tiles):
        count = jnp.where(tile == t, counts_ref[t], count)
    return jnp.where(iota((tiles, entries), 1) < count, ids_ref[...], -1)


def place():
    group = lax.axis_index("head")
    row_y, row_z = group >> 2, group & 3
    return lax.axis_index("ctx"), (row_y + 2 * row_z) & 3, (2 * row_y + row_z) & 3


def row_of(part, first, second):
    return jnp.where(part < 8, first * 8 + part, 24 + second * 8 + part)


def hot(index, target):
    return (index == target).astype(F32).astype(BF16)


def slot_sources(ids, tile):
    mine = jnp.sum(jnp.where(iota(ids.shape, 0) == tile, ids, 0), axis=0, keepdims=True)
    owner = jnp.where(mine < 0, 2 * SHARDS, mine >> 5)
    shard = iota(ids.shape, 0)
    here = jnp.sum((owner == shard).astype(F32), axis=1, keepdims=True).astype(jnp.int32)
    end = jnp.sum((owner <= shard).astype(F32), axis=1, keepdims=True).astype(jnp.int32)
    column = iota((SHARDS, 512), 1)
    entry = (column & 255) >> 3
    skipped = jnp.sum(jnp.where(entry >= end, 128 - 16 * here, 0), axis=0, keepdims=True)
    part = (column & 7) + ((column >> 8) << 3)
    return entry * PART + part + skipped, end[SHARDS - 1 :, :]


def gather_kernel(ids_hbm, counts_hbm, cache_ref, *refs):
    out_refs, (source_ref, other_ref, past_ref, ids_ref, counts_ref, held, sems) = refs[:-7], refs[-7:]
    keys = cache_ref.shape[1]
    lists = [
        pltpu.make_async_copy(ids_hbm, ids_ref, sems.at[keys // 512]),
        pltpu.make_async_copy(counts_hbm, counts_ref, sems.at[keys // 512 + 1]),
    ]
    for copy in lists:
        copy.start()
    copies = []
    for i, c in enumerate(range(0, keys, 512)):
        copies.append(pltpu.make_async_copy(cache_ref.at[:, pl.ds(c, 512)], held.at[i], sems.at[i]))
        copies[i].start()
    shard, first, second = place()
    for copy in lists:
        copy.wait()
    ids = valid_ids(ids_ref, counts_ref)
    tiles, entries = ids.shape
    blocks = keys // BLOCK
    lane = iota((tiles, 128), 1)
    block_of_lane = jnp.where(lane < blocks, lane + shard * blocks, -2)
    member = jnp.zeros((tiles, 128), F32)
    for j in range(entries):
        member = jnp.where(ids[:, j : j + 1] == block_of_lane, 1.0, member)
    before = (iota((128, 128), 0) < iota((128, 128), 1)).astype(BF16)
    rank = jnp.dot(member.astype(BF16), before, preferred_element_type=F32)
    rank = jnp.where(member > 0.0, rank, -1.0)
    slot = (lane >> 4).astype(F32)
    target = jnp.full((tiles, 128), -1, jnp.int32)
    for b in range(blocks):
        target = jnp.where(rank[:, b : b + 1] == slot, b * PART + (lane & 15), target)
    column = iota((512, 128), 1)
    keep = hot(iota((512, 128), 0), (column >> 4) * BLOCK + row_of(column & 15, first, second))
    own = []
    for i, copy in enumerate(copies):
        copy.wait()
        own.append(jnp.dot(held[i], keep, preferred_element_type=F32).astype(BF16))
    own = jnp.concatenate(own, axis=1)
    index = iota((own.shape[1], 128), 0)
    for d, out_ref in enumerate(out_refs):
        near = (shard + 2 * d) & 7
        pair = []
        for tile in (near, near ^ 1):
            chosen = iota((tiles, 128), 0) == tile
            pair.append(hot(index, jnp.sum(jnp.where(chosen, target, 0), axis=0, keepdims=True)))
        got = jnp.dot(own, jnp.concatenate(pair, axis=1), preferred_element_type=F32)
        out_ref[...] = got.astype(BF16)
    source, count = slot_sources(ids, shard)
    source_ref[...] = source
    past_ref[...] = jnp.broadcast_to((count - 2) * BLOCK, past_ref.shape)
    other_ref[...] = slot_sources(ids, shard ^ 1)[0]


def gather_parts(block_ids, block_counts, cache_t):
    width, keys = cache_t.shape
    hbm = pl.BlockSpec(memory_space=pltpu.HBM)
    chips = SHARDS // 2
    return pl.pallas_call(
        gather_kernel,
        out_shape=[pltpu.HBM((width, 256), BF16)]
        + [pltpu.VMEM((width, 256), BF16)] * (chips - 1)
        + [pltpu.HBM((SHARDS, n), jnp.int32) for n in (512, 512, 128)],
        in_specs=[hbm] * 3,
        out_specs=[VMEM] * (chips + 3),
        scratch_shapes=[
            pltpu.VMEM(block_ids.shape, jnp.int32),
            pltpu.SMEM(block_counts.shape, jnp.int32),
            pltpu.VMEM((keys // 512, width, 512), BF16),
            pltpu.SemaphoreType.DMA((keys // 512 + 2,)),
        ],
        cost_estimate=pl.CostEstimate(
            flops=2 * width * keys * 1024, bytes_accessed=2 * width * keys * 2, transcendentals=0
        ),
        compiler_params=pltpu.CompilerParams(vmem_limit_bytes=16 << 20),
        name="gather_parts",
    )(in_hbm(block_ids), in_hbm(block_counts), in_hbm(cache_t))


def compact_kernel(left, source_ref, *refs):
    part_refs, out_ref = refs[:-1], refs[-1]
    shard = lax.axis_index("ctx")
    row = iota((128, 512), 0)
    source = source_ref[0:1, :]
    total = jnp.zeros(out_ref.shape, F32)
    for d in range(0, len(part_refs), 2):
        pick = jnp.concatenate([hot(row + ((shard - 2 * u) & 7) * 128, source) for u in (d, d + 1)], axis=0)
        pair = jnp.concatenate([part_refs[u][:, left : left + 128] for u in (d, d + 1)], axis=1)
        total = total + jnp.dot(pair, pick, preferred_element_type=F32)
    out_ref[...] = total.astype(BF16)


def compact_parts(left, source, parts):
    width = parts[0].shape[0]
    return pl.pallas_call(
        functools.partial(compact_kernel, left),
        out_shape=pltpu.VMEM((width, 512), BF16),
        in_specs=[VMEM] * (1 + len(parts)),
        out_specs=VMEM,
        cost_estimate=pl.CostEstimate(flops=width * 1024 * 512, bytes_accessed=width * 1536 * 2, transcendentals=0),
        compiler_params=pltpu.CompilerParams(vmem_limit_bytes=8 << 20),
        name="compact_parts",
    )(in_hbm(source), in_hbm(parts[0]), *parts[1:])


def spread_kernel(own_ref, other_ref, up_ref, down_ref, right_ref, left_ref):
    first = own_ref[:, :256] + other_ref[:, :256]
    second = own_ref[:, 256:] + other_ref[:, 256:]
    up_ref[:, :256] = first
    up_ref[:, 256:] = second[:, :128]
    down_ref[:, :256] = first
    down_ref[:, 256:] = second[:, 128:]
    right_ref[:, :256] = second
    right_ref[:, 256:] = first[:, :128]
    left_ref[:, :256] = second
    left_ref[:, 256:] = first[:, 128:]


def spread_parts(own, other):
    width = own.shape[0]
    return pl.pallas_call(
        spread_kernel,
        out_shape=[jax.ShapeDtypeStruct((width, 384), BF16)] * 4,
        in_specs=[VMEM] * 2,
        out_specs=[VMEM] * 4,
        cost_estimate=pl.CostEstimate(flops=width * 512, bytes_accessed=width * 2560 * 2, transcendentals=0),
        compiler_params=pltpu.CompilerParams(vmem_limit_bytes=8 << 20),
        name="spread_parts",
    )(own, other)


def q_prep_kernel(q_ref, out_ref):
    groups, rows, heads, width = out_ref.shape
    for i in range(rows):
        out_ref[:, i] = q_ref[i].T.reshape(groups, heads, width)


def q_by_group(q_latent, groups):
    rows, heads, width = q_latent.shape
    return pl.pallas_call(
        q_prep_kernel,
        out_shape=jax.ShapeDtypeStruct((groups, rows, heads // groups, width), BF16),
        in_specs=[VMEM],
        out_specs=VMEM,
        cost_estimate=pl.CostEstimate(flops=0, bytes_accessed=rows * heads * width * 4, transcendentals=0),
        compiler_params=pltpu.CompilerParams(vmem_limit_bytes=8 << 20),
        name="q_by_group",
    )(q_latent.transpose(0, 2, 1))


def index_kernel(query_ref, weight_ref, keys_ref, out_ref):
    rows, heads, dim = query_ref.shape
    flat = query_ref[...].reshape(rows * heads, dim)
    weight = weight_ref[...] * INDEX_SCALE
    span = 256
    for c in range(keys_ref.shape[0] // span):
        dots = lax.dot_general(
            flat, keys_ref[c * span : (c + 1) * span, :], (((1,), (1,)), ((), ())), preferred_element_type=F32
        ).reshape(rows, heads, span)
        out_ref[:, c * span : (c + 1) * span] = jnp.sum(
            jnp.maximum(dots, 0.0) * weight[:, :, None], axis=1
        )


def more_index_kernel(query_ref, weight_ref, keys_ref, before_ref, out_ref):
    index_kernel(query_ref, weight_ref, keys_ref, out_ref)


def index_scores_of(index_query, index_weight, index_keys, first, steps, before=None):
    rows, heads, dim = index_query.shape
    keys = index_keys.shape[0]
    step = 8
    more = [] if before is None else [before]
    return pl.pallas_call(
        index_kernel if before is None else more_index_kernel,
        grid=(steps,),
        out_shape=jax.ShapeDtypeStruct((rows, keys), F32),
        in_specs=[
            pl.BlockSpec((step, heads, dim), lambda i: (i + first, 0, 0)),
            pl.BlockSpec((step, heads), lambda i: (i + first, 0)),
            pl.BlockSpec((keys, dim), lambda i: (0, 0)),
        ]
        + [pl.BlockSpec(memory_space=pl.ANY)] * len(more),
        out_specs=pl.BlockSpec((step, keys), lambda i: (i + first, 0)),
        input_output_aliases={3: 0} if more else {},
        cost_estimate=pl.CostEstimate(
            flops=8 * steps * step * heads * dim * keys, bytes_accessed=steps * step * (heads * dim * 2 + keys * 4), transcendentals=0
        ),
        compiler_params=pltpu.CompilerParams(vmem_limit_bytes=16 << 20),
        name="index_scores",
    )(in_hbm(index_query), in_hbm(index_weight), in_hbm(index_keys), *more)


def masked_scores(q, keys, tiles, limit):
    scores = jnp.dot(q, keys, preferred_element_type=F32)
    rows = q.shape[0]
    lane = iota((rows, 128), 1)
    offset = (lane >> 3) * BLOCK + (lane & 7)
    pieces = []
    for t, first_key in enumerate(tiles):
        piece = scores[:, t * 128 : (t + 1) * 128]
        if first_key is not None:
            piece = jnp.where(offset <= limit - first_key, piece, -jnp.inf)
        pieces.append(piece)
    return jnp.concatenate(pieces, axis=1)


def own_kernel(past_ref, q_ref, up_ref, down_ref, top_ref, total_ref, mixed_ref, keys_ref):
    _, first, second = place()
    past = past_ref[0:1, :]
    late = 16 * BLOCK
    tiles = (None, late + first * 8, None, late + 32 + second * 8)
    keys_ref[:, :384] = up_ref[...]
    keys_ref[:, 384:] = down_ref[:, 256:]
    rows, step = q_ref.shape[0], 256
    for a in range(0, rows, step):
        limit = past + a // 8 + (iota((step, 128), 0) >> 3)
        scores = masked_scores(q_ref[a : a + step, :], keys_ref[...], tiles, limit)
        top = jnp.max(scores, axis=1, keepdims=True)
        weights = jnp.exp((scores - top) * SCALE)
        top_ref[a : a + step, :] = jnp.broadcast_to(top, (step, 128))
        total_ref[a : a + step, :] = jnp.broadcast_to(jnp.sum(weights, axis=1, keepdims=True), (step, 128))
        mixed_ref[a : a + step, :] = lax.dot_general(
            weights.astype(BF16), keys_ref[0:512, :], (((1,), (1,)), ((), ())), preferred_element_type=F32
        )


def attend_own(past, q, up, down):
    rows, width = q.shape
    count = 512
    return pl.pallas_call(
        own_kernel,
        out_shape=[
            jax.ShapeDtypeStruct((rows, 128), F32),
            jax.ShapeDtypeStruct((rows, 128), F32),
            jax.ShapeDtypeStruct((rows, 512), F32),
        ],
        in_specs=[VMEM] * 4,
        out_specs=[VMEM] * 3,
        scratch_shapes=[pltpu.VMEM((width, count), BF16)],
        cost_estimate=pl.CostEstimate(
            flops=2 * rows * count * (width + 512), bytes_accessed=rows * 4352, transcendentals=rows * count
        ),
        compiler_params=pltpu.CompilerParams(vmem_limit_bytes=16 << 20),
        name="attend_own",
    )(in_hbm(past), q, up, down)


def rest_kernel(past_ref, q_ref, top_ref, total_ref, mixed_ref, up_ref, down_ref, right_ref, left_ref, out_ref, keys_ref, done_ref, sems):
    _, first, second = place()
    past = past_ref[0:1, :]
    late = 16 * BLOCK

    def of_first(step):
        return late + ((first + step) & 3) * 8

    def of_second(step):
        return late + 32 + ((second + step) & 3) * 8

    tiles = (
        (None, of_first(-1), None)
        + (None, of_first(1), of_second(2))
        + (None, of_second(-1), None)
        + (None, of_second(1), of_first(2))
    )
    for i, ref in enumerate((up_ref, down_ref, right_ref, left_ref)):
        keys_ref[:, i * 384 : (i + 1) * 384] = ref[...]
    rows, step = q_ref.shape[0], 256
    copies = []
    for a in range(0, rows, step):
        limit = past + a // 8 + (iota((step, 128), 0) >> 3)
        scores = masked_scores(q_ref[a : a + step, :], keys_ref[...], tiles, limit)
        before = top_ref[a : a + step, 0:1]
        top = jnp.maximum(jnp.max(scores, axis=1, keepdims=True), before)
        weights = jnp.exp((scores - top) * SCALE)
        fade = jnp.exp((before - top) * SCALE)
        total = total_ref[a : a + step, 0:1] * fade + jnp.sum(weights, axis=1, keepdims=True)
        mixed = mixed_ref[a : a + step, :] * fade + lax.dot_general(
            weights.astype(BF16), keys_ref[0:512, :], (((1,), (1,)), ((), ())), preferred_element_type=F32
        )
        done_ref[a : a + step, :] = (mixed / total).astype(BF16)
        copies.append(
            pltpu.make_async_copy(
                done_ref.at[pl.ds(a, step), :], out_ref.at[pl.ds(a, step), :], sems.at[a // step]
            )
        )
        copies[-1].start()
    for copy in copies:
        copy.wait()


def attend_rest(past, q, state, parts):
    rows, width = q.shape
    count = sum(part.shape[1] for part in parts)
    return pl.pallas_call(
        rest_kernel,
        out_shape=jax.ShapeDtypeStruct((rows, 512), BF16),
        in_specs=[VMEM] * (5 + len(parts)),
        out_specs=pl.BlockSpec(memory_space=pltpu.HBM),
        scratch_shapes=[
            pltpu.VMEM((width, count), BF16),
            pltpu.VMEM((rows, 512), BF16),
            pltpu.SemaphoreType.DMA((rows // 256,)),
        ],
        cost_estimate=pl.CostEstimate(
            flops=2 * rows * count * (width + 512), bytes_accessed=rows * 5376, transcendentals=rows * count
        ),
        compiler_params=pltpu.CompilerParams(vmem_limit_bytes=24 << 20),
        name="attend_rest",
    )(in_hbm(past), q, *state, *parts)


def turn(d):
    return [(i, (i + d) % SHARDS) for i in range(SHARDS)]


def line(dy, dz):
    return [(y * 4 + z, ((y + dy) % 4) * 4 + (z + dz) % 4) for y in range(4) for z in range(4)]


def body(q_latent, index_query, index_weight, index_keys, latent_cache, block_ids, block_counts):
    rows, heads, width = q_latent.shape
    groups = lax.axis_size("head")
    *outgoing, source, other, past = gather_parts(block_ids, block_counts, latent_cache.T)
    incoming = [outgoing[0]] + [lax.ppermute(outgoing[d], "ctx", turn(2 * d)) for d in range(1, SHARDS // 2)]
    by_group = q_by_group(q_latent, groups)
    head_query = lax.all_to_all(by_group, "head", split_axis=0, concat_axis=0, tiled=True)
    some_scores = index_scores_of(index_query, index_weight, index_keys, 0, 4)
    index_scores = index_scores_of(index_query, index_weight, index_keys, 4, 4, some_scores)
    theirs = compact_parts(128, other, incoming)
    theirs = lax.ppermute(theirs, "ctx", [(i, i ^ 1) for i in range(SHARDS)])
    mine = compact_parts(0, source, incoming)
    up, down, right, left = spread_parts(mine, theirs)
    parts = [
        lax.ppermute(part, "head", line(*step))
        for part, step in ((up, (1, 0)), (down, (-1, 0)), (right, (0, 1)), (left, (0, -1)))
    ]
    flat_query = head_query.reshape(-1, width)
    state = attend_own(past, flat_query, up, down)
    attention = attend_rest(past, flat_query, state, parts)
    return attention.reshape(rows * groups, heads // groups, 512), index_scores


def solution(mesh):
    return jax.shard_map(
        body,
        mesh=mesh,
        in_specs=(
            P(("ctx", "head"), None, None),
            P("head", None, None),
            P("head", None),
            P("ctx", None),
            P("ctx", None),
            P(),
            P(),
        ),
        out_specs=(P("ctx", "head", None), P("head", "ctx")),
        check_vma=False,
    )
```

```python
import functools

import jax
import jax.numpy as jnp
from jax import lax
from jax.experimental import pallas as pl
from jax.experimental.pallas import tpu as pltpu
from jax.sharding import PartitionSpec as P


BLOCK = 64
SHARDS = 8
PART = 16
SCALE = 192.0 ** (-0.5)
INDEX_SCALE = 128.0 ** (-0.5)
F32 = jnp.float32
BF16 = jnp.bfloat16
VMEM = pl.BlockSpec(memory_space=pltpu.VMEM)
SMEM = pl.BlockSpec(memory_space=pltpu.SMEM)


def iota(shape, dim):
    return lax.broadcasted_iota(jnp.int32, shape, dim)


def in_hbm(x):
    return pltpu.with_memory_space_constraint(x, pltpu.HBM)


def in_vmem(x):
    return pltpu.with_memory_space_constraint(x, pltpu.VMEM)


def valid_ids(ids_ref, counts_ref):
    tiles, entries = ids_ref.shape
    tile = iota((tiles, entries), 0)
    count = jnp.zeros((tiles, entries), jnp.int32)
    for t in range(tiles):
        count = jnp.where(tile == t, counts_ref[t], count)
    return jnp.where(iota((tiles, entries), 1) < count, ids_ref[...], -1)


def place():
    group = lax.axis_index("head")
    row_y, row_z = group >> 2, group & 3
    return lax.axis_index("ctx"), (row_y + 2 * row_z) & 3, (2 * row_y + row_z) & 3


def row_of(part, first, second):
    return jnp.where(part < 8, first * 8 + part, 24 + second * 8 + part)


def hot(index, target):
    return (index == target).astype(F32).astype(BF16)


def slot_sources(ids, tile):
    mine = jnp.sum(jnp.where(iota(ids.shape, 0) == tile, ids, 0), axis=0, keepdims=True)
    owner = jnp.where(mine < 0, 2 * SHARDS, mine >> 5)
    shard = iota(ids.shape, 0)
    here = jnp.sum((owner == shard).astype(F32), axis=1, keepdims=True).astype(jnp.int32)
    end = jnp.sum((owner <= shard).astype(F32), axis=1, keepdims=True).astype(jnp.int32)
    column = iota((SHARDS, 512), 1)
    entry = (column & 255) >> 3
    skipped = jnp.sum(jnp.where(entry >= end, 128 - 16 * here, 0), axis=0, keepdims=True)
    part = (column & 7) + ((column >> 8) << 3)
    return entry * PART + part + skipped, end[SHARDS - 1 :, :]


def gather_kernel(ids_hbm, counts_hbm, cache_ref, *refs):
    out_refs, (source_ref, other_ref, past_ref, ids_ref, counts_ref, held, sems) = refs[:-7], refs[-7:]
    keys = cache_ref.shape[1]
    lists = [
        pltpu.make_async_copy(ids_hbm, ids_ref, sems.at[keys // 512]),
        pltpu.make_async_copy(counts_hbm, counts_ref, sems.at[keys // 512 + 1]),
    ]
    for copy in lists:
        copy.start()
    copies = []
    for i, c in enumerate(range(0, keys, 512)):
        copies.append(pltpu.make_async_copy(cache_ref.at[:, pl.ds(c, 512)], held.at[i], sems.at[i]))
        copies[i].start()
    shard, first, second = place()
    for copy in lists:
        copy.wait()
    ids = valid_ids(ids_ref, counts_ref)
    tiles, entries = ids.shape
    blocks = keys // BLOCK
    lane = iota((tiles, 128), 1)
    block_of_lane = jnp.where(lane < blocks, lane + shard * blocks, -2)
    member = jnp.zeros((tiles, 128), F32)
    for j in range(entries):
        member = jnp.where(ids[:, j : j + 1] == block_of_lane, 1.0, member)
    before = (iota((128, 128), 0) < iota((128, 128), 1)).astype(BF16)
    rank = jnp.dot(member.astype(BF16), before, preferred_element_type=F32)
    rank = jnp.where(member > 0.0, rank, -1.0)
    slot = (lane >> 4).astype(F32)
    target = jnp.full((tiles, 128), -1, jnp.int32)
    for b in range(blocks):
        target = jnp.where(rank[:, b : b + 1] == slot, b * PART + (lane & 15), target)
    column = iota((512, 128), 1)
    keep = hot(iota((512, 128), 0), (column >> 4) * BLOCK + row_of(column & 15, first, second))
    own = []
    for i, copy in enumerate(copies):
        copy.wait()
        own.append(jnp.dot(held[i], keep, preferred_element_type=F32).astype(BF16))
    own = jnp.concatenate(own, axis=1)
    index = iota((own.shape[1], 128), 0)
    for d, out_ref in enumerate(out_refs):
        near = (shard + 2 * d) & 7
        pair = []
        for tile in (near, near ^ 1):
            chosen = iota((tiles, 128), 0) == tile
            pair.append(hot(index, jnp.sum(jnp.where(chosen, target, 0), axis=0, keepdims=True)))
        got = jnp.dot(own, jnp.concatenate(pair, axis=1), preferred_element_type=F32)
        out_ref[...] = got.astype(BF16)
    source, count = slot_sources(ids, shard)
    source_ref[...] = source
    past_ref[...] = jnp.broadcast_to((count - 2) * BLOCK, past_ref.shape)
    other_ref[...] = slot_sources(ids, shard ^ 1)[0]


def gather_parts(block_ids, block_counts, cache_t):
    width, keys = cache_t.shape
    hbm = pl.BlockSpec(memory_space=pltpu.HBM)
    chips = SHARDS // 2
    return pl.pallas_call(
        gather_kernel,
        out_shape=[pltpu.HBM((width, 256), BF16)]
        + [pltpu.VMEM((width, 256), BF16)] * (chips - 1)
        + [pltpu.HBM((SHARDS, n), jnp.int32) for n in (512, 512, 128)],
        in_specs=[hbm] * 3,
        out_specs=[VMEM] * (chips + 3),
        scratch_shapes=[
            pltpu.VMEM(block_ids.shape, jnp.int32),
            pltpu.SMEM(block_counts.shape, jnp.int32),
            pltpu.VMEM((keys // 512, width, 512), BF16),
            pltpu.SemaphoreType.DMA((keys // 512 + 2,)),
        ],
        cost_estimate=pl.CostEstimate(
            flops=2 * width * keys * 1024, bytes_accessed=2 * width * keys * 2, transcendentals=0
        ),
        compiler_params=pltpu.CompilerParams(vmem_limit_bytes=16 << 20),
        name="gather_parts",
    )(in_hbm(block_ids), in_hbm(block_counts), in_hbm(cache_t))


def compact_kernel(left, source_ref, *refs):
    part_refs, out_ref = refs[:-1], refs[-1]
    shard = lax.axis_index("ctx")
    row = iota((128, 512), 0)
    source = source_ref[0:1, :]
    total = jnp.zeros(out_ref.shape, F32)
    for d in range(0, len(part_refs), 2):
        pick = jnp.concatenate([hot(row + ((shard - 2 * u) & 7) * 128, source) for u in (d, d + 1)], axis=0)
        pair = jnp.concatenate([part_refs[u][:, left : left + 128] for u in (d, d + 1)], axis=1)
        total = total + jnp.dot(pair, pick, preferred_element_type=F32)
    out_ref[...] = total.astype(BF16)


def compact_parts(left, source, parts):
    width = parts[0].shape[0]
    return pl.pallas_call(
        functools.partial(compact_kernel, left),
        out_shape=pltpu.VMEM((width, 512), BF16),
        in_specs=[VMEM] * (1 + len(parts)),
        out_specs=VMEM,
        cost_estimate=pl.CostEstimate(flops=width * 1024 * 512, bytes_accessed=width * 1536 * 2, transcendentals=0),
        compiler_params=pltpu.CompilerParams(vmem_limit_bytes=8 << 20),
        name="compact_parts",
    )(in_hbm(source), in_hbm(parts[0]), *parts[1:])


def spread_kernel(own_ref, other_ref, up_ref, down_ref, right_ref, left_ref):
    first = own_ref[:, :256] + other_ref[:, :256]
    second = own_ref[:, 256:] + other_ref[:, 256:]
    up_ref[:, :256] = first
    up_ref[:, 256:] = second[:, :128]
    down_ref[:, :256] = first
    down_ref[:, 256:] = second[:, 128:]
    right_ref[:, :256] = second
    right_ref[:, 256:] = first[:, :128]
    left_ref[:, :256] = second
    left_ref[:, 256:] = first[:, 128:]


def spread_parts(own, other):
    width = own.shape[0]
    return pl.pallas_call(
        spread_kernel,
        out_shape=[jax.ShapeDtypeStruct((width, 384), BF16)] * 4,
        in_specs=[VMEM] * 2,
        out_specs=[VMEM] * 4,
        cost_estimate=pl.CostEstimate(flops=width * 512, bytes_accessed=width * 2560 * 2, transcendentals=0),
        compiler_params=pltpu.CompilerParams(vmem_limit_bytes=8 << 20),
        name="spread_parts",
    )(own, other)


def q_prep_kernel(q_ref, out_ref):
    groups, rows, heads, width = out_ref.shape
    for i in range(rows):
        out_ref[:, i] = q_ref[i].T.reshape(groups, heads, width)


def q_by_group(q_latent, groups):
    rows, heads, width = q_latent.shape
    return pl.pallas_call(
        q_prep_kernel,
        out_shape=jax.ShapeDtypeStruct((groups, rows, heads // groups, width), BF16),
        in_specs=[VMEM],
        out_specs=VMEM,
        cost_estimate=pl.CostEstimate(flops=0, bytes_accessed=rows * heads * width * 4, transcendentals=0),
        compiler_params=pltpu.CompilerParams(vmem_limit_bytes=8 << 20),
        name="q_by_group",
    )(q_latent.transpose(0, 2, 1))


def index_kernel(query_ref, weight_ref, keys_ref, out_ref):
    rows, heads, dim = query_ref.shape
    flat = query_ref[...].reshape(rows * heads, dim)
    weight = weight_ref[...] * INDEX_SCALE
    span = 256
    for c in range(keys_ref.shape[0] // span):
        dots = lax.dot_general(
            flat, keys_ref[c * span : (c + 1) * span, :], (((1,), (1,)), ((), ())), preferred_element_type=F32
        ).reshape(rows, heads, span)
        out_ref[:, c * span : (c + 1) * span] = jnp.sum(
            jnp.maximum(dots, 0.0) * weight[:, :, None], axis=1
        )


def index_scores_of(index_query, index_weight, index_keys):
    rows, heads, dim = index_query.shape
    keys = index_keys.shape[0]
    step = 8
    return pl.pallas_call(
        index_kernel,
        grid=(rows // step,),
        out_shape=jax.ShapeDtypeStruct((rows, keys), F32),
        in_specs=[
            pl.BlockSpec((step, heads, dim), lambda i: (i, 0, 0)),
            pl.BlockSpec((step, heads), lambda i: (i, 0)),
            pl.BlockSpec((keys, dim), lambda i: (0, 0)),
        ],
        out_specs=pl.BlockSpec((step, keys), lambda i: (i, 0)),
        cost_estimate=pl.CostEstimate(
            flops=8 * rows * heads * dim * keys, bytes_accessed=rows * heads * dim * 2 + rows * keys * 4, transcendentals=0
        ),
        compiler_params=pltpu.CompilerParams(vmem_limit_bytes=16 << 20),
        name="index_scores",
    )(index_query, index_weight, index_keys)


def masked_scores(q, keys, tiles, limit):
    scores = jnp.dot(q, keys, preferred_element_type=F32)
    rows = q.shape[0]
    lane = iota((rows, 128), 1)
    offset = (lane >> 3) * BLOCK + (lane & 7)
    pieces = []
    for t, first_key in enumerate(tiles):
        piece = scores[:, t * 128 : (t + 1) * 128]
        if first_key is not None:
            piece = jnp.where(offset <= limit - first_key, piece, -jnp.inf)
        pieces.append(piece)
    return jnp.concatenate(pieces, axis=1)


def own_kernel(past_ref, q_ref, up_ref, down_ref, top_ref, total_ref, mixed_ref, keys_ref):
    _, first, second = place()
    past = past_ref[0:1, :]
    late = 16 * BLOCK
    tiles = (None, late + first * 8, None, late + 32 + second * 8)
    keys_ref[:, :384] = up_ref[...]
    keys_ref[:, 384:] = down_ref[:, 256:]
    rows, step = q_ref.shape[0], 256
    for a in range(0, rows, step):
        limit = past + a // 8 + (iota((step, 128), 0) >> 3)
        scores = masked_scores(q_ref[a : a + step, :], keys_ref[...], tiles, limit)
        top = jnp.max(scores, axis=1, keepdims=True)
        weights = jnp.exp((scores - top) * SCALE)
        top_ref[a : a + step, :] = jnp.broadcast_to(top, (step, 128))
        total_ref[a : a + step, :] = jnp.broadcast_to(jnp.sum(weights, axis=1, keepdims=True), (step, 128))
        mixed_ref[a : a + step, :] = lax.dot_general(
            weights.astype(BF16), keys_ref[0:512, :], (((1,), (1,)), ((), ())), preferred_element_type=F32
        )


def attend_own(past, q, up, down):
    rows, width = q.shape
    count = 512
    return pl.pallas_call(
        own_kernel,
        out_shape=[
            jax.ShapeDtypeStruct((rows, 128), F32),
            jax.ShapeDtypeStruct((rows, 128), F32),
            jax.ShapeDtypeStruct((rows, 512), F32),
        ],
        in_specs=[VMEM] * 4,
        out_specs=[VMEM] * 3,
        scratch_shapes=[pltpu.VMEM((width, count), BF16)],
        cost_estimate=pl.CostEstimate(
            flops=2 * rows * count * (width + 512), bytes_accessed=rows * 4352, transcendentals=rows * count
        ),
        compiler_params=pltpu.CompilerParams(vmem_limit_bytes=16 << 20),
        name="attend_own",
    )(in_hbm(past), q, in_vmem(up), in_vmem(down))


def rest_kernel(past_ref, q_ref, top_ref, total_ref, mixed_ref, up_ref, down_ref, right_ref, left_ref, out_ref, keys_ref, done_ref, sems):
    _, first, second = place()
    past = past_ref[0:1, :]
    late = 16 * BLOCK

    def of_first(step):
        return late + ((first + step) & 3) * 8

    def of_second(step):
        return late + 32 + ((second + step) & 3) * 8

    tiles = (
        (None, of_first(-1), None)
        + (None, of_first(1), of_second(2))
        + (None, of_second(-1), None)
        + (None, of_second(1), of_first(2))
    )
    for i, ref in enumerate((up_ref, down_ref, right_ref, left_ref)):
        keys_ref[:, i * 384 : (i + 1) * 384] = ref[...]
    rows, step = q_ref.shape[0], 256
    copies = []
    for a in range(0, rows, step):
        limit = past + a // 8 + (iota((step, 128), 0) >> 3)
        scores = masked_scores(q_ref[a : a + step, :], keys_ref[...], tiles, limit)
        before = top_ref[a : a + step, 0:1]
        top = jnp.maximum(jnp.max(scores, axis=1, keepdims=True), before)
        weights = jnp.exp((scores - top) * SCALE)
        fade = jnp.exp((before - top) * SCALE)
        total = total_ref[a : a + step, 0:1] * fade + jnp.sum(weights, axis=1, keepdims=True)
        mixed = mixed_ref[a : a + step, :] * fade + lax.dot_general(
            weights.astype(BF16), keys_ref[0:512, :], (((1,), (1,)), ((), ())), preferred_element_type=F32
        )
        done_ref[a : a + step, :] = (mixed / total).astype(BF16)
        copies.append(
            pltpu.make_async_copy(
                done_ref.at[pl.ds(a, step), :], out_ref.at[pl.ds(a, step), :], sems.at[a // step]
            )
        )
        copies[-1].start()
    for copy in copies:
        copy.wait()


def attend_rest(past, q, state, parts):
    rows, width = q.shape
    count = sum(part.shape[1] for part in parts)
    return pl.pallas_call(
        rest_kernel,
        out_shape=jax.ShapeDtypeStruct((rows, 512), BF16),
        in_specs=[VMEM] * (5 + len(parts)),
        out_specs=pl.BlockSpec(memory_space=pltpu.HBM),
        scratch_shapes=[
            pltpu.VMEM((width, count), BF16),
            pltpu.VMEM((rows, 512), BF16),
            pltpu.SemaphoreType.DMA((rows // 256,)),
        ],
        cost_estimate=pl.CostEstimate(
            flops=2 * rows * count * (width + 512), bytes_accessed=rows * 5376, transcendentals=rows * count
        ),
        compiler_params=pltpu.CompilerParams(vmem_limit_bytes=24 << 20),
        name="attend_rest",
    )(in_hbm(past), q, *state, *[in_vmem(part) for part in parts])


def turn(d):
    return [(i, (i + d) % SHARDS) for i in range(SHARDS)]


def line(dy, dz):
    return [(y * 4 + z, ((y + dy) % 4) * 4 + (z + dz) % 4) for y in range(4) for z in range(4)]


def body(q_latent, index_query, index_weight, index_keys, latent_cache, block_ids, block_counts):
    rows, heads, width = q_latent.shape
    groups = lax.axis_size("head")
    *outgoing, source, other, past = gather_parts(block_ids, block_counts, latent_cache.T)
    incoming = [outgoing[0]] + [lax.ppermute(outgoing[d], "ctx", turn(2 * d)) for d in range(1, SHARDS // 2)]
    by_group = q_by_group(q_latent, groups)
    head_query = lax.all_to_all(by_group, "head", split_axis=0, concat_axis=0, tiled=True)
    index_scores = index_scores_of(index_query, index_weight, index_keys)
    theirs = compact_parts(128, other, incoming)
    theirs = lax.ppermute(theirs, "ctx", [(i, i ^ 1) for i in range(SHARDS)])
    mine = compact_parts(0, source, incoming)
    up, down, right, left = spread_parts(mine, theirs)
    parts = [
        lax.ppermute(part, "head", line(*step))
        for part, step in ((up, (1, 0)), (down, (-1, 0)), (right, (0, 1)), (left, (0, -1)))
    ]
    flat_query = head_query.reshape(-1, width)
    state = attend_own(past, flat_query, up, down)
    attention = attend_rest(past, flat_query, state, parts)
    return attention.reshape(rows * groups, heads // groups, 512), index_scores


def solution(mesh):
    return jax.shard_map(
        body,
        mesh=mesh,
        in_specs=(
            P(("ctx", "head"), None, None),
            P("head", None, None),
            P("head", None),
            P("ctx", None),
            P("ctx", None),
            P(),
            P(),
        ),
        out_specs=(P("ctx", "head", None), P("head", "ctx")),
        check_vma=False,
    )
```

```python
import functools

import jax
import jax.numpy as jnp
from jax import lax
from jax.experimental import pallas as pl
from jax.experimental.pallas import tpu as pltpu
from jax.sharding import PartitionSpec as P


BLOCK = 64
SHARDS = 8
PART = 16
SCALE = 192.0 ** (-0.5)
INDEX_SCALE = 128.0 ** (-0.5)
F32 = jnp.float32
BF16 = jnp.bfloat16
VMEM = pl.BlockSpec(memory_space=pltpu.VMEM)
SMEM = pl.BlockSpec(memory_space=pltpu.SMEM)


def iota(shape, dim):
    return lax.broadcasted_iota(jnp.int32, shape, dim)


def in_hbm(x):
    return pltpu.with_memory_space_constraint(x, pltpu.HBM)


def valid_ids(ids_ref, counts_ref):
    tiles, entries = ids_ref.shape
    tile = iota((tiles, entries), 0)
    count = jnp.zeros((tiles, entries), jnp.int32)
    for t in range(tiles):
        count = jnp.where(tile == t, counts_ref[t], count)
    return jnp.where(iota((tiles, entries), 1) < count, ids_ref[...], -1)


def place():
    group = lax.axis_index("head")
    row_y, row_z = group >> 2, group & 3
    return lax.axis_index("ctx"), (row_y + 2 * row_z) & 3, (2 * row_y + row_z) & 3


def row_of(part, first, second):
    return jnp.where(part < 8, first * 8 + part, 24 + second * 8 + part)


def hot(index, target):
    return (index == target).astype(F32).astype(BF16)


def slot_sources(ids, tile):
    mine = jnp.sum(jnp.where(iota(ids.shape, 0) == tile, ids, 0), axis=0, keepdims=True)
    owner = jnp.where(mine < 0, 2 * SHARDS, mine >> 5)
    shard = iota(ids.shape, 0)
    here = jnp.sum((owner == shard).astype(F32), axis=1, keepdims=True).astype(jnp.int32)
    end = jnp.sum((owner <= shard).astype(F32), axis=1, keepdims=True).astype(jnp.int32)
    column = iota((SHARDS, 512), 1)
    entry = (column & 255) >> 3
    skipped = jnp.sum(jnp.where(entry >= end, 128 - 16 * here, 0), axis=0, keepdims=True)
    part = (column & 7) + ((column >> 8) << 3)
    return entry * PART + part + skipped, end[SHARDS - 1 :, :]


def gather_kernel(ids_hbm, counts_hbm, cache_ref, *refs):
    out_refs, (source_ref, other_ref, past_ref, ids_ref, counts_ref, held, sems) = refs[:-7], refs[-7:]
    keys = cache_ref.shape[1]
    lists = [
        pltpu.make_async_copy(ids_hbm, ids_ref, sems.at[keys // 512]),
        pltpu.make_async_copy(counts_hbm, counts_ref, sems.at[keys // 512 + 1]),
    ]
    for copy in lists:
        copy.start()
    copies = []
    for i, c in enumerate(range(0, keys, 512)):
        copies.append(pltpu.make_async_copy(cache_ref.at[:, pl.ds(c, 512)], held.at[i], sems.at[i]))
        copies[i].start()
    shard, first, second = place()
    tiles, entries = ids_ref.shape
    blocks = keys // BLOCK
    column = iota((512, 128), 1)
    keep = hot(iota((512, 128), 0), (column >> 4) * BLOCK + row_of(column & 15, first, second))

    def kept(i):
        return jnp.dot(held[i], keep, preferred_element_type=F32).astype(BF16)

    early = len(copies) // 2
    for copy in lists + copies[:early]:
        copy.wait()
    own = [kept(i) for i in range(early)]
    ids = valid_ids(ids_ref, counts_ref)
    lane = iota((tiles, 128), 1)
    block_of_lane = jnp.where(lane < blocks, lane + shard * blocks, -2)
    member = jnp.zeros((tiles, 128), F32)
    for j in range(entries):
        member = jnp.where(ids[:, j : j + 1] == block_of_lane, 1.0, member)
    before = (iota((128, 128), 0) < iota((128, 128), 1)).astype(BF16)
    rank = jnp.dot(member.astype(BF16), before, preferred_element_type=F32)
    rank = jnp.where(member > 0.0, rank, -1.0)
    slot = (lane >> 4).astype(F32)
    target = jnp.full((tiles, 128), -1, jnp.int32)
    for b in range(blocks):
        target = jnp.where(rank[:, b : b + 1] == slot, b * PART + (lane & 15), target)
    for copy in copies[early:]:
        copy.wait()
    own = jnp.concatenate(own + [kept(i) for i in range(early, len(copies))], axis=1)
    index = iota((own.shape[1], 128), 0)
    for d, out_ref in enumerate(out_refs):
        near = (shard + 2 * d) & 7
        pair = []
        for tile in (near, near ^ 1):
            chosen = iota((tiles, 128), 0) == tile
            pair.append(hot(index, jnp.sum(jnp.where(chosen, target, 0), axis=0, keepdims=True)))
        got = jnp.dot(own, jnp.concatenate(pair, axis=1), preferred_element_type=F32)
        out_ref[...] = got.astype(BF16)
    source, count = slot_sources(ids, shard)
    source_ref[...] = source
    past_ref[...] = jnp.broadcast_to((count - 2) * BLOCK, past_ref.shape)
    other_ref[...] = slot_sources(ids, shard ^ 1)[0]


def gather_parts(block_ids, block_counts, cache_t):
    width, keys = cache_t.shape
    hbm = pl.BlockSpec(memory_space=pltpu.HBM)
    chips = SHARDS // 2
    return pl.pallas_call(
        gather_kernel,
        out_shape=[pltpu.HBM((width, 256), BF16)]
        + [pltpu.VMEM((width, 256), BF16)] * (chips - 1)
        + [pltpu.HBM((SHARDS, n), jnp.int32) for n in (512, 512, 128)],
        in_specs=[hbm] * 3,
        out_specs=[VMEM] * (chips + 3),
        scratch_shapes=[
            pltpu.VMEM(block_ids.shape, jnp.int32),
            pltpu.SMEM(block_counts.shape, jnp.int32),
            pltpu.VMEM((keys // 512, width, 512), BF16),
            pltpu.SemaphoreType.DMA((keys // 512 + 2,)),
        ],
        cost_estimate=pl.CostEstimate(
            flops=2 * width * keys * 1024, bytes_accessed=2 * width * keys * 2, transcendentals=0
        ),
        compiler_params=pltpu.CompilerParams(vmem_limit_bytes=16 << 20),
        name="gather_parts",
    )(in_hbm(block_ids), in_hbm(block_counts), in_hbm(cache_t))


def compact_kernel(left, source_ref, *refs):
    part_refs, out_ref = refs[:-1], refs[-1]
    shard = lax.axis_index("ctx")
    row = iota((128, 512), 0)
    source = source_ref[0:1, :]
    total = jnp.zeros(out_ref.shape, F32)
    for d in range(0, len(part_refs), 2):
        pick = jnp.concatenate([hot(row + ((shard - 2 * u) & 7) * 128, source) for u in (d, d + 1)], axis=0)
        pair = jnp.concatenate([part_refs[u][:, left : left + 128] for u in (d, d + 1)], axis=1)
        total = total + jnp.dot(pair, pick, preferred_element_type=F32)
    out_ref[...] = total.astype(BF16)


def compact_parts(left, source, parts):
    width = parts[0].shape[0]
    return pl.pallas_call(
        functools.partial(compact_kernel, left),
        out_shape=pltpu.VMEM((width, 512), BF16),
        in_specs=[VMEM] * (1 + len(parts)),
        out_specs=VMEM,
        cost_estimate=pl.CostEstimate(flops=width * 1024 * 512, bytes_accessed=width * 1536 * 2, transcendentals=0),
        compiler_params=pltpu.CompilerParams(vmem_limit_bytes=8 << 20),
        name="compact_parts",
    )(in_hbm(source), in_hbm(parts[0]), *parts[1:])


def spread_kernel(own_ref, other_ref, up_ref, down_ref, right_ref, left_ref):
    first = own_ref[:, :256] + other_ref[:, :256]
    second = own_ref[:, 256:] + other_ref[:, 256:]
    up_ref[:, :256] = first
    up_ref[:, 256:] = second[:, :128]
    down_ref[:, :256] = first
    down_ref[:, 256:] = second[:, 128:]
    right_ref[:, :256] = second
    right_ref[:, 256:] = first[:, :128]
    left_ref[:, :256] = second
    left_ref[:, 256:] = first[:, 128:]


def spread_parts(own, other):
    width = own.shape[0]
    return pl.pallas_call(
        spread_kernel,
        out_shape=[jax.ShapeDtypeStruct((width, 384), BF16)] * 4,
        in_specs=[VMEM] * 2,
        out_specs=[VMEM] * 4,
        cost_estimate=pl.CostEstimate(flops=width * 512, bytes_accessed=width * 2560 * 2, transcendentals=0),
        compiler_params=pltpu.CompilerParams(vmem_limit_bytes=8 << 20),
        name="spread_parts",
    )(own, other)


def q_prep_kernel(q_ref, out_ref):
    rows = q_ref.shape[0]
    for i in range(rows):
        query = q_ref[i].T
        for g in range(out_ref.shape[0]):
            part = query[g * 8 : (g + 1) * 8, :]
            for t in range(4):
                out_ref[g, t * 64 + i * 8 : t * 64 + (i + 1) * 8, :] = part[:, t * 128 : (t + 1) * 128]
            low = 256 + (i % 4) * 8
            left = (i // 4) * 64
            out_ref[g, low : low + 8, left : left + 64] = part[:, 512:]


def q_by_group(q_latent, groups):
    rows, heads, width = q_latent.shape
    return pl.pallas_call(
        q_prep_kernel,
        out_shape=jax.ShapeDtypeStruct((groups, rows * heads * width // (groups * 128), 128), BF16),
        in_specs=[VMEM],
        out_specs=VMEM,
        cost_estimate=pl.CostEstimate(flops=0, bytes_accessed=rows * heads * width * 4, transcendentals=0),
        compiler_params=pltpu.CompilerParams(vmem_limit_bytes=8 << 20),
        name="q_by_group",
    )(q_latent.transpose(0, 2, 1))


def index_kernel(query_ref, weight_ref, keys_ref, out_ref):
    rows, heads, dim = query_ref.shape
    flat = query_ref[...].reshape(rows * heads, dim)
    weight = weight_ref[...] * INDEX_SCALE
    span = 256
    for c in range(keys_ref.shape[0] // span):
        dots = lax.dot_general(
            flat, keys_ref[c * span : (c + 1) * span, :], (((1,), (1,)), ((), ())), preferred_element_type=F32
        ).reshape(rows, heads, span)
        out_ref[:, c * span : (c + 1) * span] = jnp.sum(
            jnp.maximum(dots, 0.0) * weight[:, :, None], axis=1
        )


def index_scores_of(index_query, index_weight, index_keys):
    rows, heads, dim = index_query.shape
    keys = index_keys.shape[0]
    step = 8
    return pl.pallas_call(
        index_kernel,
        grid=(rows // step,),
        out_shape=jax.ShapeDtypeStruct((rows, keys), F32),
        in_specs=[
            pl.BlockSpec((step, heads, dim), lambda i: (i, 0, 0)),
            pl.BlockSpec((step, heads), lambda i: (i, 0)),
            pl.BlockSpec((keys, dim), lambda i: (0, 0)),
        ],
        out_specs=pl.BlockSpec((step, keys), lambda i: (i, 0)),
        cost_estimate=pl.CostEstimate(
            flops=8 * rows * heads * dim * keys, bytes_accessed=rows * heads * dim * 2 + rows * keys * 4, transcendentals=0
        ),
        compiler_params=pltpu.CompilerParams(vmem_limit_bytes=16 << 20),
        name="index_scores",
    )(index_query, index_weight, index_keys)


def masked_scores(q, keys, tiles, limit):
    scores = jnp.dot(q, keys, preferred_element_type=F32)
    rows = q.shape[0]
    lane = iota((rows, 128), 1)
    offset = (lane >> 3) * BLOCK + (lane & 7)
    pieces = []
    for t, first_key in enumerate(tiles):
        piece = scores[:, t * 128 : (t + 1) * 128]
        if first_key is not None:
            piece = jnp.where(offset <= limit - first_key, piece, -jnp.inf)
        pieces.append(piece)
    return jnp.concatenate(pieces, axis=1)


def own_kernel(past_ref, packed_ref, up_ref, down_ref, top_ref, total_ref, mixed_ref, q_ref, keys_ref):
    _, first, second = place()
    past = past_ref[0:1, :]
    late = 16 * BLOCK
    tiles = (None, late + first * 8, None, late + 32 + second * 8)
    for g in range(packed_ref.shape[0]):
        low = g * 64
        for t in range(4):
            q_ref[low : low + 64, t * 128 : (t + 1) * 128] = packed_ref[g, t * 64 : (t + 1) * 64, :]
        q_ref[low : low + 32, 512:] = packed_ref[g, 256:, :64]
        q_ref[low + 32 : low + 64, 512:] = packed_ref[g, 256:, 64:]
    keys_ref[:, :384] = up_ref[...]
    keys_ref[:, 384:] = down_ref[:, 256:]
    rows, step = q_ref.shape[0], 256
    for a in range(0, rows, step):
        limit = past + a // 8 + (iota((step, 128), 0) >> 3)
        scores = masked_scores(q_ref[a : a + step, :], keys_ref[...], tiles, limit)
        top = jnp.max(scores, axis=1, keepdims=True)
        weights = jnp.exp((scores - top) * SCALE)
        lane = iota((step, 128), 1)
        top_ref[a : a + step, :] = jnp.where(lane < 64, top, past.astype(F32))
        total_ref[a : a + step, :] = jnp.broadcast_to(jnp.sum(weights, axis=1, keepdims=True), (step, 128))
        mixed_ref[a : a + step, :] = lax.dot_general(
            weights.astype(BF16), keys_ref[0:512, :], (((1,), (1,)), ((), ())), preferred_element_type=F32
        )


def attend_own(past, packed, up, down):
    width = up.shape[0]
    rows = packed.size // width
    count = 512
    return pl.pallas_call(
        own_kernel,
        out_shape=[
            jax.ShapeDtypeStruct((rows, 128), F32),
            jax.ShapeDtypeStruct((rows, 128), F32),
            jax.ShapeDtypeStruct((rows, 512), F32),
            jax.ShapeDtypeStruct((rows, width), BF16),
        ],
        in_specs=[VMEM] * 4,
        out_specs=[VMEM] * 4,
        scratch_shapes=[pltpu.VMEM((width, count), BF16)],
        cost_estimate=pl.CostEstimate(
            flops=2 * rows * count * (width + 512), bytes_accessed=rows * 4352, transcendentals=rows * count
        ),
        compiler_params=pltpu.CompilerParams(vmem_limit_bytes=16 << 20),
        name="attend_own",
    )(in_hbm(past), packed, up, down)


def rest_kernel(top_ref, total_ref, mixed_ref, q_ref, up_ref, down_ref, right_ref, left_ref, out_ref, keys_ref, done_ref, sems):
    _, first, second = place()
    past = top_ref[0:1, 64:65].astype(jnp.int32)
    late = 16 * BLOCK

    def of_first(step):
        return late + ((first + step) & 3) * 8

    def of_second(step):
        return late + 32 + ((second + step) & 3) * 8

    tiles = (
        (None, of_first(-1), None)
        + (None, of_first(1), of_second(2))
        + (None, of_second(-1), None)
        + (None, of_second(1), of_first(2))
    )
    for i, ref in enumerate((up_ref, down_ref, right_ref, left_ref)):
        keys_ref[:, i * 384 : (i + 1) * 384] = ref[...]
    rows, step = q_ref.shape[0], 256
    copies = []
    for a in range(0, rows, step):
        limit = past + a // 8 + (iota((step, 128), 0) >> 3)
        scores = masked_scores(q_ref[a : a + step, :], keys_ref[...], tiles, limit)
        before = top_ref[a : a + step, 0:1]
        top = jnp.maximum(jnp.max(scores, axis=1, keepdims=True), before)
        weights = jnp.exp((scores - top) * SCALE)
        fade = jnp.exp((before - top) * SCALE)
        total = total_ref[a : a + step, 0:1] * fade + jnp.sum(weights, axis=1, keepdims=True)
        mixed = mixed_ref[a : a + step, :] * fade + lax.dot_general(
            weights.astype(BF16), keys_ref[0:512, :], (((1,), (1,)), ((), ())), preferred_element_type=F32
        )
        done_ref[a : a + step, :] = (mixed / total).astype(BF16)
        copies.append(
            pltpu.make_async_copy(
                done_ref.at[pl.ds(a, step), :], out_ref.at[pl.ds(a, step), :], sems.at[a // step]
            )
        )
        copies[-1].start()
    for copy in copies:
        copy.wait()


def attend_rest(state, parts):
    rows, width = state[-1].shape
    count = sum(part.shape[1] for part in parts)
    return pl.pallas_call(
        rest_kernel,
        out_shape=jax.ShapeDtypeStruct((rows, 512), BF16),
        in_specs=[VMEM] * (4 + len(parts)),
        out_specs=pl.BlockSpec(memory_space=pltpu.HBM),
        scratch_shapes=[
            pltpu.VMEM((width, count), BF16),
            pltpu.VMEM((rows, 512), BF16),
            pltpu.SemaphoreType.DMA((rows // 256,)),
        ],
        cost_estimate=pl.CostEstimate(
            flops=2 * rows * count * (width + 512), bytes_accessed=rows * 5376, transcendentals=rows * count
        ),
        compiler_params=pltpu.CompilerParams(vmem_limit_bytes=24 << 20),
        name="attend_rest",
    )(*state, *parts)


def turn(d):
    return [(i, (i + d) % SHARDS) for i in range(SHARDS)]


def line(dy, dz):
    return [(y * 4 + z, ((y + dy) % 4) * 4 + (z + dz) % 4) for y in range(4) for z in range(4)]


def body(q_latent, index_query, index_weight, index_keys, latent_cache, block_ids, block_counts):
    rows, heads, _ = q_latent.shape
    groups = lax.axis_size("head")
    *outgoing, source, other, past = gather_parts(block_ids, block_counts, latent_cache.T)
    incoming = [outgoing[0]] + [lax.ppermute(outgoing[d], "ctx", turn(2 * d)) for d in range(1, SHARDS // 2)]
    by_group = q_by_group(q_latent, groups)
    head_query = lax.all_to_all(by_group, "head", split_axis=0, concat_axis=0, tiled=True)
    index_scores = index_scores_of(index_query, index_weight, index_keys)
    theirs = compact_parts(128, other, incoming)
    theirs = lax.ppermute(theirs, "ctx", [(i, i ^ 1) for i in range(SHARDS)])
    mine = compact_parts(0, source, incoming)
    up, down, right, left = spread_parts(mine, theirs)
    parts = [
        lax.ppermute(part, "head", line(*step))
        for part, step in ((up, (1, 0)), (down, (-1, 0)), (right, (0, 1)), (left, (0, -1)))
    ]
    state = attend_own(past, head_query, up, down)
    attention = attend_rest(state, parts)
    return attention.reshape(rows * groups, heads // groups, 512), index_scores


def solution(mesh):
    return jax.shard_map(
        body,
        mesh=mesh,
        in_specs=(
            P(("ctx", "head"), None, None),
            P("head", None, None),
            P("head", None),
            P("ctx", None),
            P("ctx", None),
            P(),
            P(),
        ),
        out_specs=(P("ctx", "head", None), P("head", "ctx")),
        check_vma=False,
    )
```

```python
import functools

import jax
import jax.numpy as jnp
from jax import lax
from jax.experimental import pallas as pl
from jax.experimental.pallas import tpu as pltpu
from jax.sharding import PartitionSpec as P


BLOCK = 64
SHARDS = 8
PART = 16
SCALE = 192.0 ** (-0.5)
INDEX_SCALE = 128.0 ** (-0.5)
F32 = jnp.float32
BF16 = jnp.bfloat16
VMEM = pl.BlockSpec(memory_space=pltpu.VMEM)
SMEM = pl.BlockSpec(memory_space=pltpu.SMEM)


def iota(shape, dim):
    return lax.broadcasted_iota(jnp.int32, shape, dim)


def in_hbm(x):
    return pltpu.with_memory_space_constraint(x, pltpu.HBM)


def valid_ids(ids_ref, counts_ref):
    tiles, entries = ids_ref.shape
    tile = iota((tiles, entries), 0)
    count = jnp.zeros((tiles, entries), jnp.int32)
    for t in range(tiles):
        count = jnp.where(tile == t, counts_ref[t], count)
    return jnp.where(iota((tiles, entries), 1) < count, ids_ref[...], -1)


def place():
    group = lax.axis_index("head")
    row_y, row_z = group >> 2, group & 3
    return lax.axis_index("ctx"), (row_y + 2 * row_z) & 3, (2 * row_y + row_z) & 3


def row_of(part, first, second):
    return jnp.where(part < 8, first * 8 + part, 24 + second * 8 + part)


def hot(index, target):
    return (index == target).astype(F32).astype(BF16)


def slot_sources(ids, tile):
    mine = jnp.sum(jnp.where(iota(ids.shape, 0) == tile, ids, 0), axis=0, keepdims=True)
    owner = jnp.where(mine < 0, 2 * SHARDS, mine >> 5)
    shard = iota(ids.shape, 0)
    here = jnp.sum((owner == shard).astype(F32), axis=1, keepdims=True).astype(jnp.int32)
    end = jnp.sum((owner <= shard).astype(F32), axis=1, keepdims=True).astype(jnp.int32)
    column = iota((SHARDS, 512), 1)
    entry = (column & 255) >> 3
    skipped = jnp.sum(jnp.where(entry >= end, 128 - 16 * here, 0), axis=0, keepdims=True)
    part = (column & 7) + ((column >> 8) << 3)
    return entry * PART + part + skipped, end[SHARDS - 1 :, :]


def gather_kernel(ids_hbm, counts_hbm, cache_ref, *refs):
    out_refs, (source_ref, other_ref, past_ref, ids_ref, counts_ref, held, sems) = refs[:-7], refs[-7:]
    keys = cache_ref.shape[1]
    lists = [
        pltpu.make_async_copy(ids_hbm, ids_ref, sems.at[keys // 512]),
        pltpu.make_async_copy(counts_hbm, counts_ref, sems.at[keys // 512 + 1]),
    ]
    for copy in lists:
        copy.start()
    copies = []
    for i, c in enumerate(range(0, keys, 512)):
        copies.append(pltpu.make_async_copy(cache_ref.at[:, pl.ds(c, 512)], held.at[i], sems.at[i]))
        copies[i].start()
    shard, first, second = place()
    tiles, entries = ids_ref.shape
    blocks = keys // BLOCK
    column = iota((512, 128), 1)
    keep = hot(iota((512, 128), 0), (column >> 4) * BLOCK + row_of(column & 15, first, second))

    def kept(i):
        return jnp.dot(held[i], keep, preferred_element_type=F32).astype(BF16)

    early = len(copies) // 2
    for copy in lists + copies[:early]:
        copy.wait()
    own = [kept(i) for i in range(early)]
    ids = valid_ids(ids_ref, counts_ref)
    lane = iota((tiles, 128), 1)
    block_of_lane = jnp.where(lane < blocks, lane + shard * blocks, -2)
    member = jnp.zeros((tiles, 128), F32)
    for j in range(entries):
        member = jnp.where(ids[:, j : j + 1] == block_of_lane, 1.0, member)
    before = (iota((128, 128), 0) < iota((128, 128), 1)).astype(BF16)
    rank = jnp.dot(member.astype(BF16), before, preferred_element_type=F32)
    rank = jnp.where(member > 0.0, rank, -1.0)
    slot = (lane >> 4).astype(F32)
    target = jnp.full((tiles, 128), -1, jnp.int32)
    for b in range(blocks):
        target = jnp.where(rank[:, b : b + 1] == slot, b * PART + (lane & 15), target)
    for copy in copies[early:]:
        copy.wait()
    own = jnp.concatenate(own + [kept(i) for i in range(early, len(copies))], axis=1)
    index = iota((own.shape[1], 128), 0)
    for d, out_ref in enumerate(out_refs):
        near = shard ^ (2 * d)
        pair = []
        for tile in (near, near ^ 1):
            chosen = iota((tiles, 128), 0) == tile
            pair.append(hot(index, jnp.sum(jnp.where(chosen, target, 0), axis=0, keepdims=True)))
        got = jnp.dot(own, jnp.concatenate(pair, axis=1), preferred_element_type=F32)
        out_ref[...] = got.astype(BF16)
    source, count = slot_sources(ids, shard)
    source_ref[...] = source
    past_ref[...] = jnp.broadcast_to((count - 2) * BLOCK, past_ref.shape)
    other_ref[...] = slot_sources(ids, shard ^ 1)[0]


def gather_parts(block_ids, block_counts, cache_t):
    width, keys = cache_t.shape
    hbm = pl.BlockSpec(memory_space=pltpu.HBM)
    chips = SHARDS // 2
    return pl.pallas_call(
        gather_kernel,
        out_shape=[pltpu.HBM((width, 256), BF16)]
        + [pltpu.VMEM((width, 256), BF16)] * (chips - 1)
        + [pltpu.HBM((SHARDS, n), jnp.int32) for n in (512, 512, 128)],
        in_specs=[hbm] * 3,
        out_specs=[VMEM] * (chips + 3),
        scratch_shapes=[
            pltpu.VMEM(block_ids.shape, jnp.int32),
            pltpu.SMEM(block_counts.shape, jnp.int32),
            pltpu.VMEM((keys // 512, width, 512), BF16),
            pltpu.SemaphoreType.DMA((keys // 512 + 2,)),
        ],
        cost_estimate=pl.CostEstimate(
            flops=2 * width * keys * 1024, bytes_accessed=2 * width * keys * 2, transcendentals=0
        ),
        compiler_params=pltpu.CompilerParams(vmem_limit_bytes=16 << 20),
        name="gather_parts",
    )(in_hbm(block_ids), in_hbm(block_counts), in_hbm(cache_t))


def compact_kernel(left, source_ref, *refs):
    part_refs, out_ref = refs[:-1], refs[-1]
    shard = lax.axis_index("ctx")
    row = iota((128, 512), 0)
    source = source_ref[0:1, :]
    total = jnp.zeros(out_ref.shape, F32)
    for d in range(0, len(part_refs), 2):
        pick = jnp.concatenate([hot(row + (shard ^ (2 * u)) * 128, source) for u in (d, d + 1)], axis=0)
        pair = jnp.concatenate([part_refs[u][:, left : left + 128] for u in (d, d + 1)], axis=1)
        total = total + jnp.dot(pair, pick, preferred_element_type=F32)
    out_ref[...] = total.astype(BF16)


def compact_parts(left, source, parts):
    width = parts[0].shape[0]
    return pl.pallas_call(
        functools.partial(compact_kernel, left),
        out_shape=pltpu.VMEM((width, 512), BF16),
        in_specs=[VMEM] * (1 + len(parts)),
        out_specs=VMEM,
        cost_estimate=pl.CostEstimate(flops=width * 1024 * 512, bytes_accessed=width * 1536 * 2, transcendentals=0),
        compiler_params=pltpu.CompilerParams(vmem_limit_bytes=8 << 20),
        name="compact_parts",
    )(in_hbm(source), in_hbm(parts[0]), *parts[1:])


def spread_kernel(own_ref, other_ref, y1_ref, y3_ref, z1_ref, z3_ref):
    group = lax.axis_index("head")
    odd_y, odd_z = (group >> 2) & 1, group & 1
    first = own_ref[:, :256] + other_ref[:, :256]
    second = own_ref[:, 256:] + other_ref[:, 256:]

    def pick(whole, late):
        return jnp.where(late == 1, whole[:, 128:], whole[:, :128])

    y1_ref[:, :256] = first
    y1_ref[:, 256:] = pick(second, odd_y)
    y3_ref[:, :256] = first
    y3_ref[:, 256:] = pick(second, 1 - odd_y)
    z1_ref[:, :256] = second
    z1_ref[:, 256:] = pick(first, odd_z)
    z3_ref[:, :256] = second
    z3_ref[:, 256:] = pick(first, 1 - odd_z)


def spread_parts(own, other):
    width = own.shape[0]
    return pl.pallas_call(
        spread_kernel,
        out_shape=[jax.ShapeDtypeStruct((width, 384), BF16)] * 4,
        in_specs=[VMEM] * 2,
        out_specs=[VMEM] * 4,
        cost_estimate=pl.CostEstimate(flops=width * 512, bytes_accessed=width * 2560 * 2, transcendentals=0),
        compiler_params=pltpu.CompilerParams(vmem_limit_bytes=8 << 20),
        name="spread_parts",
    )(own, other)


def q_prep_kernel(q_ref, out_ref):
    rows = q_ref.shape[0]
    for i in range(rows):
        query = q_ref[i].T
        for g in range(out_ref.shape[0]):
            part = query[g * 8 : (g + 1) * 8, :]
            for t in range(4):
                out_ref[g, t * 64 + i * 8 : t * 64 + (i + 1) * 8, :] = part[:, t * 128 : (t + 1) * 128]
            low = 256 + (i % 4) * 8
            left = (i // 4) * 64
            out_ref[g, low : low + 8, left : left + 64] = part[:, 512:]


def q_by_group(q_latent, groups):
    rows, heads, width = q_latent.shape
    return pl.pallas_call(
        q_prep_kernel,
        out_shape=jax.ShapeDtypeStruct((groups, rows * heads * width // (groups * 128), 128), BF16),
        in_specs=[VMEM],
        out_specs=VMEM,
        cost_estimate=pl.CostEstimate(flops=0, bytes_accessed=rows * heads * width * 4, transcendentals=0),
        compiler_params=pltpu.CompilerParams(vmem_limit_bytes=8 << 20),
        name="q_by_group",
    )(q_latent.transpose(0, 2, 1))


def index_kernel(query_ref, weight_ref, keys_ref, out_ref):
    rows, heads, dim = query_ref.shape
    flat = query_ref[...].reshape(rows * heads, dim)
    weight = weight_ref[...] * INDEX_SCALE
    span = 256
    for c in range(keys_ref.shape[0] // span):
        dots = lax.dot_general(
            flat, keys_ref[c * span : (c + 1) * span, :], (((1,), (1,)), ((), ())), preferred_element_type=F32
        ).reshape(rows, heads, span)
        out_ref[:, c * span : (c + 1) * span] = jnp.sum(
            jnp.maximum(dots, 0.0) * weight[:, :, None], axis=1
        )


def index_scores_of(index_query, index_weight, index_keys):
    rows, heads, dim = index_query.shape
    keys = index_keys.shape[0]
    step = 8
    return pl.pallas_call(
        index_kernel,
        grid=(rows // step,),
        out_shape=jax.ShapeDtypeStruct((rows, keys), F32),
        in_specs=[
            pl.BlockSpec((step, heads, dim), lambda i: (i, 0, 0)),
            pl.BlockSpec((step, heads), lambda i: (i, 0)),
            pl.BlockSpec((keys, dim), lambda i: (0, 0)),
        ],
        out_specs=pl.BlockSpec((step, keys), lambda i: (i, 0)),
        cost_estimate=pl.CostEstimate(
            flops=8 * rows * heads * dim * keys, bytes_accessed=rows * heads * dim * 2 + rows * keys * 4, transcendentals=0
        ),
        compiler_params=pltpu.CompilerParams(vmem_limit_bytes=16 << 20),
        name="index_scores",
    )(index_query, index_weight, index_keys)


def masked_scores(q, keys, tiles, limit):
    scores = jnp.dot(q, keys, preferred_element_type=F32)
    rows = q.shape[0]
    lane = iota((rows, 128), 1)
    offset = (lane >> 3) * BLOCK + (lane & 7)
    pieces = []
    for t, first_key in enumerate(tiles):
        piece = scores[:, t * 128 : (t + 1) * 128]
        if first_key is not None:
            piece = jnp.where(offset <= limit - first_key, piece, -jnp.inf)
        pieces.append(piece)
    return jnp.concatenate(pieces, axis=1)


def own_kernel(past_ref, packed_ref, y1_ref, y3_ref, top_ref, total_ref, mixed_ref, q_ref, keys_ref):
    _, first, second = place()
    past = past_ref[0:1, :]
    late = 16 * BLOCK
    odd_y = (lax.axis_index("head") >> 2) & 1
    low = 32 + second * 8
    tiles = (None, late + first * 8, odd_y * late + low, (1 - odd_y) * late + low)
    for g in range(packed_ref.shape[0]):
        low = g * 64
        for t in range(4):
            q_ref[low : low + 64, t * 128 : (t + 1) * 128] = packed_ref[g, t * 64 : (t + 1) * 64, :]
        q_ref[low : low + 32, 512:] = packed_ref[g, 256:, :64]
        q_ref[low + 32 : low + 64, 512:] = packed_ref[g, 256:, 64:]
    keys_ref[:, :384] = y1_ref[...]
    keys_ref[:, 384:] = y3_ref[:, 256:]
    rows, step = q_ref.shape[0], 256
    for a in range(0, rows, step):
        limit = past + a // 8 + (iota((step, 128), 0) >> 3)
        scores = masked_scores(q_ref[a : a + step, :], keys_ref[...], tiles, limit)
        top = jnp.max(scores, axis=1, keepdims=True)
        weights = jnp.exp((scores - top) * SCALE)
        lane = iota((step, 128), 1)
        top_ref[a : a + step, :] = jnp.where(lane < 64, top, past.astype(F32))
        total_ref[a : a + step, :] = jnp.broadcast_to(jnp.sum(weights, axis=1, keepdims=True), (step, 128))
        mixed_ref[a : a + step, :] = lax.dot_general(
            weights.astype(BF16), keys_ref[0:512, :], (((1,), (1,)), ((), ())), preferred_element_type=F32
        )


def attend_own(past, packed, y1, y3):
    width = y1.shape[0]
    rows = packed.size // width
    count = 512
    return pl.pallas_call(
        own_kernel,
        out_shape=[
            jax.ShapeDtypeStruct((rows, 128), F32),
            jax.ShapeDtypeStruct((rows, 128), F32),
            jax.ShapeDtypeStruct((rows, 512), F32),
            jax.ShapeDtypeStruct((rows, width), BF16),
        ],
        in_specs=[VMEM] * 4,
        out_specs=[VMEM] * 4,
        scratch_shapes=[pltpu.VMEM((width, count), BF16)],
        cost_estimate=pl.CostEstimate(
            flops=2 * rows * count * (width + 512), bytes_accessed=rows * 4352, transcendentals=rows * count
        ),
        compiler_params=pltpu.CompilerParams(vmem_limit_bytes=16 << 20),
        name="attend_own",
    )(in_hbm(past), packed, y1, y3)


def rest_kernel(top_ref, total_ref, mixed_ref, q_ref, y1_ref, y3_ref, z1_ref, z3_ref, out_ref, keys_ref, done_ref, sems):
    _, first, second = place()
    group = lax.axis_index("head")
    row_y, row_z = group >> 2, group & 3
    odd_y, odd_z = row_y & 1, row_z & 1
    past = top_ref[0:1, 64:65].astype(jnp.int32)
    late = 16 * BLOCK
    across_first, across_second = ((first + 2) & 3) * 8, 32 + ((second + 2) & 3) * 8
    tiles = ()
    for flip in (1, 3):
        sent_late = 1 - odd_y if flip == 1 else odd_y
        tiles += (None, late + (((row_y ^ flip) + 2 * row_z) & 3) * 8, sent_late * late + across_second)
    for flip in (1, 3):
        sent_late = 1 - odd_z if flip == 1 else odd_z
        tiles += (None, late + 32 + ((2 * row_y + (row_z ^ flip)) & 3) * 8, sent_late * late + across_first)
    for i, ref in enumerate((y1_ref, y3_ref, z1_ref, z3_ref)):
        keys_ref[:, i * 384 : (i + 1) * 384] = ref[...]
    rows, step = q_ref.shape[0], 256
    copies = []
    for a in range(0, rows, step):
        limit = past + a // 8 + (iota((step, 128), 0) >> 3)
        scores = masked_scores(q_ref[a : a + step, :], keys_ref[...], tiles, limit)
        before = top_ref[a : a + step, 0:1]
        top = jnp.maximum(jnp.max(scores, axis=1, keepdims=True), before)
        weights = jnp.exp((scores - top) * SCALE)
        fade = jnp.exp((before - top) * SCALE)
        total = total_ref[a : a + step, 0:1] * fade + jnp.sum(weights, axis=1, keepdims=True)
        mixed = mixed_ref[a : a + step, :] * fade + lax.dot_general(
            weights.astype(BF16), keys_ref[0:512, :], (((1,), (1,)), ((), ())), preferred_element_type=F32
        )
        done_ref[a : a + step, :] = (mixed / total).astype(BF16)
        copies.append(
            pltpu.make_async_copy(
                done_ref.at[pl.ds(a, step), :], out_ref.at[pl.ds(a, step), :], sems.at[a // step]
            )
        )
        copies[-1].start()
    for copy in copies:
        copy.wait()


def attend_rest(state, parts):
    rows, width = state[-1].shape
    count = sum(part.shape[1] for part in parts)
    return pl.pallas_call(
        rest_kernel,
        out_shape=jax.ShapeDtypeStruct((rows, 512), BF16),
        in_specs=[VMEM] * (4 + len(parts)),
        out_specs=pl.BlockSpec(memory_space=pltpu.HBM),
        scratch_shapes=[
            pltpu.VMEM((width, count), BF16),
            pltpu.VMEM((rows, 512), BF16),
            pltpu.SemaphoreType.DMA((rows // 256,)),
        ],
        cost_estimate=pl.CostEstimate(
            flops=2 * rows * count * (width + 512), bytes_accessed=rows * 5376, transcendentals=rows * count
        ),
        compiler_params=pltpu.CompilerParams(vmem_limit_bytes=24 << 20),
        name="attend_rest",
    )(*state, *parts)


def partners(count, flip):
    return [(i, i ^ flip) for i in range(count)]


def body(q_latent, index_query, index_weight, index_keys, latent_cache, block_ids, block_counts):
    rows, heads, _ = q_latent.shape
    groups = lax.axis_size("head")
    *outgoing, source, other, past = gather_parts(block_ids, block_counts, latent_cache.T)
    incoming = [outgoing[0]] + [lax.ppermute(outgoing[d], "ctx", partners(SHARDS, 2 * d)) for d in range(1, SHARDS // 2)]
    by_group = q_by_group(q_latent, groups)
    head_query = lax.all_to_all(by_group, "head", split_axis=0, concat_axis=0, tiled=True)
    index_scores = index_scores_of(index_query, index_weight, index_keys)
    theirs = compact_parts(128, other, incoming)
    theirs = lax.ppermute(theirs, "ctx", partners(SHARDS, 1))
    mine = compact_parts(0, source, incoming)
    y1, y3, z1, z3 = spread_parts(mine, theirs)
    parts = [lax.ppermute(part, "head", partners(groups, flip)) for part, flip in ((y1, 4), (y3, 12), (z1, 1), (z3, 3))]
    state = attend_own(past, head_query, y1, y3)
    attention = attend_rest(state, parts)
    return attention.reshape(rows * groups, heads // groups, 512), index_scores


def solution(mesh):
    return jax.shard_map(
        body,
        mesh=mesh,
        in_specs=(
            P(("ctx", "head"), None, None),
            P("head", None, None),
            P("head", None),
            P("ctx", None),
            P("ctx", None),
            P(),
            P(),
        ),
        out_specs=(P("ctx", "head", None), P("head", "ctx")),
        check_vma=False,
    )
```

```python
import functools

import jax
import jax.numpy as jnp
from jax import lax
from jax.experimental import pallas as pl
from jax.experimental.pallas import tpu as pltpu
from jax.sharding import PartitionSpec as P


BLOCK = 64
SHARDS = 8
PART = 16
SCALE = 192.0 ** (-0.5)
INDEX_SCALE = 128.0 ** (-0.5)
F32 = jnp.float32
BF16 = jnp.bfloat16
VMEM = pl.BlockSpec(memory_space=pltpu.VMEM)
SMEM = pl.BlockSpec(memory_space=pltpu.SMEM)


def iota(shape, dim):
    return lax.broadcasted_iota(jnp.int32, shape, dim)


def in_hbm(x):
    return pltpu.with_memory_space_constraint(x, pltpu.HBM)


def valid_ids(ids_ref, counts_ref):
    tiles, entries = ids_ref.shape
    tile = iota((tiles, entries), 0)
    count = jnp.zeros((tiles, entries), jnp.int32)
    for t in range(tiles):
        count = jnp.where(tile == t, counts_ref[t], count)
    return jnp.where(iota((tiles, entries), 1) < count, ids_ref[...], -1)


def place():
    group = lax.axis_index("head")
    row_y, row_z = group >> 2, group & 3
    return lax.axis_index("ctx"), (row_y + 2 * row_z) & 3, (2 * row_y + row_z) & 3


def row_of(part, first, second):
    return jnp.where(part < 8, first * 8 + part, 24 + second * 8 + part)


def hot(index, target):
    return (index == target).astype(F32).astype(BF16)


def slot_sources(ids, tile):
    mine = jnp.sum(jnp.where(iota(ids.shape, 0) == tile, ids, 0), axis=0, keepdims=True)
    owner = jnp.where(mine < 0, 2 * SHARDS, mine >> 5)
    shard = iota(ids.shape, 0)
    here = jnp.sum((owner == shard).astype(F32), axis=1, keepdims=True).astype(jnp.int32)
    end = jnp.sum((owner <= shard).astype(F32), axis=1, keepdims=True).astype(jnp.int32)
    column = iota((SHARDS, 512), 1)
    entry = (column & 255) >> 3
    skipped = jnp.sum(jnp.where(entry >= end, 128 - 16 * here, 0), axis=0, keepdims=True)
    part = (column & 7) + ((column >> 8) << 3)
    return entry * PART + part + skipped, end[SHARDS - 1 :, :]


def gather_kernel(ids_hbm, counts_hbm, cache_ref, *refs):
    out_refs, (source_ref, other_ref, past_ref, ids_ref, counts_ref, held, sems) = refs[:-7], refs[-7:]
    keys = cache_ref.shape[1]
    lists = [
        pltpu.make_async_copy(ids_hbm, ids_ref, sems.at[keys // 512]),
        pltpu.make_async_copy(counts_hbm, counts_ref, sems.at[keys // 512 + 1]),
    ]
    for copy in lists:
        copy.start()
    copies = []
    for i, c in enumerate(range(0, keys, 512)):
        copies.append(pltpu.make_async_copy(cache_ref.at[:, pl.ds(c, 512)], held.at[i], sems.at[i]))
        copies[i].start()
    shard, first, second = place()
    tiles, entries = ids_ref.shape
    blocks = keys // BLOCK
    column = iota((512, 128), 1)
    keep = hot(iota((512, 128), 0), (column >> 4) * BLOCK + row_of(column & 15, first, second))

    def kept(i):
        return jnp.dot(held[i], keep, preferred_element_type=F32).astype(BF16)

    early = len(copies) // 2
    for copy in lists + copies[:early]:
        copy.wait()
    own = [kept(i) for i in range(early)]
    ids = valid_ids(ids_ref, counts_ref)
    lane = iota((tiles, 128), 1)
    block_of_lane = jnp.where(lane < blocks, lane + shard * blocks, -2)
    member = jnp.zeros((tiles, 128), F32)
    for j in range(entries):
        member = jnp.where(ids[:, j : j + 1] == block_of_lane, 1.0, member)
    before = (iota((128, 128), 0) < iota((128, 128), 1)).astype(BF16)
    rank = jnp.dot(member.astype(BF16), before, preferred_element_type=F32)
    rank = jnp.where(member > 0.0, rank, -1.0)
    slot = (lane >> 4).astype(F32)
    target = jnp.full((tiles, 128), -1, jnp.int32)
    for b in range(blocks):
        target = jnp.where(rank[:, b : b + 1] == slot, b * PART + (lane & 15), target)
    for copy in copies[early:]:
        copy.wait()
    own = jnp.concatenate(own + [kept(i) for i in range(early, len(copies))], axis=1)
    index = iota((own.shape[1], 128), 0)
    for d, out_ref in enumerate(out_refs):
        near = (shard + 2 * d) & 7
        pair = []
        for tile in (near, near ^ 1):
            chosen = iota((tiles, 128), 0) == tile
            pair.append(hot(index, jnp.sum(jnp.where(chosen, target, 0), axis=0, keepdims=True)))
        got = jnp.dot(own, jnp.concatenate(pair, axis=1), preferred_element_type=F32)
        out_ref[...] = got.astype(BF16)
    source, count = slot_sources(ids, shard)
    source_ref[...] = source
    past_ref[...] = jnp.broadcast_to((count - 2) * BLOCK, past_ref.shape)
    other_ref[...] = slot_sources(ids, shard ^ 1)[0]


def gather_parts(block_ids, block_counts, cache_t):
    width, keys = cache_t.shape
    hbm = pl.BlockSpec(memory_space=pltpu.HBM)
    chips = SHARDS // 2
    return pl.pallas_call(
        gather_kernel,
        out_shape=[pltpu.HBM((width, 256), BF16)]
        + [pltpu.VMEM((width, 256), BF16)] * (chips - 1)
        + [pltpu.HBM((SHARDS, n), jnp.int32) for n in (512, 512, 128)],
        in_specs=[hbm] * 3,
        out_specs=[VMEM] * (chips + 3),
        scratch_shapes=[
            pltpu.VMEM(block_ids.shape, jnp.int32),
            pltpu.SMEM(block_counts.shape, jnp.int32),
            pltpu.VMEM((keys // 512, width, 512), BF16),
            pltpu.SemaphoreType.DMA((keys // 512 + 2,)),
        ],
        cost_estimate=pl.CostEstimate(
            flops=2 * width * keys * 1024, bytes_accessed=2 * width * keys * 2, transcendentals=0
        ),
        compiler_params=pltpu.CompilerParams(vmem_limit_bytes=16 << 20),
        name="gather_parts",
    )(in_hbm(block_ids), in_hbm(block_counts), in_hbm(cache_t))


def compact_kernel(left, source_ref, *refs):
    part_refs, out_ref = refs[:-1], refs[-1]
    shard = lax.axis_index("ctx")
    row = iota((128, 512), 0)
    source = source_ref[0:1, :]
    total = jnp.zeros(out_ref.shape, F32)
    for d in range(0, len(part_refs), 2):
        pick = jnp.concatenate([hot(row + ((shard - 2 * u) & 7) * 128, source) for u in (d, d + 1)], axis=0)
        pair = jnp.concatenate([part_refs[u][:, left : left + 128] for u in (d, d + 1)], axis=1)
        total = total + jnp.dot(pair, pick, preferred_element_type=F32)
    out_ref[...] = total.astype(BF16)


def compact_parts(left, source, parts):
    width = parts[0].shape[0]
    return pl.pallas_call(
        functools.partial(compact_kernel, left),
        out_shape=pltpu.VMEM((width, 512), BF16),
        in_specs=[VMEM] * (1 + len(parts)),
        out_specs=VMEM,
        cost_estimate=pl.CostEstimate(flops=width * 1024 * 512, bytes_accessed=width * 1536 * 2, transcendentals=0),
        compiler_params=pltpu.CompilerParams(vmem_limit_bytes=8 << 20),
        name="compact_parts",
    )(in_hbm(source), in_hbm(parts[0]), *parts[1:])


def spread_kernel(own_ref, other_ref, up_ref, down_ref, right_ref, left_ref):
    first = own_ref[:, :256] + other_ref[:, :256]
    second = own_ref[:, 256:] + other_ref[:, 256:]
    up_ref[:, :256] = first
    up_ref[:, 256:] = second[:, :128]
    down_ref[:, :256] = first
    down_ref[:, 256:] = second[:, 128:]
    right_ref[:, :256] = second
    right_ref[:, 256:] = first[:, :128]
    left_ref[:, :256] = second
    left_ref[:, 256:] = first[:, 128:]


def spread_parts(own, other):
    width = own.shape[0]
    return pl.pallas_call(
        spread_kernel,
        out_shape=[jax.ShapeDtypeStruct((width, 384), BF16)] * 4,
        in_specs=[VMEM] * 2,
        out_specs=[VMEM] * 4,
        cost_estimate=pl.CostEstimate(flops=width * 512, bytes_accessed=width * 2560 * 2, transcendentals=0),
        compiler_params=pltpu.CompilerParams(vmem_limit_bytes=8 << 20),
        name="spread_parts",
    )(own, other)


def q_prep_kernel(q_ref, out_ref):
    rows = q_ref.shape[0]
    for i in range(rows):
        query = q_ref[i].T
        for g in range(out_ref.shape[0]):
            part = query[g * 8 : (g + 1) * 8, :]
            for t in range(4):
                out_ref[g, t * 64 + i * 8 : t * 64 + (i + 1) * 8, :] = part[:, t * 128 : (t + 1) * 128]
            low = 256 + (i % 4) * 8
            left = (i // 4) * 64
            out_ref[g, low : low + 8, left : left + 64] = part[:, 512:]


def q_by_group(q_latent, groups):
    rows, heads, width = q_latent.shape
    return pl.pallas_call(
        q_prep_kernel,
        out_shape=jax.ShapeDtypeStruct((groups, rows * heads * width // (groups * 128), 128), BF16),
        in_specs=[VMEM],
        out_specs=VMEM,
        cost_estimate=pl.CostEstimate(flops=0, bytes_accessed=rows * heads * width * 4, transcendentals=0),
        compiler_params=pltpu.CompilerParams(vmem_limit_bytes=8 << 20),
        name="q_by_group",
    )(q_latent.transpose(0, 2, 1))


def index_kernel(query_ref, weight_ref, keys_ref, out_ref):
    rows, heads, dim = query_ref.shape
    flat = query_ref[...].reshape(rows * heads, dim)
    weight = weight_ref[...] * INDEX_SCALE
    span = 256
    for c in range(keys_ref.shape[0] // span):
        dots = lax.dot_general(
            flat, keys_ref[c * span : (c + 1) * span, :], (((1,), (1,)), ((), ())), preferred_element_type=F32
        ).reshape(rows, heads, span)
        out_ref[:, c * span : (c + 1) * span] = jnp.sum(
            jnp.maximum(dots, 0.0) * weight[:, :, None], axis=1
        )


def index_scores_of(index_query, index_weight, index_keys):
    rows, heads, dim = index_query.shape
    keys = index_keys.shape[0]
    step = 8
    return pl.pallas_call(
        index_kernel,
        grid=(rows // step,),
        out_shape=jax.ShapeDtypeStruct((rows, keys), F32),
        in_specs=[
            pl.BlockSpec((step, heads, dim), lambda i: (i, 0, 0)),
            pl.BlockSpec((step, heads), lambda i: (i, 0)),
            pl.BlockSpec((keys, dim), lambda i: (0, 0)),
        ],
        out_specs=pl.BlockSpec((step, keys), lambda i: (i, 0)),
        cost_estimate=pl.CostEstimate(
            flops=8 * rows * heads * dim * keys, bytes_accessed=rows * heads * dim * 2 + rows * keys * 4, transcendentals=0
        ),
        compiler_params=pltpu.CompilerParams(vmem_limit_bytes=16 << 20),
        name="index_scores",
    )(index_query, index_weight, index_keys)


def masked_scores(q, keys, tiles, limit):
    scores = jnp.dot(q, keys, preferred_element_type=F32)
    rows = q.shape[0]
    lane = iota((rows, 128), 1)
    offset = (lane >> 3) * BLOCK + (lane & 7)
    pieces = []
    for t, first_key in enumerate(tiles):
        piece = scores[:, t * 128 : (t + 1) * 128]
        if first_key is not None:
            piece = jnp.where(offset <= limit - first_key, piece, -jnp.inf)
        pieces.append(piece)
    return jnp.concatenate(pieces, axis=1)


def own_kernel(past_ref, packed_ref, up_ref, down_ref, top_ref, total_ref, mixed_ref, q_ref, keys_ref):
    _, first, second = place()
    past = past_ref[0:1, :]
    late = 16 * BLOCK
    tiles = (None, late + first * 8, None, late + 32 + second * 8)
    for g in range(packed_ref.shape[0]):
        low = g * 64
        for t in range(4):
            q_ref[low : low + 64, t * 128 : (t + 1) * 128] = packed_ref[g, t * 64 : (t + 1) * 64, :]
        q_ref[low : low + 32, 512:] = packed_ref[g, 256:, :64]
        q_ref[low + 32 : low + 64, 512:] = packed_ref[g, 256:, 64:]
    keys_ref[:, :384] = up_ref[...]
    keys_ref[:, 384:] = down_ref[:, 256:]
    rows, step = q_ref.shape[0], 256
    for a in range(0, rows, step):
        limit = past + a // 8 + (iota((step, 128), 0) >> 3)
        scores = masked_scores(q_ref[a : a + step, :], keys_ref[...], tiles, limit)
        top = jnp.max(scores, axis=1, keepdims=True)
        weights = jnp.exp((scores - top) * SCALE)
        lane = iota((step, 128), 1)
        top_ref[a : a + step, :] = jnp.where(lane < 64, top, past.astype(F32))
        total_ref[a : a + step, :] = jnp.broadcast_to(jnp.sum(weights, axis=1, keepdims=True), (step, 128))
        mixed_ref[a : a + step, :] = lax.dot_general(
            weights.astype(BF16), keys_ref[0:512, :], (((1,), (1,)), ((), ())), preferred_element_type=F32
        )


def attend_own(past, packed, up, down):
    width = up.shape[0]
    rows = packed.size // width
    count = 512
    return pl.pallas_call(
        own_kernel,
        out_shape=[
            jax.ShapeDtypeStruct((rows, 128), F32),
            jax.ShapeDtypeStruct((rows, 128), F32),
            jax.ShapeDtypeStruct((rows, 512), F32),
            jax.ShapeDtypeStruct((rows, width), BF16),
        ],
        in_specs=[VMEM] * 4,
        out_specs=[VMEM] * 4,
        scratch_shapes=[pltpu.VMEM((width, count), BF16)],
        cost_estimate=pl.CostEstimate(
            flops=2 * rows * count * (width + 512), bytes_accessed=rows * 4352, transcendentals=rows * count
        ),
        compiler_params=pltpu.CompilerParams(vmem_limit_bytes=16 << 20),
        name="attend_own",
    )(in_hbm(past), packed, up, down)


def more_kernel(along_y, top_ref, total_ref, mixed_ref, q_ref, plus_ref, minus_ref, *refs):
    out_refs, (keys_ref, done_ref, sems) = refs[:-3], refs[-3:]
    _, first, second = place()
    past = top_ref[0:1, 64:65].astype(jnp.int32)
    late = 16 * BLOCK

    def of_first(step):
        return late + ((first + step) & 3) * 8

    def of_second(step):
        return late + 32 + ((second + step) & 3) * 8

    near, far = (of_first, of_second) if along_y else (of_second, of_first)
    tiles = (None, near(-1), None, None, near(1), far(2))
    keys_ref[:, :384] = plus_ref[...]
    keys_ref[:, 384:] = minus_ref[...]
    rows, step = q_ref.shape[0], 256
    copies = []
    for a in range(0, rows, step):
        limit = past + a // 8 + (iota((step, 128), 0) >> 3)
        scores = masked_scores(q_ref[a : a + step, :], keys_ref[...], tiles, limit)
        before = top_ref[a : a + step, 0:1]
        top = jnp.maximum(jnp.max(scores, axis=1, keepdims=True), before)
        weights = jnp.exp((scores - top) * SCALE)
        fade = jnp.exp((before - top) * SCALE)
        total = total_ref[a : a + step, 0:1] * fade + jnp.sum(weights, axis=1, keepdims=True)
        mixed = mixed_ref[a : a + step, :] * fade + lax.dot_general(
            weights.astype(BF16), keys_ref[0:512, :], (((1,), (1,)), ((), ())), preferred_element_type=F32
        )
        if along_y:
            top_out, total_out, mixed_out = out_refs
            top_out[a : a + step, :] = jnp.where(iota((step, 128), 1) < 64, top, past.astype(F32))
            total_out[a : a + step, :] = jnp.broadcast_to(total, (step, 128))
            mixed_out[a : a + step, :] = mixed
            continue
        done_ref[a : a + step, :] = (mixed / total).astype(BF16)
        copies.append(
            pltpu.make_async_copy(
                done_ref.at[pl.ds(a, step), :], out_refs[0].at[pl.ds(a, step), :], sems.at[a // step]
            )
        )
        copies[-1].start()
    for copy in copies:
        copy.wait()


def attend_more(along_y, state, q, parts):
    rows, width = q.shape
    count = sum(part.shape[1] for part in parts)
    if along_y:
        out_shape, out_specs = [jax.ShapeDtypeStruct(x.shape, x.dtype) for x in state], [VMEM] * 3
    else:
        out_shape, out_specs = jax.ShapeDtypeStruct((rows, 512), BF16), pl.BlockSpec(memory_space=pltpu.HBM)
    return pl.pallas_call(
        functools.partial(more_kernel, along_y),
        out_shape=out_shape,
        in_specs=[VMEM] * (4 + len(parts)),
        out_specs=out_specs,
        scratch_shapes=[
            pltpu.VMEM((width, count), BF16),
            pltpu.VMEM((8, 512) if along_y else (rows, 512), BF16),
            pltpu.SemaphoreType.DMA((rows // 256,)),
        ],
        cost_estimate=pl.CostEstimate(
            flops=2 * rows * count * (width + 512), bytes_accessed=rows * 5376, transcendentals=rows * count
        ),
        compiler_params=pltpu.CompilerParams(vmem_limit_bytes=16 << 20),
        name="attend_more",
    )(*state, q, *parts)


def turn(d):
    return [(i, (i + d) % SHARDS) for i in range(SHARDS)]


def line(dy, dz):
    return [(y * 4 + z, ((y + dy) % 4) * 4 + (z + dz) % 4) for y in range(4) for z in range(4)]


def body(q_latent, index_query, index_weight, index_keys, latent_cache, block_ids, block_counts):
    rows, heads, _ = q_latent.shape
    groups = lax.axis_size("head")
    *outgoing, source, other, past = gather_parts(block_ids, block_counts, latent_cache.T)
    incoming = [outgoing[0]] + [lax.ppermute(outgoing[d], "ctx", turn(2 * d)) for d in (2, 1, 3)]
    incoming = [incoming[0], incoming[2], incoming[1], incoming[3]]
    by_group = q_by_group(q_latent, groups)
    head_query = lax.all_to_all(by_group, "head", split_axis=0, concat_axis=0, tiled=True)
    index_scores = index_scores_of(index_query, index_weight, index_keys)
    theirs = compact_parts(128, other, incoming)
    theirs = lax.ppermute(theirs, "ctx", [(i, i ^ 1) for i in range(SHARDS)])
    mine = compact_parts(0, source, incoming)
    up, down, right, left = spread_parts(mine, theirs)
    y_parts = [lax.ppermute(part, "head", line(*step)) for part, step in ((up, (1, 0)), (down, (-1, 0)))]
    z_parts = [lax.ppermute(part, "head", line(*step)) for part, step in ((right, (0, 1)), (left, (0, -1)))]
    *state, query = attend_own(past, head_query, up, down)
    state = attend_more(True, state, query, y_parts)
    attention = attend_more(False, state, query, z_parts)
    return attention.reshape(rows * groups, heads // groups, 512), index_scores


def solution(mesh):
    return jax.shard_map(
        body,
        mesh=mesh,
        in_specs=(
            P(("ctx", "head"), None, None),
            P("head", None, None),
            P("head", None),
            P("ctx", None),
            P("ctx", None),
            P(),
            P(),
        ),
        out_specs=(P("ctx", "head", None), P("head", "ctx")),
        check_vma=False,
    )
```

```python
import functools

import jax
import jax.numpy as jnp
from jax import lax
from jax.experimental import pallas as pl
from jax.experimental.pallas import tpu as pltpu
from jax.sharding import PartitionSpec as P


BLOCK = 64
SHARDS = 8
PART = 16
SCALE = 192.0 ** (-0.5)
SCALE_LOG2 = SCALE * 1.4426950408889634
INDEX_SCALE = 128.0 ** (-0.5)
F32 = jnp.float32
BF16 = jnp.bfloat16
VMEM = pl.BlockSpec(memory_space=pltpu.VMEM)
SMEM = pl.BlockSpec(memory_space=pltpu.SMEM)


def iota(shape, dim):
    return lax.broadcasted_iota(jnp.int32, shape, dim)


def in_hbm(x):
    return pltpu.with_memory_space_constraint(x, pltpu.HBM)


def valid_ids(ids_ref, counts_ref):
    tiles, entries = ids_ref.shape
    tile = iota((tiles, entries), 0)
    count = jnp.zeros((tiles, entries), jnp.int32)
    for t in range(tiles):
        count = jnp.where(tile == t, counts_ref[t], count)
    return jnp.where(iota((tiles, entries), 1) < count, ids_ref[...], -1)


def place():
    group = lax.axis_index("head")
    row_y, row_z = group >> 2, group & 3
    return lax.axis_index("ctx"), (row_y + 2 * row_z) & 3, (2 * row_y + row_z) & 3


def row_of(part, first, second):
    return jnp.where(part < 8, first * 8 + part, 24 + second * 8 + part)


def hot(index, target):
    return (index == target).astype(F32).astype(BF16)


def slot_sources(ids, tile):
    mine = jnp.sum(jnp.where(iota(ids.shape, 0) == tile, ids, 0), axis=0, keepdims=True)
    owner = jnp.where(mine < 0, 2 * SHARDS, mine >> 5)
    shard = iota(ids.shape, 0)
    here = jnp.sum((owner == shard).astype(F32), axis=1, keepdims=True).astype(jnp.int32)
    end = jnp.sum((owner <= shard).astype(F32), axis=1, keepdims=True).astype(jnp.int32)
    column = iota((SHARDS, 512), 1)
    entry = (column & 255) >> 3
    skipped = jnp.sum(jnp.where(entry >= end, 128 - 16 * here, 0), axis=0, keepdims=True)
    part = (column & 7) + ((column >> 8) << 3)
    return entry * PART + part + skipped, end[SHARDS - 1 :, :]


def gather_kernel(ids_hbm, counts_hbm, cache_ref, *refs):
    out_refs, (source_ref, other_ref, past_ref, ids_ref, counts_ref, held, sems) = refs[:-7], refs[-7:]
    keys = cache_ref.shape[1]
    lists = [
        pltpu.make_async_copy(ids_hbm, ids_ref, sems.at[keys // 512]),
        pltpu.make_async_copy(counts_hbm, counts_ref, sems.at[keys // 512 + 1]),
    ]
    for copy in lists:
        copy.start()
    copies = []
    for i, c in enumerate(range(0, keys, 512)):
        copies.append(pltpu.make_async_copy(cache_ref.at[:, pl.ds(c, 512)], held.at[i], sems.at[i]))
        copies[i].start()
    shard, first, second = place()
    tiles, entries = ids_ref.shape
    blocks = keys // BLOCK
    column = iota((512, 128), 1)
    keep = hot(iota((512, 128), 0), (column >> 4) * BLOCK + row_of(column & 15, first, second))

    def kept(i):
        return jnp.dot(held[i], keep, preferred_element_type=F32).astype(BF16)

    early = len(copies) // 2
    for copy in lists + copies[:early]:
        copy.wait()
    own = [kept(i) for i in range(early)]
    ids = valid_ids(ids_ref, counts_ref)
    lane = iota((tiles, 128), 1)
    block_of_lane = jnp.where(lane < blocks, lane + shard * blocks, -2)
    member = jnp.zeros((tiles, 128), F32)
    for j in range(entries):
        member = jnp.where(ids[:, j : j + 1] == block_of_lane, 1.0, member)
    before = (iota((128, 128), 0) < iota((128, 128), 1)).astype(BF16)
    rank = jnp.dot(member.astype(BF16), before, preferred_element_type=F32)
    rank = jnp.where(member > 0.0, rank, -1.0)
    slot = (lane >> 4).astype(F32)
    target = jnp.full((tiles, 128), -1, jnp.int32)
    for b in range(blocks):
        target = jnp.where(rank[:, b : b + 1] == slot, b * PART + (lane & 15), target)
    for copy in copies[early:]:
        copy.wait()
    own = jnp.concatenate(own + [kept(i) for i in range(early, len(copies))], axis=1)
    index = iota((own.shape[1], 128), 0)
    for d, out_ref in enumerate(out_refs):
        near = (shard + 2 * d) & 7
        pair = []
        for tile in (near, near ^ 1):
            chosen = iota((tiles, 128), 0) == tile
            pair.append(hot(index, jnp.sum(jnp.where(chosen, target, 0), axis=0, keepdims=True)))
        got = jnp.dot(own, jnp.concatenate(pair, axis=1), preferred_element_type=F32)
        out_ref[...] = got.astype(BF16)
    source, count = slot_sources(ids, shard)
    source_ref[...] = source
    past_ref[...] = jnp.broadcast_to((count - 2) * BLOCK, past_ref.shape)
    other_ref[...] = slot_sources(ids, shard ^ 1)[0]


def gather_parts(block_ids, block_counts, cache_t):
    width, keys = cache_t.shape
    hbm = pl.BlockSpec(memory_space=pltpu.HBM)
    chips = SHARDS // 2
    return pl.pallas_call(
        gather_kernel,
        out_shape=[pltpu.HBM((width, 256), BF16)]
        + [pltpu.VMEM((width, 256), BF16)] * (chips - 1)
        + [pltpu.HBM((SHARDS, n), jnp.int32) for n in (512, 512, 128)],
        in_specs=[hbm] * 3,
        out_specs=[VMEM] * (chips + 3),
        scratch_shapes=[
            pltpu.VMEM(block_ids.shape, jnp.int32),
            pltpu.SMEM(block_counts.shape, jnp.int32),
            pltpu.VMEM((keys // 512, width, 512), BF16),
            pltpu.SemaphoreType.DMA((keys // 512 + 2,)),
        ],
        cost_estimate=pl.CostEstimate(
            flops=2 * width * keys * 1024, bytes_accessed=2 * width * keys * 2, transcendentals=0
        ),
        compiler_params=pltpu.CompilerParams(vmem_limit_bytes=16 << 20),
        name="gather_parts",
    )(in_hbm(block_ids), in_hbm(block_counts), in_hbm(cache_t))


def compact_kernel(left, source_ref, *refs):
    part_refs, out_ref = refs[:-1], refs[-1]
    shard = lax.axis_index("ctx")
    row = iota((128, 512), 0)
    source = source_ref[0:1, :]
    total = jnp.zeros(out_ref.shape, F32)
    for d in range(0, len(part_refs), 2):
        pick = jnp.concatenate([hot(row + ((shard - 2 * u) & 7) * 128, source) for u in (d, d + 1)], axis=0)
        pair = jnp.concatenate([part_refs[u][:, left : left + 128] for u in (d, d + 1)], axis=1)
        total = total + jnp.dot(pair, pick, preferred_element_type=F32)
    out_ref[...] = total.astype(BF16)


def compact_parts(left, source, parts):
    width = parts[0].shape[0]
    return pl.pallas_call(
        functools.partial(compact_kernel, left),
        out_shape=pltpu.VMEM((width, 512), BF16),
        in_specs=[VMEM] * (1 + len(parts)),
        out_specs=VMEM,
        cost_estimate=pl.CostEstimate(flops=width * 1024 * 512, bytes_accessed=width * 1536 * 2, transcendentals=0),
        compiler_params=pltpu.CompilerParams(vmem_limit_bytes=8 << 20),
        name="compact_parts",
    )(in_hbm(source), in_hbm(parts[0]), *parts[1:])


def spread_kernel(own_ref, other_ref, up_ref, down_ref, right_ref, left_ref):
    first = own_ref[:, :256] + other_ref[:, :256]
    second = own_ref[:, 256:] + other_ref[:, 256:]
    up_ref[:, :256] = first
    up_ref[:, 256:] = second[:, :128]
    down_ref[:, :256] = first
    down_ref[:, 256:] = second[:, 128:]
    right_ref[:, :256] = second
    right_ref[:, 256:] = first[:, :128]
    left_ref[:, :256] = second
    left_ref[:, 256:] = first[:, 128:]


def spread_parts(own, other):
    width = own.shape[0]
    return pl.pallas_call(
        spread_kernel,
        out_shape=[jax.ShapeDtypeStruct((width, 384), BF16)] * 4,
        in_specs=[VMEM] * 2,
        out_specs=[VMEM] * 4,
        cost_estimate=pl.CostEstimate(flops=width * 512, bytes_accessed=width * 2560 * 2, transcendentals=0),
        compiler_params=pltpu.CompilerParams(vmem_limit_bytes=8 << 20),
        name="spread_parts",
    )(own, other)


def q_prep_kernel(q_ref, out_ref):
    rows = q_ref.shape[0]
    for i in range(rows):
        query = q_ref[i].T
        for g in range(out_ref.shape[0]):
            part = query[g * 8 : (g + 1) * 8, :]
            for t in range(4):
                out_ref[g, t * 64 + i * 8 : t * 64 + (i + 1) * 8, :] = part[:, t * 128 : (t + 1) * 128]
            low = 256 + (i % 4) * 8
            left = (i // 4) * 64
            out_ref[g, low : low + 8, left : left + 64] = part[:, 512:]


def q_by_group(q_latent, groups):
    rows, heads, width = q_latent.shape
    return pl.pallas_call(
        q_prep_kernel,
        out_shape=jax.ShapeDtypeStruct((groups, rows * heads * width // (groups * 128), 128), BF16),
        in_specs=[VMEM],
        out_specs=VMEM,
        cost_estimate=pl.CostEstimate(flops=0, bytes_accessed=rows * heads * width * 4, transcendentals=0),
        compiler_params=pltpu.CompilerParams(vmem_limit_bytes=8 << 20),
        name="q_by_group",
    )(q_latent.transpose(0, 2, 1))


def index_kernel(query_ref, weight_ref, keys_ref, out_ref):
    rows, heads, dim = query_ref.shape
    flat = query_ref[...].reshape(rows * heads, dim)
    weight = weight_ref[...] * INDEX_SCALE
    span = 256
    for c in range(keys_ref.shape[0] // span):
        dots = lax.dot_general(
            flat, keys_ref[c * span : (c + 1) * span, :], (((1,), (1,)), ((), ())), preferred_element_type=F32
        ).reshape(rows, heads, span)
        out_ref[:, c * span : (c + 1) * span] = jnp.sum(
            jnp.maximum(dots, 0.0) * weight[:, :, None], axis=1
        )


def index_scores_of(index_query, index_weight, index_keys):
    rows, heads, dim = index_query.shape
    keys = index_keys.shape[0]
    step = 8
    return pl.pallas_call(
        index_kernel,
        grid=(rows // step,),
        out_shape=jax.ShapeDtypeStruct((rows, keys), F32),
        in_specs=[
            pl.BlockSpec((step, heads, dim), lambda i: (i, 0, 0)),
            pl.BlockSpec((step, heads), lambda i: (i, 0)),
            pl.BlockSpec((keys, dim), lambda i: (0, 0)),
        ],
        out_specs=pl.BlockSpec((step, keys), lambda i: (i, 0)),
        cost_estimate=pl.CostEstimate(
            flops=8 * rows * heads * dim * keys, bytes_accessed=rows * heads * dim * 2 + rows * keys * 4, transcendentals=0
        ),
        compiler_params=pltpu.CompilerParams(vmem_limit_bytes=16 << 20),
        name="index_scores",
    )(index_query, index_weight, index_keys)


def masked_scores(q, keys, tiles, limit):
    scores = jnp.dot(q, keys, preferred_element_type=F32)
    rows = q.shape[0]
    lane = iota((rows, 128), 1)
    offset = (lane >> 3) * BLOCK + (lane & 7)
    pieces = []
    for t, first_key in enumerate(tiles):
        piece = scores[:, t * 128 : (t + 1) * 128]
        if first_key is not None:
            piece = jnp.where(offset <= limit - first_key, piece, -jnp.inf)
        pieces.append(piece)
    return jnp.concatenate(pieces, axis=1)


def own_kernel(past_ref, packed_ref, up_ref, down_ref, top_ref, total_ref, mixed_ref, q_ref, keys_ref):
    _, first, second = place()
    past = past_ref[0:1, :]
    late = 16 * BLOCK
    tiles = (None, late + first * 8, None, late + 32 + second * 8)
    for g in range(packed_ref.shape[0]):
        low = g * 64
        for t in range(4):
            q_ref[low : low + 64, t * 128 : (t + 1) * 128] = packed_ref[g, t * 64 : (t + 1) * 64, :]
        q_ref[low : low + 32, 512:] = packed_ref[g, 256:, :64]
        q_ref[low + 32 : low + 64, 512:] = packed_ref[g, 256:, 64:]
    keys_ref[:, :384] = up_ref[...]
    keys_ref[:, 384:] = down_ref[:, 256:]
    rows, step = q_ref.shape[0], 512
    lane = iota((step, 128), 1)

    def scores_at(a):
        limit = past + a // 8 + (iota((step, 128), 0) >> 3)
        return masked_scores(q_ref[a : a + step, :], keys_ref[...], tiles, limit)

    coming = scores_at(0)
    for a in range(0, rows, step):
        scores = coming
        if a + step < rows:
            coming = scores_at(a + step)
        top = jnp.max(scores, axis=1, keepdims=True)
        weights = jnp.exp2((scores - top) * SCALE_LOG2)
        top_ref[a : a + step, :] = jnp.where(lane < 64, top, past.astype(F32))
        total_ref[a : a + step, :] = jnp.broadcast_to(jnp.sum(weights, axis=1, keepdims=True), (step, 128))
        mixed_ref[a : a + step, :] = lax.dot_general(
            weights.astype(BF16), keys_ref[0:512, :], (((1,), (1,)), ((), ())), preferred_element_type=F32
        )


def attend_own(past, packed, up, down):
    width = up.shape[0]
    rows = packed.size // width
    count = 512
    return pl.pallas_call(
        own_kernel,
        out_shape=[
            jax.ShapeDtypeStruct((rows, 128), F32),
            jax.ShapeDtypeStruct((rows, 128), F32),
            jax.ShapeDtypeStruct((rows, 512), F32),
            jax.ShapeDtypeStruct((rows, width), BF16),
        ],
        in_specs=[VMEM] * 4,
        out_specs=[VMEM] * 4,
        scratch_shapes=[pltpu.VMEM((width, count), BF16)],
        cost_estimate=pl.CostEstimate(
            flops=2 * rows * count * (width + 512), bytes_accessed=rows * 4352, transcendentals=rows * count
        ),
        compiler_params=pltpu.CompilerParams(vmem_limit_bytes=16 << 20),
        name="attend_own",
    )(in_hbm(past), packed, up, down)


def rest_kernel(top_ref, total_ref, mixed_ref, q_ref, up_ref, down_ref, right_ref, left_ref, out_ref, keys_ref, done_ref, sems):
    _, first, second = place()
    past = top_ref[0:1, 64:65].astype(jnp.int32)
    late = 16 * BLOCK

    def of_first(step):
        return late + ((first + step) & 3) * 8

    def of_second(step):
        return late + 32 + ((second + step) & 3) * 8

    tiles = (
        (None, of_first(-1), None)
        + (None, of_first(1), of_second(2))
        + (None, of_second(-1), None)
        + (None, of_second(1), of_first(2))
    )
    for i, ref in enumerate((up_ref, down_ref, right_ref, left_ref)):
        keys_ref[:, i * 384 : (i + 1) * 384] = ref[...]
    rows, step = q_ref.shape[0], 512
    copies = []

    def scores_at(a):
        limit = past + a // 8 + (iota((step, 128), 0) >> 3)
        return masked_scores(q_ref[a : a + step, :], keys_ref[...], tiles, limit)

    coming = scores_at(0)
    for a in range(0, rows, step):
        scores = coming
        if a + step < rows:
            coming = scores_at(a + step)
        before = top_ref[a : a + step, 0:1]
        top = jnp.maximum(jnp.max(scores, axis=1, keepdims=True), before)
        weights = jnp.exp2((scores - top) * SCALE_LOG2)
        fade = jnp.exp2((before - top) * SCALE_LOG2)
        share = 1.0 / (total_ref[a : a + step, 0:1] * fade + jnp.sum(weights, axis=1, keepdims=True))
        added = lax.dot_general(
            weights.astype(BF16), keys_ref[0:512, :], (((1,), (1,)), ((), ())), preferred_element_type=F32
        )
        done_ref[a : a + step, :] = ((mixed_ref[a : a + step, :] * fade + added) * share).astype(BF16)
        copies.append(
            pltpu.make_async_copy(
                done_ref.at[pl.ds(a, step), :], out_ref.at[pl.ds(a, step), :], sems.at[a // step]
            )
        )
        copies[-1].start()
    for copy in copies:
        copy.wait()


def attend_rest(state, parts):
    rows, width = state[-1].shape
    count = sum(part.shape[1] for part in parts)
    return pl.pallas_call(
        rest_kernel,
        out_shape=jax.ShapeDtypeStruct((rows, 512), BF16),
        in_specs=[VMEM] * (4 + len(parts)),
        out_specs=pl.BlockSpec(memory_space=pltpu.HBM),
        scratch_shapes=[
            pltpu.VMEM((width, count), BF16),
            pltpu.VMEM((rows, 512), BF16),
            pltpu.SemaphoreType.DMA((rows // 512,)),
        ],
        cost_estimate=pl.CostEstimate(
            flops=2 * rows * count * (width + 512), bytes_accessed=rows * 5376, transcendentals=rows * count
        ),
        compiler_params=pltpu.CompilerParams(vmem_limit_bytes=24 << 20),
        name="attend_rest",
    )(*state, *parts)


def turn(d):
    return [(i, (i + d) % SHARDS) for i in range(SHARDS)]


def line(dy, dz):
    return [(y * 4 + z, ((y + dy) % 4) * 4 + (z + dz) % 4) for y in range(4) for z in range(4)]


def body(q_latent, index_query, index_weight, index_keys, latent_cache, block_ids, block_counts):
    rows, heads, _ = q_latent.shape
    groups = lax.axis_size("head")
    *outgoing, source, other, past = gather_parts(block_ids, block_counts, latent_cache.T)
    incoming = [outgoing[0]] + [lax.ppermute(outgoing[d], "ctx", turn(2 * d)) for d in (2, 1, 3)]
    incoming = [incoming[0], incoming[2], incoming[1], incoming[3]]
    by_group = q_by_group(q_latent, groups)
    head_query = lax.all_to_all(by_group, "head", split_axis=0, concat_axis=0, tiled=True)
    index_scores = index_scores_of(index_query, index_weight, index_keys)
    theirs = compact_parts(128, other, incoming)
    theirs = lax.ppermute(theirs, "ctx", [(i, i ^ 1) for i in range(SHARDS)])
    mine = compact_parts(0, source, incoming)
    up, down, right, left = spread_parts(mine, theirs)
    parts = [
        lax.ppermute(part, "head", line(*step))
        for part, step in ((up, (1, 0)), (down, (-1, 0)), (right, (0, 1)), (left, (0, -1)))
    ]
    state = attend_own(past, head_query, up, down)
    attention = attend_rest(state, parts)
    return attention.reshape(rows * groups, heads // groups, 512), index_scores


def solution(mesh):
    return jax.shard_map(
        body,
        mesh=mesh,
        in_specs=(
            P(("ctx", "head"), None, None),
            P("head", None, None),
            P("head", None),
            P("ctx", None),
            P("ctx", None),
            P(),
            P(),
        ),
        out_specs=(P("ctx", "head", None), P("head", "ctx")),
        check_vma=False,
    )
```

```python
import functools

import jax
import jax.numpy as jnp
from jax import lax
from jax.experimental import pallas as pl
from jax.experimental.pallas import tpu as pltpu
from jax.sharding import PartitionSpec as P


BLOCK = 64
SHARDS = 8
PART = 16
SCALE = 192.0 ** (-0.5)
SCALE_LOG2 = SCALE * 1.4426950408889634
INDEX_SCALE = 128.0 ** (-0.5)
F32 = jnp.float32
BF16 = jnp.bfloat16
VMEM = pl.BlockSpec(memory_space=pltpu.VMEM)
SMEM = pl.BlockSpec(memory_space=pltpu.SMEM)


def iota(shape, dim):
    return lax.broadcasted_iota(jnp.int32, shape, dim)


def in_hbm(x):
    return pltpu.with_memory_space_constraint(x, pltpu.HBM)


def valid_ids(ids_ref, counts_ref):
    tiles, entries = ids_ref.shape
    tile = iota((tiles, entries), 0)
    count = jnp.zeros((tiles, entries), jnp.int32)
    for t in range(tiles):
        count = jnp.where(tile == t, counts_ref[t], count)
    return jnp.where(iota((tiles, entries), 1) < count, ids_ref[...], -1)


def place():
    group = lax.axis_index("head")
    row_y, row_z = group >> 2, group & 3
    return lax.axis_index("ctx"), (row_y + 2 * row_z) & 3, (2 * row_y + row_z) & 3


def row_of(part, first, second):
    return jnp.where(part < 8, first * 8 + part, 24 + second * 8 + part)


def hot(index, target):
    return (index == target).astype(F32).astype(BF16)


def slot_sources(ids, tile):
    mine = jnp.sum(jnp.where(iota(ids.shape, 0) == tile, ids, 0), axis=0, keepdims=True)
    owner = jnp.where(mine < 0, 2 * SHARDS, mine >> 5)
    shard = iota(ids.shape, 0)
    here = jnp.sum((owner == shard).astype(F32), axis=1, keepdims=True).astype(jnp.int32)
    end = jnp.sum((owner <= shard).astype(F32), axis=1, keepdims=True).astype(jnp.int32)
    column = iota((SHARDS, 512), 1)
    entry = (column & 255) >> 3
    skipped = jnp.sum(jnp.where(entry >= end, 128 - 16 * here, 0), axis=0, keepdims=True)
    part = (column & 7) + ((column >> 8) << 3)
    return entry * PART + part + skipped, end[SHARDS - 1 :, :]


def gather_kernel(ids_hbm, counts_hbm, cache_ref, *refs):
    out_refs, (source_ref, other_ref, past_ref, ids_ref, counts_ref, held, sems) = refs[:-7], refs[-7:]
    keys = cache_ref.shape[1]
    lists = [
        pltpu.make_async_copy(ids_hbm, ids_ref, sems.at[keys // 512]),
        pltpu.make_async_copy(counts_hbm, counts_ref, sems.at[keys // 512 + 1]),
    ]
    for copy in lists:
        copy.start()
    copies = []
    for i, c in enumerate(range(0, keys, 512)):
        copies.append(pltpu.make_async_copy(cache_ref.at[:, pl.ds(c, 512)], held.at[i], sems.at[i]))
        copies[i].start()
    shard, first, second = place()
    tiles, entries = ids_ref.shape
    blocks = keys // BLOCK
    column = iota((512, 128), 1)
    keep = hot(iota((512, 128), 0), (column >> 4) * BLOCK + row_of(column & 15, first, second))

    def kept(i):
        return jnp.dot(held[i], keep, preferred_element_type=F32).astype(BF16)

    early = len(copies) // 2
    for copy in lists + copies[:early]:
        copy.wait()
    own = [kept(i) for i in range(early)]
    ids = valid_ids(ids_ref, counts_ref)
    lane = iota((tiles, 128), 1)
    block_of_lane = jnp.where(lane < blocks, lane + shard * blocks, -2)
    member = jnp.zeros((tiles, 128), F32)
    for j in range(entries):
        member = jnp.where(ids[:, j : j + 1] == block_of_lane, 1.0, member)
    before = (iota((128, 128), 0) < iota((128, 128), 1)).astype(BF16)
    rank = jnp.dot(member.astype(BF16), before, preferred_element_type=F32)
    rank = jnp.where(member > 0.0, rank, -1.0)
    slot = (lane >> 4).astype(F32)
    target = jnp.full((tiles, 128), -1, jnp.int32)
    for b in range(blocks):
        target = jnp.where(rank[:, b : b + 1] == slot, b * PART + (lane & 15), target)
    for copy in copies[early:]:
        copy.wait()
    own = jnp.concatenate(own + [kept(i) for i in range(early, len(copies))], axis=1)
    index = iota((own.shape[1], 128), 0)
    for d, out_ref in enumerate(out_refs):
        near = (shard + 2 * d) & 7
        pair = []
        for tile in (near, near ^ 1):
            chosen = iota((tiles, 128), 0) == tile
            pair.append(hot(index, jnp.sum(jnp.where(chosen, target, 0), axis=0, keepdims=True)))
        got = jnp.dot(own, jnp.concatenate(pair, axis=1), preferred_element_type=F32)
        out_ref[...] = got.astype(BF16)
    source, count = slot_sources(ids, shard)
    source_ref[...] = source
    past_ref[...] = jnp.broadcast_to((count - 2) * BLOCK, past_ref.shape)
    other_ref[...] = slot_sources(ids, shard ^ 1)[0]


def gather_parts(block_ids, block_counts, cache_t):
    width, keys = cache_t.shape
    hbm = pl.BlockSpec(memory_space=pltpu.HBM)
    chips = SHARDS // 2
    return pl.pallas_call(
        gather_kernel,
        out_shape=[pltpu.HBM((width, 256), BF16)]
        + [pltpu.VMEM((width, 256), BF16)] * (chips - 1)
        + [pltpu.HBM((SHARDS, n), jnp.int32) for n in (512, 512, 128)],
        in_specs=[hbm] * 3,
        out_specs=[VMEM] * (chips + 3),
        scratch_shapes=[
            pltpu.VMEM(block_ids.shape, jnp.int32),
            pltpu.SMEM(block_counts.shape, jnp.int32),
            pltpu.VMEM((keys // 512, width, 512), BF16),
            pltpu.SemaphoreType.DMA((keys // 512 + 2,)),
        ],
        cost_estimate=pl.CostEstimate(
            flops=2 * width * keys * 1024, bytes_accessed=2 * width * keys * 2, transcendentals=0
        ),
        compiler_params=pltpu.CompilerParams(vmem_limit_bytes=16 << 20),
        name="gather_parts",
    )(in_hbm(block_ids), in_hbm(block_counts), in_hbm(cache_t))


def compact_kernel(left, source_ref, *refs):
    part_refs, out_ref = refs[:-1], refs[-1]
    shard = lax.axis_index("ctx")
    row = iota((128, 512), 0)
    source = source_ref[0:1, :]
    total = jnp.zeros(out_ref.shape, F32)
    for d in range(0, len(part_refs), 2):
        pick = jnp.concatenate([hot(row + ((shard - 2 * u) & 7) * 128, source) for u in (d, d + 1)], axis=0)
        pair = jnp.concatenate([part_refs[u][:, left : left + 128] for u in (d, d + 1)], axis=1)
        total = total + jnp.dot(pair, pick, preferred_element_type=F32)
    out_ref[...] = total.astype(BF16)


def compact_parts(left, source, parts):
    width = parts[0].shape[0]
    return pl.pallas_call(
        functools.partial(compact_kernel, left),
        out_shape=pltpu.VMEM((width, 512), BF16),
        in_specs=[VMEM] * (1 + len(parts)),
        out_specs=VMEM,
        cost_estimate=pl.CostEstimate(flops=width * 1024 * 512, bytes_accessed=width * 1536 * 2, transcendentals=0),
        compiler_params=pltpu.CompilerParams(vmem_limit_bytes=8 << 20),
        name="compact_parts",
    )(in_hbm(source), in_hbm(parts[0]), *parts[1:])


def spread_kernel(own_ref, other_ref, up_ref, down_ref, right_ref, left_ref):
    first = own_ref[:, :256] + other_ref[:, :256]
    second = own_ref[:, 256:] + other_ref[:, 256:]
    up_ref[:, :256] = first
    up_ref[:, 256:] = second
    down_ref[...] = first
    right_ref[:, :256] = second
    right_ref[:, 256:] = first[:, :128]
    left_ref[:, :256] = second
    left_ref[:, 256:] = first[:, 128:]


def spread_parts(own, other):
    width = own.shape[0]
    return pl.pallas_call(
        spread_kernel,
        out_shape=[jax.ShapeDtypeStruct((width, n), BF16) for n in (512, 256, 384, 384)],
        in_specs=[VMEM] * 2,
        out_specs=[VMEM] * 4,
        cost_estimate=pl.CostEstimate(flops=width * 512, bytes_accessed=width * 2560 * 2, transcendentals=0),
        compiler_params=pltpu.CompilerParams(vmem_limit_bytes=8 << 20),
        name="spread_parts",
    )(own, other)


def q_prep_kernel(q_ref, out_ref):
    rows = q_ref.shape[0]
    for i in range(rows):
        query = q_ref[i].T
        for g in range(out_ref.shape[0]):
            part = query[g * 8 : (g + 1) * 8, :]
            for t in range(4):
                out_ref[g, t * 64 + i * 8 : t * 64 + (i + 1) * 8, :] = part[:, t * 128 : (t + 1) * 128]
            low = 256 + (i % 4) * 8
            left = (i // 4) * 64
            out_ref[g, low : low + 8, left : left + 64] = part[:, 512:]


def q_by_group(q_latent, groups):
    rows, heads, width = q_latent.shape
    return pl.pallas_call(
        q_prep_kernel,
        out_shape=jax.ShapeDtypeStruct((groups, rows * heads * width // (groups * 128), 128), BF16),
        in_specs=[VMEM],
        out_specs=VMEM,
        cost_estimate=pl.CostEstimate(flops=0, bytes_accessed=rows * heads * width * 4, transcendentals=0),
        compiler_params=pltpu.CompilerParams(vmem_limit_bytes=8 << 20),
        name="q_by_group",
    )(q_latent.transpose(0, 2, 1))


def index_kernel(query_ref, weight_ref, keys_ref, out_ref):
    rows, heads, dim = query_ref.shape
    flat = query_ref[...].reshape(rows * heads, dim)
    weight = weight_ref[...] * INDEX_SCALE
    span = 256
    for c in range(keys_ref.shape[0] // span):
        dots = lax.dot_general(
            flat, keys_ref[c * span : (c + 1) * span, :], (((1,), (1,)), ((), ())), preferred_element_type=F32
        ).reshape(rows, heads, span)
        out_ref[:, c * span : (c + 1) * span] = jnp.sum(
            jnp.maximum(dots, 0.0) * weight[:, :, None], axis=1
        )


def index_scores_of(index_query, index_weight, index_keys):
    rows, heads, dim = index_query.shape
    keys = index_keys.shape[0]
    step = 8
    return pl.pallas_call(
        index_kernel,
        grid=(rows // step,),
        out_shape=jax.ShapeDtypeStruct((rows, keys), F32),
        in_specs=[
            pl.BlockSpec((step, heads, dim), lambda i: (i, 0, 0)),
            pl.BlockSpec((step, heads), lambda i: (i, 0)),
            pl.BlockSpec((keys, dim), lambda i: (0, 0)),
        ],
        out_specs=pl.BlockSpec((step, keys), lambda i: (i, 0)),
        cost_estimate=pl.CostEstimate(
            flops=8 * rows * heads * dim * keys, bytes_accessed=rows * heads * dim * 2 + rows * keys * 4, transcendentals=0
        ),
        compiler_params=pltpu.CompilerParams(vmem_limit_bytes=16 << 20),
        name="index_scores",
    )(index_query, index_weight, index_keys)


def masked_scores(q, keys, tiles, limit):
    scores = jnp.dot(q, keys, preferred_element_type=F32)
    rows = q.shape[0]
    lane = iota((rows, 128), 1)
    offset = (lane >> 3) * BLOCK + (lane & 7)
    pieces = []
    for t, first_key in enumerate(tiles):
        piece = scores[:, t * 128 : (t + 1) * 128]
        if first_key is not None:
            piece = jnp.where(offset <= limit - first_key, piece, -jnp.inf)
        pieces.append(piece)
    return jnp.concatenate(pieces, axis=1)


def own_kernel(past_ref, packed_ref, keys_ref, top_ref, total_ref, mixed_ref, q_ref):
    _, first, second = place()
    past = past_ref[0:1, :]
    late = 16 * BLOCK
    tiles = (None, late + first * 8, None, late + 32 + second * 8)
    for g in range(packed_ref.shape[0]):
        low = g * 64
        for t in range(4):
            q_ref[low : low + 64, t * 128 : (t + 1) * 128] = packed_ref[g, t * 64 : (t + 1) * 64, :]
        q_ref[low : low + 32, 512:] = packed_ref[g, 256:, :64]
        q_ref[low + 32 : low + 64, 512:] = packed_ref[g, 256:, 64:]
    rows, step = q_ref.shape[0], 512
    lane = iota((step, 128), 1)

    def scores_at(a):
        limit = past + a // 8 + (iota((step, 128), 0) >> 3)
        return masked_scores(q_ref[a : a + step, :], keys_ref[...], tiles, limit)

    coming = scores_at(0)
    for a in range(0, rows, step):
        scores = coming
        if a + step < rows:
            coming = scores_at(a + step)
        top = jnp.max(scores, axis=1, keepdims=True)
        weights = jnp.exp2((scores - top) * SCALE_LOG2)
        top_ref[a : a + step, :] = jnp.where(lane < 64, top, past.astype(F32))
        total_ref[a : a + step, :] = jnp.broadcast_to(jnp.sum(weights, axis=1, keepdims=True), (step, 128))
        mixed_ref[a : a + step, :] = lax.dot_general(
            weights.astype(BF16), keys_ref[0:512, :], (((1,), (1,)), ((), ())), preferred_element_type=F32
        )


def attend_own(past, packed, keys):
    width = keys.shape[0]
    rows = packed.size // width
    count = 512
    return pl.pallas_call(
        own_kernel,
        out_shape=[
            jax.ShapeDtypeStruct((rows, 128), F32),
            jax.ShapeDtypeStruct((rows, 128), F32),
            jax.ShapeDtypeStruct((rows, 512), F32),
            jax.ShapeDtypeStruct((rows, width), BF16),
        ],
        in_specs=[VMEM] * 3,
        out_specs=[VMEM] * 4,
        cost_estimate=pl.CostEstimate(
            flops=2 * rows * count * (width + 512), bytes_accessed=rows * 4352, transcendentals=rows * count
        ),
        compiler_params=pltpu.CompilerParams(vmem_limit_bytes=16 << 20),
        name="attend_own",
    )(in_hbm(past), packed, keys)


def rest_kernel(top_ref, total_ref, mixed_ref, q_ref, up_ref, down_ref, right_ref, left_ref, out_ref, keys_ref, done_ref, sems):
    _, first, second = place()
    past = top_ref[0:1, 64:65].astype(jnp.int32)
    late = 16 * BLOCK

    def of_first(step):
        return late + ((first + step) & 3) * 8

    def of_second(step):
        return late + 32 + ((second + step) & 3) * 8

    tiles = (
        (None, of_first(-1), None, of_second(2))
        + (None, of_first(1))
        + (None, of_second(-1), None)
        + (None, of_second(1), of_first(2))
    )
    low = 0
    for ref in (up_ref, down_ref, right_ref, left_ref):
        keys_ref[:, low : low + ref.shape[1]] = ref[...]
        low += ref.shape[1]
    rows, step = q_ref.shape[0], 512
    copies = []

    def scores_at(a):
        limit = past + a // 8 + (iota((step, 128), 0) >> 3)
        return masked_scores(q_ref[a : a + step, :], keys_ref[...], tiles, limit)

    coming = scores_at(0)
    for a in range(0, rows, step):
        scores = coming
        if a + step < rows:
            coming = scores_at(a + step)
        before = top_ref[a : a + step, 0:1]
        top = jnp.maximum(jnp.max(scores, axis=1, keepdims=True), before)
        weights = jnp.exp2((scores - top) * SCALE_LOG2)
        fade = jnp.exp2((before - top) * SCALE_LOG2)
        share = 1.0 / (total_ref[a : a + step, 0:1] * fade + jnp.sum(weights, axis=1, keepdims=True))
        added = lax.dot_general(
            weights.astype(BF16), keys_ref[0:512, :], (((1,), (1,)), ((), ())), preferred_element_type=F32
        )
        done_ref[a : a + step, :] = ((mixed_ref[a : a + step, :] * fade + added) * share).astype(BF16)
        copies.append(
            pltpu.make_async_copy(
                done_ref.at[pl.ds(a, step), :], out_ref.at[pl.ds(a, step), :], sems.at[a // step]
            )
        )
        copies[-1].start()
    for copy in copies:
        copy.wait()


def attend_rest(state, parts):
    rows, width = state[-1].shape
    count = sum(part.shape[1] for part in parts)
    return pl.pallas_call(
        rest_kernel,
        out_shape=jax.ShapeDtypeStruct((rows, 512), BF16),
        in_specs=[VMEM] * (4 + len(parts)),
        out_specs=pl.BlockSpec(memory_space=pltpu.HBM),
        scratch_shapes=[
            pltpu.VMEM((width, count), BF16),
            pltpu.VMEM((rows, 512), BF16),
            pltpu.SemaphoreType.DMA((rows // 512,)),
        ],
        cost_estimate=pl.CostEstimate(
            flops=2 * rows * count * (width + 512), bytes_accessed=rows * 5376, transcendentals=rows * count
        ),
        compiler_params=pltpu.CompilerParams(vmem_limit_bytes=24 << 20),
        name="attend_rest",
    )(*state, *parts)


def turn(d):
    return [(i, (i + d) % SHARDS) for i in range(SHARDS)]


def line(dy, dz):
    return [(y * 4 + z, ((y + dy) % 4) * 4 + (z + dz) % 4) for y in range(4) for z in range(4)]


def body(q_latent, index_query, index_weight, index_keys, latent_cache, block_ids, block_counts):
    rows, heads, _ = q_latent.shape
    groups = lax.axis_size("head")
    *outgoing, source, other, past = gather_parts(block_ids, block_counts, latent_cache.T)
    incoming = [outgoing[0]] + [lax.ppermute(outgoing[d], "ctx", turn(2 * d)) for d in (2, 1, 3)]
    incoming = [incoming[0], incoming[2], incoming[1], incoming[3]]
    by_group = q_by_group(q_latent, groups)
    head_query = lax.all_to_all(by_group, "head", split_axis=0, concat_axis=0, tiled=True)
    index_scores = index_scores_of(index_query, index_weight, index_keys)
    theirs = compact_parts(128, other, incoming)
    theirs = lax.ppermute(theirs, "ctx", [(i, i ^ 1) for i in range(SHARDS)])
    mine = compact_parts(0, source, incoming)
    up, down, right, left = spread_parts(mine, theirs)
    from_up = lax.ppermute(up, "head", line(1, 0))
    from_right = lax.ppermute(right, "head", line(0, 1))
    from_left = lax.ppermute(left, "head", line(0, -1))
    from_down = lax.ppermute(down, "head", line(-1, 0))
    parts = (from_up, from_down, from_right, from_left)
    state = attend_own(past, head_query, up)
    attention = attend_rest(state, parts)
    return attention.reshape(rows * groups, heads // groups, 512), index_scores


def solution(mesh):
    return jax.shard_map(
        body,
        mesh=mesh,
        in_specs=(
            P(("ctx", "head"), None, None),
            P("head", None, None),
            P("head", None),
            P("ctx", None),
            P("ctx", None),
            P(),
            P(),
        ),
        out_specs=(P("ctx", "head", None), P("head", "ctx")),
        check_vma=False,
    )
```

```python
import functools

import jax
import jax.numpy as jnp
from jax import lax
from jax.experimental import pallas as pl
from jax.experimental.pallas import tpu as pltpu
from jax.sharding import PartitionSpec as P


BLOCK = 64
SHARDS = 8
PART = 16
SCALE = 192.0 ** (-0.5)
SCALE_LOG2 = SCALE * 1.4426950408889634
INDEX_SCALE = 128.0 ** (-0.5)
F32 = jnp.float32
BF16 = jnp.bfloat16
VMEM = pl.BlockSpec(memory_space=pltpu.VMEM)
SMEM = pl.BlockSpec(memory_space=pltpu.SMEM)


def iota(shape, dim):
    return lax.broadcasted_iota(jnp.int32, shape, dim)


def in_hbm(x):
    return pltpu.with_memory_space_constraint(x, pltpu.HBM)


def valid_ids(ids_ref, counts_ref):
    tiles, entries = ids_ref.shape
    tile = iota((tiles, entries), 0)
    count = jnp.zeros((tiles, entries), jnp.int32)
    for t in range(tiles):
        count = jnp.where(tile == t, counts_ref[t], count)
    return jnp.where(iota((tiles, entries), 1) < count, ids_ref[...], -1)


def place():
    group = lax.axis_index("head")
    row_y, row_z = group >> 2, group & 3
    return lax.axis_index("ctx"), (row_y + 2 * row_z) & 3, (2 * row_y + row_z) & 3


def row_of(part, first, second):
    return jnp.where(part < 8, first * 8 + part, 24 + second * 8 + part)


def hot(index, target):
    return (index == target).astype(F32).astype(BF16)


def slot_sources(ids, tile):
    mine = jnp.sum(jnp.where(iota(ids.shape, 0) == tile, ids, 0), axis=0, keepdims=True)
    owner = jnp.where(mine < 0, 2 * SHARDS, mine >> 5)
    shard = iota(ids.shape, 0)
    here = jnp.sum((owner == shard).astype(F32), axis=1, keepdims=True).astype(jnp.int32)
    end = jnp.sum((owner <= shard).astype(F32), axis=1, keepdims=True).astype(jnp.int32)
    column = iota((SHARDS, 512), 1)
    entry = (column & 255) >> 3
    skipped = jnp.sum(jnp.where(entry >= end, 128 - 16 * here, 0), axis=0, keepdims=True)
    part = (column & 7) + ((column >> 8) << 3)
    return entry * PART + part + skipped, end[SHARDS - 1 :, :]


def gather_kernel(ids_hbm, counts_hbm, cache_ref, *refs):
    out_refs, (source_ref, other_ref, past_ref, ids_ref, counts_ref, held, sems) = refs[:-7], refs[-7:]
    keys = cache_ref.shape[1]
    lists = [
        pltpu.make_async_copy(ids_hbm, ids_ref, sems.at[keys // 512]),
        pltpu.make_async_copy(counts_hbm, counts_ref, sems.at[keys // 512 + 1]),
    ]
    for copy in lists:
        copy.start()
    copies = []
    for i, c in enumerate(range(0, keys, 512)):
        copies.append(pltpu.make_async_copy(cache_ref.at[:, pl.ds(c, 512)], held.at[i], sems.at[i]))
        copies[i].start()
    shard, first, second = place()
    tiles, entries = ids_ref.shape
    blocks = keys // BLOCK
    column = iota((512, 128), 1)
    keep = hot(iota((512, 128), 0), (column >> 4) * BLOCK + row_of(column & 15, first, second))

    def kept(i):
        return jnp.dot(held[i], keep, preferred_element_type=F32).astype(BF16)

    early = len(copies) // 2
    for copy in lists + copies[:early]:
        copy.wait()
    own = [kept(i) for i in range(early)]
    ids = valid_ids(ids_ref, counts_ref)
    lane = iota((tiles, 128), 1)
    block_of_lane = jnp.where(lane < blocks, lane + shard * blocks, -2)
    member = jnp.zeros((tiles, 128), F32)
    for j in range(entries):
        member = jnp.where(ids[:, j : j + 1] == block_of_lane, 1.0, member)
    before = (iota((128, 128), 0) < iota((128, 128), 1)).astype(BF16)
    rank = jnp.dot(member.astype(BF16), before, preferred_element_type=F32)
    rank = jnp.where(member > 0.0, rank, -1.0)
    slot = (lane >> 4).astype(F32)
    target = jnp.full((tiles, 128), -1, jnp.int32)
    for b in range(blocks):
        target = jnp.where(rank[:, b : b + 1] == slot, b * PART + (lane & 15), target)
    for copy in copies[early:]:
        copy.wait()
    own = jnp.concatenate(own + [kept(i) for i in range(early, len(copies))], axis=1)
    index = iota((own.shape[1], 128), 0)
    for d, out_ref in enumerate(out_refs):
        near = (shard + 2 * d) & 7
        pair = []
        for tile in (near, near ^ 1):
            chosen = iota((tiles, 128), 0) == tile
            pair.append(hot(index, jnp.sum(jnp.where(chosen, target, 0), axis=0, keepdims=True)))
        got = jnp.dot(own, jnp.concatenate(pair, axis=1), preferred_element_type=F32)
        out_ref[...] = got.astype(BF16)
    source, count = slot_sources(ids, shard)
    source_ref[...] = source
    past_ref[...] = jnp.broadcast_to((count - 2) * BLOCK, past_ref.shape)
    other_ref[...] = slot_sources(ids, shard ^ 1)[0]


def gather_parts(block_ids, block_counts, cache_t):
    width, keys = cache_t.shape
    hbm = pl.BlockSpec(memory_space=pltpu.HBM)
    chips = SHARDS // 2
    return pl.pallas_call(
        gather_kernel,
        out_shape=[pltpu.HBM((width, 256), BF16)]
        + [pltpu.VMEM((width, 256), BF16)] * (chips - 1)
        + [pltpu.HBM((SHARDS, n), jnp.int32) for n in (512, 512, 128)],
        in_specs=[hbm] * 3,
        out_specs=[VMEM] * (chips + 3),
        scratch_shapes=[
            pltpu.VMEM(block_ids.shape, jnp.int32),
            pltpu.SMEM(block_counts.shape, jnp.int32),
            pltpu.VMEM((keys // 512, width, 512), BF16),
            pltpu.SemaphoreType.DMA((keys // 512 + 2,)),
        ],
        cost_estimate=pl.CostEstimate(
            flops=2 * width * keys * 1024, bytes_accessed=2 * width * keys * 2, transcendentals=0
        ),
        compiler_params=pltpu.CompilerParams(vmem_limit_bytes=16 << 20),
        name="gather_parts",
    )(in_hbm(block_ids), in_hbm(block_counts), in_hbm(cache_t))


def compact_kernel(left, source_ref, *refs):
    part_refs, out_ref = refs[:-1], refs[-1]
    shard = lax.axis_index("ctx")
    row = iota((128, 512), 0)
    source = source_ref[0:1, :]
    total = jnp.zeros(out_ref.shape, F32)
    for d in range(0, len(part_refs), 2):
        pick = jnp.concatenate([hot(row + ((shard - 2 * u) & 7) * 128, source) for u in (d, d + 1)], axis=0)
        pair = jnp.concatenate([part_refs[u][:, left : left + 128] for u in (d, d + 1)], axis=1)
        total = total + jnp.dot(pair, pick, preferred_element_type=F32)
    out_ref[...] = total.astype(BF16)


def compact_parts(left, source, parts):
    width = parts[0].shape[0]
    return pl.pallas_call(
        functools.partial(compact_kernel, left),
        out_shape=pltpu.VMEM((width, 512), BF16),
        in_specs=[VMEM] * (1 + len(parts)),
        out_specs=VMEM,
        cost_estimate=pl.CostEstimate(flops=width * 1024 * 512, bytes_accessed=width * 1536 * 2, transcendentals=0),
        compiler_params=pltpu.CompilerParams(vmem_limit_bytes=8 << 20),
        name="compact_parts",
    )(in_hbm(source), in_hbm(parts[0]), *parts[1:])


def spread_kernel(own_ref, other_ref, up_ref, down_ref, right_ref, left_ref):
    first = own_ref[:, :256] + other_ref[:, :256]
    second = own_ref[:, 256:] + other_ref[:, 256:]
    up_ref[:, :256] = first
    up_ref[:, 256:] = second[:, :128]
    down_ref[:, :256] = first
    down_ref[:, 256:] = second[:, 128:]
    right_ref[:, :256] = second
    right_ref[:, 256:] = first[:, :128]
    left_ref[:, :256] = second
    left_ref[:, 256:] = first[:, 128:]


def spread_parts(own, other):
    width = own.shape[0]
    return pl.pallas_call(
        spread_kernel,
        out_shape=[jax.ShapeDtypeStruct((width, 384), BF16)] * 4,
        in_specs=[VMEM] * 2,
        out_specs=[VMEM] * 4,
        cost_estimate=pl.CostEstimate(flops=width * 512, bytes_accessed=width * 2560 * 2, transcendentals=0),
        compiler_params=pltpu.CompilerParams(vmem_limit_bytes=8 << 20),
        name="spread_parts",
    )(own, other)


def q_prep_kernel(q_ref, out_ref):
    rows = q_ref.shape[0]
    for i in range(rows):
        query = q_ref[i].T
        for g in range(out_ref.shape[0]):
            part = query[g * 8 : (g + 1) * 8, :]
            for t in range(4):
                out_ref[g, t * 64 + i * 8 : t * 64 + (i + 1) * 8, :] = part[:, t * 128 : (t + 1) * 128]
            low = 256 + (i % 4) * 8
            left = (i // 4) * 64
            out_ref[g, low : low + 8, left : left + 64] = part[:, 512:]


def q_by_group(q_latent, groups):
    rows, heads, width = q_latent.shape
    return pl.pallas_call(
        q_prep_kernel,
        out_shape=jax.ShapeDtypeStruct((groups, rows * heads * width // (groups * 128), 128), BF16),
        in_specs=[VMEM],
        out_specs=VMEM,
        cost_estimate=pl.CostEstimate(flops=0, bytes_accessed=rows * heads * width * 4, transcendentals=0),
        compiler_params=pltpu.CompilerParams(vmem_limit_bytes=8 << 20),
        name="q_by_group",
    )(q_latent.transpose(0, 2, 1))


def index_kernel(query_ref, weight_ref, keys_ref, out_ref):
    rows, heads, dim = query_ref.shape
    flat = query_ref[...].reshape(rows * heads, dim)
    weight = weight_ref[...] * INDEX_SCALE
    span = 256
    for c in range(keys_ref.shape[0] // span):
        dots = lax.dot_general(
            flat, keys_ref[c * span : (c + 1) * span, :], (((1,), (1,)), ((), ())), preferred_element_type=F32
        ).reshape(rows, heads, span)
        out_ref[:, c * span : (c + 1) * span] = jnp.sum(
            jnp.maximum(dots, 0.0) * weight[:, :, None], axis=1
        )


def index_scores_of(index_query, index_weight, index_keys):
    rows, heads, dim = index_query.shape
    keys = index_keys.shape[0]
    step = 8
    return pl.pallas_call(
        index_kernel,
        grid=(rows // step,),
        out_shape=jax.ShapeDtypeStruct((rows, keys), F32),
        in_specs=[
            pl.BlockSpec((step, heads, dim), lambda i: (i, 0, 0)),
            pl.BlockSpec((step, heads), lambda i: (i, 0)),
            pl.BlockSpec((keys, dim), lambda i: (0, 0)),
        ],
        out_specs=pl.BlockSpec((step, keys), lambda i: (i, 0)),
        cost_estimate=pl.CostEstimate(
            flops=8 * rows * heads * dim * keys, bytes_accessed=rows * heads * dim * 2 + rows * keys * 4, transcendentals=0
        ),
        compiler_params=pltpu.CompilerParams(vmem_limit_bytes=16 << 20),
        name="index_scores",
    )(index_query, index_weight, index_keys)


def masked_scores(q, keys, tiles, limit):
    scores = jnp.dot(q, keys, preferred_element_type=F32)
    rows = q.shape[0]
    lane = iota((rows, 128), 1)
    offset = (lane >> 3) * BLOCK + (lane & 7)
    pieces = []
    for t, first_key in enumerate(tiles):
        piece = scores[:, t * 128 : (t + 1) * 128]
        if first_key is not None:
            piece = jnp.where(offset <= limit - first_key, piece, -jnp.inf)
        pieces.append(piece)
    return jnp.concatenate(pieces, axis=1)


def own_kernel(past_ref, packed_ref, up_ref, down_ref, top_ref, total_ref, mixed_ref, q_ref, keys_ref):
    _, first, second = place()
    past = past_ref[0:1, :]
    late = 16 * BLOCK
    tiles = (None, late + first * 8, None, late + 32 + second * 8)
    for g in range(packed_ref.shape[0]):
        low = g * 64
        for t in range(4):
            q_ref[low : low + 64, t * 128 : (t + 1) * 128] = packed_ref[g, t * 64 : (t + 1) * 64, :]
        q_ref[low : low + 32, 512:] = packed_ref[g, 256:, :64]
        q_ref[low + 32 : low + 64, 512:] = packed_ref[g, 256:, 64:]
    keys_ref[:, :384] = up_ref[...]
    keys_ref[:, 384:] = down_ref[:, 256:]
    rows, step = q_ref.shape[0], 512
    lane = iota((step, 128), 1)

    def scores_at(a):
        limit = past + a // 8 + (iota((step, 128), 0) >> 3)
        return masked_scores(q_ref[a : a + step, :], keys_ref[...], tiles, limit)

    coming = scores_at(0)
    for a in range(0, rows, step):
        scores = coming
        if a + step < rows:
            coming = scores_at(a + step)
        top = jnp.max(scores, axis=1, keepdims=True)
        weights = jnp.exp2((scores - top) * SCALE_LOG2)
        top_ref[a : a + step, :] = jnp.where(lane < 64, top, past.astype(F32))
        total_ref[a : a + step, :] = jnp.broadcast_to(jnp.sum(weights, axis=1, keepdims=True), (step, 128))
        mixed_ref[a : a + step, :] = lax.dot_general(
            weights.astype(BF16), keys_ref[0:512, :], (((1,), (1,)), ((), ())), preferred_element_type=F32
        )


def attend_own(past, packed, up, down):
    width = up.shape[0]
    rows = packed.size // width
    count = 512
    return pl.pallas_call(
        own_kernel,
        out_shape=[
            jax.ShapeDtypeStruct((rows, 128), F32),
            jax.ShapeDtypeStruct((rows, 128), F32),
            jax.ShapeDtypeStruct((rows, 512), F32),
            jax.ShapeDtypeStruct((rows, width), BF16),
        ],
        in_specs=[VMEM] * 4,
        out_specs=[VMEM] * 4,
        scratch_shapes=[pltpu.VMEM((width, count), BF16)],
        cost_estimate=pl.CostEstimate(
            flops=2 * rows * count * (width + 512), bytes_accessed=rows * 4352, transcendentals=rows * count
        ),
        compiler_params=pltpu.CompilerParams(vmem_limit_bytes=16 << 20),
        name="attend_own",
    )(in_hbm(past), packed, up, down)


def rest_kernel(top_ref, total_ref, mixed_ref, q_ref, up_ref, down_ref, right_ref, left_ref, out_ref, keys_ref, done_ref, sems):
    _, first, second = place()
    past = top_ref[0:1, 64:65].astype(jnp.int32)
    late = 16 * BLOCK

    def of_first(step):
        return late + ((first + step) & 3) * 8

    def of_second(step):
        return late + 32 + ((second + step) & 3) * 8

    tiles = (
        (None, of_first(-1), None)
        + (None, of_first(1), of_second(2))
        + (None, of_second(-1), None)
        + (None, of_second(1), of_first(2))
    )
    rows, step = q_ref.shape[0], 512
    fetches = [
        pltpu.make_async_copy(ref, keys_ref.at[:, pl.ds(768 + i * 384, 384)], sems.at[rows // step + i])
        for i, ref in enumerate((right_ref, left_ref))
    ]
    for fetch in fetches:
        fetch.start()
    keys_ref[:, :384] = up_ref[...]
    keys_ref[:, 384:768] = down_ref[...]
    copies = []

    def scores_at(a):
        limit = past + a // 8 + (iota((step, 128), 0) >> 3)
        q = q_ref[a : a + step, :]
        near = masked_scores(q, keys_ref[:, :768], tiles[:6], limit)
        if a == 0:
            for fetch in fetches:
                fetch.wait()
        return jnp.concatenate([near, masked_scores(q, keys_ref[:, 768:], tiles[6:], limit)], axis=1)

    coming = scores_at(0)
    for a in range(0, rows, step):
        scores = coming
        if a + step < rows:
            coming = scores_at(a + step)
        before = top_ref[a : a + step, 0:1]
        top = jnp.maximum(jnp.max(scores, axis=1, keepdims=True), before)
        weights = jnp.exp2((scores - top) * SCALE_LOG2)
        fade = jnp.exp2((before - top) * SCALE_LOG2)
        share = 1.0 / (total_ref[a : a + step, 0:1] * fade + jnp.sum(weights, axis=1, keepdims=True))
        added = lax.dot_general(
            weights.astype(BF16), keys_ref[0:512, :], (((1,), (1,)), ((), ())), preferred_element_type=F32
        )
        done_ref[a : a + step, :] = ((mixed_ref[a : a + step, :] * fade + added) * share).astype(BF16)
        copies.append(
            pltpu.make_async_copy(
                done_ref.at[pl.ds(a, step), :], out_ref.at[pl.ds(a, step), :], sems.at[a // step]
            )
        )
        copies[-1].start()
    for copy in copies:
        copy.wait()


def attend_rest(state, parts):
    rows, width = state[-1].shape
    count = sum(part.shape[1] for part in parts)
    return pl.pallas_call(
        rest_kernel,
        out_shape=jax.ShapeDtypeStruct((rows, 512), BF16),
        in_specs=[VMEM] * 6 + [pl.BlockSpec(memory_space=pl.ANY)] * 2,
        out_specs=pl.BlockSpec(memory_space=pltpu.HBM),
        scratch_shapes=[
            pltpu.VMEM((width, count), BF16),
            pltpu.VMEM((rows, 512), BF16),
            pltpu.SemaphoreType.DMA((rows // 512 + 2,)),
        ],
        cost_estimate=pl.CostEstimate(
            flops=2 * rows * count * (width + 512), bytes_accessed=rows * 5376, transcendentals=rows * count
        ),
        compiler_params=pltpu.CompilerParams(vmem_limit_bytes=24 << 20),
        name="attend_rest",
    )(*state, *parts)


def turn(d):
    return [(i, (i + d) % SHARDS) for i in range(SHARDS)]


def line(dy, dz):
    return [(y * 4 + z, ((y + dy) % 4) * 4 + (z + dz) % 4) for y in range(4) for z in range(4)]


def body(q_latent, index_query, index_weight, index_keys, latent_cache, block_ids, block_counts):
    rows, heads, _ = q_latent.shape
    groups = lax.axis_size("head")
    *outgoing, source, other, past = gather_parts(block_ids, block_counts, latent_cache.T)
    incoming = [outgoing[0]] + [lax.ppermute(outgoing[d], "ctx", turn(2 * d)) for d in (2, 1, 3)]
    incoming = [incoming[0], incoming[2], incoming[1], incoming[3]]
    by_group = q_by_group(q_latent, groups)
    head_query = lax.all_to_all(by_group, "head", split_axis=0, concat_axis=0, tiled=True)
    index_scores = index_scores_of(index_query, index_weight, index_keys)
    theirs = compact_parts(128, other, incoming)
    theirs = lax.ppermute(theirs, "ctx", [(i, i ^ 1) for i in range(SHARDS)])
    mine = compact_parts(0, source, incoming)
    up, down, right, left = spread_parts(mine, theirs)
    parts = [
        lax.ppermute(part, "head", line(*step))
        for part, step in ((up, (1, 0)), (down, (-1, 0)), (right, (0, 1)), (left, (0, -1)))
    ]
    state = attend_own(past, head_query, up, down)
    attention = attend_rest(state, parts)
    return attention.reshape(rows * groups, heads // groups, 512), index_scores


def solution(mesh):
    return jax.shard_map(
        body,
        mesh=mesh,
        in_specs=(
            P(("ctx", "head"), None, None),
            P("head", None, None),
            P("head", None),
            P("ctx", None),
            P("ctx", None),
            P(),
            P(),
        ),
        out_specs=(P("ctx", "head", None), P("head", "ctx")),
        check_vma=False,
    )
```
